128 devices in a mesh: doc: 2 (over core), coarse: 4 (over z), fine: 16 (over y, x).
Axes of the slice: x: 4, y: 4, z: 4, core: 2. Of those that a mesh axis runs over, the one named last changes fastest.
Arguments:
- q_light: bfloat16 [2, 8192, 1024], P('doc', ('coarse', 'fine')), may hold values from -8 to 8
- k_light: bfloat16 [2, 8192, 1024], P('doc', ('coarse', 'fine')), may hold values from -8 to 8
- v_light: bfloat16 [2, 8192, 1024], P('doc', ('coarse', 'fine')), may hold values from -6 to 6
- q_heavy: bfloat16 [2, 8192, 1024], P('doc', ('coarse', 'fine')), may hold values from -8 to 8
- k_heavy: bfloat16 [2, 8192, 1024], P('doc', ('coarse', 'fine')), may hold values from -8 to 8
- v_heavy: bfloat16 [2, 8192, 1024], P('doc', ('coarse', 'fine')), may hold values from -6 to 6
- enc_kv: bfloat16 [2, 8192, 128], P('doc', ('coarse', 'fine')), may hold values from -8 to 8
- dec_queries: bfloat16 [2, 512, 1024], P('doc'), may hold values from -8 to 8
- query_ids: int32 [2, 64], P('doc'), may hold values from 0 to 63, as said below
- key_ids: int32 [2, 32], P('doc'), may hold values from 0 to 63, as said below
Outputs:
- encoded: bfloat16 [2, 8192, 1024], P('doc', ('coarse', 'fine'))
- decoded: bfloat16 [2, 512, 1024], P('doc')
The draws below stay inside these ranges and needn't reach their ends.
Inputs may be any that keep to these rules, and one draw needn't show every extreme that they name: `query_ids`: for each document and each c below the number of coarse groups, entries c * 16 to (c + 1) * 16 - 1 are distinct block numbers among blocks c * 16 to (c + 1) * 16 - 1 (so every block of the group is listed), and entry c * 16 + f is the block assigned to the f-th device of that group. `key_ids`: for each document and each c below the number of coarse groups, entries c * 8 to (c + 1) * 8 - 1 are distinct block numbers among blocks c * 16 * 1 to (c + 1) * 16 - 1.
All inputs are finite; a program needn't handle non-finite values.
Results may differ from the reference program's by a relative error of at most 0.009.
Values may be sent and summed in bfloat16 or wider, within the bound.
No kernel may reach another device: no remote copies, remote signals or barrier semaphores. Data moves between devices by JAX's collectives and lax.ppermute only.
A program may use at most 384 MiB of HBM per device.

```python
import jax
import jax.numpy as jnp
from jax import lax

HEADS = 16
HEAD = 64
ROUTED_BLOCK = 128
KGRP = 8
DEC = 512
TOK_DEV = 128
DOCS = 2
DOCUMENT_TOKENS = 8192
N_COARSE = 4
N_FINE = 16


def choose_blocks(key, count):
    per_group = N_FINE * (TOK_DEV // ROUTED_BLOCK)
    blk_dev = TOK_DEV // ROUTED_BLOCK

    def one_group(sub):
        leading_entry, second, third = jax.random.split(sub, 3)
        fullest = jax.random.randint(leading_entry, (), 0, N_FINE)
        scores = jax.random.permutation(second, per_group).astype(jnp.int32)
        local = jnp.arange(per_group, dtype=jnp.int32)
        forced = (local // blk_dev == fullest) & (local % blk_dev < min(blk_dev, count))
        scores = jnp.where(forced, scores + per_group, scores)
        order = jnp.argsort(-scores, stable=True)
        chosen = order[:count].astype(jnp.int32)
        return jax.random.permutation(third, chosen)
    keys = jax.random.split(key, DOCS * N_COARSE)
    picks = jax.vmap(one_group)(keys).reshape(DOCS, N_COARSE, count)
    block_offsets = jnp.arange(N_COARSE, dtype=jnp.int32) * per_group
    return (picks + block_offsets[None, :, None]).reshape(DOCS, N_COARSE * count).astype(jnp.int32)


def draw_query_ids(key, part):
    return choose_blocks(jax.random.fold_in(key, 11), N_FINE)


def draw_key_ids(key, part):
    return choose_blocks(jax.random.fold_in(key, 23), KGRP)


def drawn(key, shape):
    return jnp.clip(jax.random.normal(key, shape, jnp.float32), -6.0, 6.0)


def draw_q_light(key, part):
    field_key = jax.random.fold_in(key, 31)
    shape = (DOCS, DOCUMENT_TOKENS, HEADS * HEAD)
    return drawn(field_key, shape).astype(jnp.bfloat16)


def draw_k_light(key, part):
    field_key = jax.random.fold_in(key, 37)
    shape = (DOCS, DOCUMENT_TOKENS, HEADS * HEAD)
    return drawn(field_key, shape).astype(jnp.bfloat16)


def draw_q_heavy(key, part):
    field_key = jax.random.fold_in(key, 41)
    shape = (DOCS, DOCUMENT_TOKENS, HEADS * HEAD)
    return drawn(field_key, shape).astype(jnp.bfloat16)


def draw_k_heavy(key, part):
    field_key = jax.random.fold_in(key, 43)
    shape = (DOCS, DOCUMENT_TOKENS, HEADS * HEAD)
    return jnp.clip(3.0 * jax.random.normal(field_key, shape, jnp.float32), -8.0, 8.0).astype(jnp.bfloat16)


def draw_enc_kv(key, part):
    field_key = jax.random.fold_in(key, 47)
    shape = (DOCS, DOCUMENT_TOKENS, 2 * HEAD)
    return drawn(field_key, shape).astype(jnp.bfloat16)


def draw_dec_queries(key, part):
    field_key = jax.random.fold_in(key, 53)
    shape = (DOCS, DEC, HEADS * HEAD)
    return drawn(field_key, shape).astype(jnp.bfloat16)


def steps_of(own_key, shape, shards, low, largest):
    level, own = 1.0, jax.random.fold_in(own_key, 6)
    for axis_at, shards_of in shards:
        draws = jnp.exp(jax.random.uniform(jax.random.fold_in(own, axis_at), (shards_of,), jnp.float32, low / len(shards), largest / len(shards)))
        level = level * jnp.repeat(draws, shape[axis_at] // shards_of).reshape([-1 if axis == axis_at else 1 for axis in range(len(shape))])
    return level


def bell_draw(key, shape, deviation, most, shards=(), kind=jnp.bfloat16):
    entries = jax.random.normal(key, shape, jnp.float32) * deviation
    if len(shards) > 0:
        entries = steps_of(key, shape, shards, -0.22, 0.18) * entries
    return jnp.clip(entries, min=-most, max=most).astype(kind)


def setup_inputs(seed: int = 0) -> dict:
    splits = jax.random.split(jax.random.key(seed), 11)
    return {
        "q_light": draw_q_light(jax.random.fold_in(splits[10], 71), 0),
        "k_light": draw_k_light(jax.random.fold_in(splits[10], 71), 0),
        "v_light": bell_draw(splits[2], (DOCS, DOCUMENT_TOKENS, HEADS * HEAD), 1.0, 6.0, ((0, 2), (1, 64))),
        "q_heavy": draw_q_heavy(jax.random.fold_in(splits[10], 71), 0),
        "k_heavy": draw_k_heavy(jax.random.fold_in(splits[10], 71), 0),
        "v_heavy": bell_draw(splits[5], (DOCS, DOCUMENT_TOKENS, HEADS * HEAD), 1.0, 6.0, ((0, 2), (1, 64))),
        "enc_kv": draw_enc_kv(jax.random.fold_in(splits[10], 71), 0),
        "dec_queries": draw_dec_queries(jax.random.fold_in(splits[10], 71), 0),
        "query_ids": draw_query_ids(jax.random.fold_in(splits[10], 71), 0),
        "key_ids": draw_key_ids(jax.random.fold_in(splits[10], 71), 0),
    }


def attend(query, keys, value_rows, mask):
    rows = query.shape[0]
    count = keys.shape[0]
    heads = query.shape[1] // HEAD
    qh = query.reshape(rows, heads, HEAD).transpose(1, 0, 2)
    kh = keys.reshape(count, heads, HEAD).transpose(1, 0, 2)
    vh = value_rows.reshape(count, heads, HEAD).transpose(1, 0, 2)

    def one_head(triple):
        qa, ka, va = triple
        scores = jnp.dot(qa, ka.T, preferred_element_type=jnp.float32) * (HEAD ** -0.5)
        if mask is not None:
            scores = jnp.where(mask, scores, jnp.float32(-1e30))
        peak = jnp.max(scores, axis=1, keepdims=True)
        weights = jnp.exp(scores - peak)
        weights = (weights / jnp.sum(weights, axis=1, keepdims=True)).astype(jnp.bfloat16)
        return jnp.dot(weights, va, preferred_element_type=jnp.float32)

    out = lax.map(one_head, (qh, kh, vh))
    return out.transpose(1, 0, 2).reshape(rows, heads * HEAD)


def light_part(query, keys, value_rows):
    length = query.shape[0]
    width = query.shape[1]
    kpad = jnp.pad(keys, ((ROUTED_BLOCK, ROUTED_BLOCK), (0, 0)))
    padded_values = jnp.pad(value_rows, ((ROUTED_BLOCK, ROUTED_BLOCK), (0, 0)))

    def one_block(index):
        leading_entry = index * ROUTED_BLOCK
        qb = lax.dynamic_slice_in_dim(query, leading_entry, ROUTED_BLOCK)
        kb = lax.dynamic_slice_in_dim(kpad, leading_entry, 3 * ROUTED_BLOCK)
        value_block = lax.dynamic_slice_in_dim(padded_values, leading_entry, 3 * ROUTED_BLOCK)
        qpos = leading_entry + jnp.arange(ROUTED_BLOCK, dtype=jnp.int32)
        kpos = leading_entry - ROUTED_BLOCK + jnp.arange(3 * ROUTED_BLOCK, dtype=jnp.int32)
        mask = (jnp.abs(qpos[:, None] - kpos[None, :]) <= ROUTED_BLOCK - 1) & (kpos[None, :] >= 0) & (kpos[None, :] < length)
        return attend(qb, kb, value_block, mask)

    out = lax.map(one_block, jnp.arange(length // ROUTED_BLOCK, dtype=jnp.int32))
    return out.reshape(length, width)


def heavy_part(query, keys, value_rows, qids, kids):
    length, width = query.shape
    nblk = length // ROUTED_BLOCK
    qblocks = jnp.take(query.reshape(nblk, ROUTED_BLOCK, width), qids.astype(jnp.int32), axis=0)
    kall = jnp.take(keys.reshape(nblk, ROUTED_BLOCK, width), kids.astype(jnp.int32), axis=0).reshape(-1, width)
    vall = jnp.take(value_rows.reshape(nblk, ROUTED_BLOCK, width), kids.astype(jnp.int32), axis=0).reshape(-1, width)
    res = lax.map(lambda qb: attend(qb, kall, vall, None).astype(jnp.bfloat16), qblocks)
    full = jnp.zeros((nblk, ROUTED_BLOCK, width), jnp.bfloat16).at[qids.astype(jnp.int32)].set(res)
    return full.reshape(length, width)


def decoder_part(queries, enc):
    count = queries.shape[0]
    heads = queries.shape[1] // HEAD
    kenc = enc[:, :HEAD]
    venc = enc[:, HEAD:]
    qh = queries.reshape(count, heads, HEAD).transpose(1, 0, 2)

    def one_head(qa):
        scores = jnp.dot(qa, kenc.T, preferred_element_type=jnp.float32) * (HEAD ** -0.5)
        peak = jnp.max(scores, axis=1, keepdims=True)
        weights = jnp.exp(scores - peak)
        total = jnp.sum(weights, axis=1, keepdims=True)
        return jnp.dot(weights.astype(jnp.bfloat16), venc, preferred_element_type=jnp.float32) / total

    out = lax.map(one_head, qh)
    return out.transpose(1, 0, 2).reshape(count, heads * HEAD).astype(jnp.bfloat16)


def reference(q_light, k_light, v_light, q_heavy, k_heavy, v_heavy, enc_kv, dec_queries, query_ids, key_ids):
    encoded = []
    decoded = []
    for doc in range(DOCS):
        light = light_part(q_light[doc], k_light[doc], v_light[doc])
        heavy = heavy_part(q_heavy[doc], k_heavy[doc], v_heavy[doc], query_ids[doc], key_ids[doc])
        encoded.append((light + heavy.astype(jnp.float32)).astype(jnp.bfloat16))
        decoded.append(decoder_part(dec_queries[doc], enc_kv[doc]))
    return jnp.stack(encoded), jnp.stack(decoded)
```

```python
import jax
import jax.numpy as jnp
from jax import lax
from jax.experimental import pallas as pl
from jax.experimental.pallas import tpu as pltpu
from jax.sharding import PartitionSpec as P

HEAD = 64
LANES = 2 * HEAD
BLOCK = 128
KGRP = 8
HALF = BLOCK // 2
SCALE = HEAD**-0.5
LOG2E = 1.4426950408889634
TOKENS = ("coarse", "fine")
VMEM = 48 * 1024 * 1024

f32 = jnp.float32
bf16 = jnp.bfloat16


def params(**kw):
    return pltpu.CompilerParams(vmem_limit_bytes=VMEM, **kw)


def lane_ids(shape):
    return lax.broadcasted_iota(jnp.int32, shape, len(shape) - 1)


def nt(a, b):
    return lax.dot_general(a, b, (((1,), (1,)), ((), ())), preferred_element_type=f32)


def nn(a, b):
    return jnp.dot(a, b, preferred_element_type=f32)


def pack_kernel(q, k, v, enc, kv_out, q_out):
    heads = kv_out.shape[0]
    for h in range(heads):
        cols = slice(h * HEAD, (h + 1) * HEAD)
        kv_out[h] = jnp.concatenate([k[:, cols], v[:, cols]], axis=1)
        qh = q[:, cols]
        q_out[h, :HALF] = jnp.concatenate([qh[:HALF], qh[HALF:]], axis=1)
        q_out[h, HALF:] = enc[...]


def pack(q, k, v, enc):
    heads = q.shape[1] // HEAD
    return pl.pallas_call(
        pack_kernel,
        out_shape=(
            jax.ShapeDtypeStruct((heads, BLOCK, LANES), bf16),
            jax.ShapeDtypeStruct((heads, HALF + BLOCK, LANES), bf16),
        ),
        compiler_params=params(),
        name="pack",
    )(q, k, v, enc)


def pick_kernel(ids, kv, out):
    for s in range(KGRP):
        out[s] = kv[ids[s]]


def pick(ids, kv):
    return pl.pallas_call(
        pick_kernel,
        out_shape=jax.ShapeDtypeStruct((KGRP, BLOCK, LANES), bf16),
        in_specs=[pl.BlockSpec(memory_space=pltpu.SMEM), pl.BlockSpec(memory_space=pltpu.VMEM)],
        compiler_params=params(),
        name="pick",
    )(ids, kv)


def probs(q, keys, m=None):
    scores = [nt(q, k) for k in keys]
    peak = scores[0].max(axis=1, keepdims=True)
    for s in scores[1:]:
        peak = jnp.maximum(peak, s.max(axis=1, keepdims=True))
    return [jnp.exp2((s - peak) * (SCALE * LOG2E)).astype(bf16) for s in scores], peak


def with_ones(kv):
    return jnp.where(lane_ids(kv.shape) < HEAD, jnp.ones_like(kv), kv)


def summed(q, keys, values):
    p, peak = probs(q, keys)
    total = nn(p[0], values[0])
    for a, b in zip(p[1:], values[1:]):
        total = total + nn(a, b)
    return total, peak


def heavy_kernel(q, kv0, kv1, kv2, kv3, out, values):
    kvs = (kv0, kv1, kv2, kv3)

    @pl.when(pl.program_id(0) == 0)
    def _():
        for n, kv in enumerate(kvs):
            values[n] = with_ones(kv[...])

    rows = q.shape[0] * q.shape[1]
    both = q[...].reshape(rows, LANES)
    zero = jnp.zeros((rows, HEAD), bf16)
    keys = [kv[...] for kv in kvs]
    vals = [values[n] for n in range(len(kvs))]
    a, _ = summed(jnp.concatenate([both[:, :HEAD], zero], axis=1), keys, vals)
    b, _ = summed(jnp.concatenate([both[:, HEAD:], zero], axis=1), keys, vals)
    low = lane_ids(a.shape) < HEAD
    top = jnp.where(low, pltpu.roll(a, HEAD, 1), b)
    sums = jnp.where(low, a, pltpu.roll(b, HEAD, 1))
    out[...] = (top / sums).astype(bf16).reshape(out.shape)


def heavy_attend(q, kvs, step):
    blocks = q.shape[0]
    full = pl.BlockSpec(kvs[0].shape, lambda i: (0, 0))
    return pl.pallas_call(
        heavy_kernel,
        grid=(blocks // step,),
        in_specs=[pl.BlockSpec((step, HALF, LANES), lambda i: (i, 0, 0))] + [full] * len(kvs),
        out_specs=pl.BlockSpec((step, HALF, LANES), lambda i: (i, 0, 0)),
        out_shape=jax.ShapeDtypeStruct((blocks, HALF, LANES), bf16),
        scratch_shapes=[pltpu.VMEM((len(kvs),) + kvs[0].shape, bf16)],
        compiler_params=params(),
        name="heavy",
    )(q, *kvs)


def light_kernel(edge, q, k, v, pk, pv, nk, nv, out):
    qq = q[...]
    low = lane_ids(qq.shape) < HEAD
    zero = jnp.zeros_like(qq)
    rows = qq.shape[0]
    two = jnp.concatenate([jnp.where(low, qq, zero), jnp.where(low, zero, qq)], axis=0)
    i = lax.broadcasted_iota(jnp.int32, (2 * rows, BLOCK), 0) % rows
    j = lax.broadcasted_iota(jnp.int32, (2 * rows, BLOCK), 1)
    here = nt(two, k[...]) * SCALE
    prev = jnp.where((j > i) & (edge[0] > 0), nt(two, pk[...]) * SCALE, f32(-1e30))
    after = jnp.where((j < i) & (edge[1] > 0), nt(two, nk[...]) * SCALE, f32(-1e30))
    peak = jnp.maximum(jnp.maximum(here, prev), after).max(axis=1, keepdims=True)
    ph, pp, pn = (jnp.exp(s - peak) for s in (here, prev, after))
    total = (ph + pp + pn).sum(axis=1, keepdims=True)
    o = nn(ph.astype(bf16), v[...]) + nn(pp.astype(bf16), pv[...]) + nn(pn.astype(bf16), nv[...])
    o = o / total
    out[...] = jnp.where(low, o[:rows], o[rows:])


def light_attend(edge, q, k, v, prev, after):
    rows, width = q.shape
    pairs = width // LANES
    col = pl.BlockSpec((rows, LANES), lambda p: (0, p))
    col_v = pl.BlockSpec((rows, LANES), lambda p: (0, p + pairs))
    return pl.pallas_call(
        light_kernel,
        grid=(pairs,),
        in_specs=[pl.BlockSpec(memory_space=pltpu.SMEM), col, col, col, col, col_v, col, col_v],
        out_specs=col,
        out_shape=jax.ShapeDtypeStruct((rows, width), f32),
        compiler_params=params(),
        name="light",
    )(edge, q, k, v, prev, prev, after, after)


def join_kernel(chosen, light, heavy, out):
    scale = chosen[0].astype(f32)
    for p in range(heavy.shape[0] // 2):
        e, o = heavy[2 * p], heavy[2 * p + 1]
        for n in range(2):
            rows, lanes = slice(n * HALF, (n + 1) * HALF), slice(n * HEAD, (n + 1) * HEAD)
            cols = slice(p * LANES, (p + 1) * LANES)
            both = jnp.concatenate([e[:, lanes], o[:, lanes]], axis=1)
            out[rows, cols] = (light[rows, cols] + both.astype(f32) * scale).astype(bf16)


def join(chosen, light, heavy):
    vmem = pl.BlockSpec(memory_space=pltpu.VMEM)
    return pl.pallas_call(
        join_kernel,
        in_specs=[pl.BlockSpec(memory_space=pltpu.SMEM), vmem, vmem],
        out_shape=jax.ShapeDtypeStruct(light.shape, bf16),
        compiler_params=params(),
        name="join",
    )(chosen, light, heavy)


def decode_kernel(at, q, enc_a, enc_b, out):
    del at
    heads = q.shape[1] // HEAD
    rows = q.shape[0]
    zero = jnp.zeros((rows, HEAD), bf16)
    stack = jnp.concatenate(
        [
            jnp.concatenate([q[:, h * HEAD : (h + 1) * HEAD], zero], axis=1)
            for h in range(heads)
        ],
        axis=0,
    )
    keys = [e[...].reshape(-1, LANES) for e in (enc_a, enc_b)]
    vals = [with_ones(k) for k in keys]
    half = stack.shape[0] // 2
    for n in range(2):
        total, peak = summed(stack[n * half : (n + 1) * half], keys, vals)
        low = lane_ids(total.shape) < HEAD
        level = peak * SCALE + jnp.log(total)
        hi = level.astype(bf16).astype(f32)
        mid = (level - hi).astype(bf16).astype(f32)
        least = level - hi - mid
        lane = lane_ids(total.shape)
        parts = jnp.where(lane < 16, hi, jnp.where(lane < 32, mid, least))
        ratio = total / pltpu.roll(total, HEAD, 1)
        out[n * half : (n + 1) * half] = jnp.where(low, parts, ratio).astype(bf16)


def decode(at, q, enc, rows):
    blocks = enc.shape[0]
    width = q.shape[1]
    spec = lambda n: pl.BlockSpec((blocks, HALF, LANES), lambda i, at: (0, n, 0))
    out = (rows * (width // HEAD), LANES)
    return pl.pallas_call(
        decode_kernel,
        grid_spec=pltpu.PrefetchScalarGridSpec(
            num_scalar_prefetch=1,
            grid=(1,),
            in_specs=[pl.BlockSpec((rows, width), lambda i, at: (at[0], 0)), spec(1), spec(2)],
            out_specs=pl.BlockSpec(out, lambda i, at: (0, 0)),
        ),
        out_shape=jax.ShapeDtypeStruct(out, bf16),
        compiler_params=params(),
        name="decode",
    )(at, q, enc, enc)


def meet_kernel(a, b, c, d, out):
    parts = [x[...].astype(f32) for x in (a, b, c, d)]
    levels = [x[:, 0:1] + x[:, 16:17] + x[:, 32:33] for x in parts]
    peak = jnp.maximum(jnp.maximum(levels[0], levels[1]), jnp.maximum(levels[2], levels[3]))
    scales = [jnp.exp(n - peak) for n in levels]
    total = scales[0] + scales[1] + scales[2] + scales[3]
    value = parts[0] * scales[0]
    for x, s in zip(parts[1:], scales[1:]):
        value = value + x * s
    value = (value / total).astype(bf16)
    copies, rows, width = out.shape
    for p in range(width // LANES):
        e = value[2 * p * rows : (2 * p + 1) * rows, HEAD:]
        o = value[(2 * p + 1) * rows : (2 * p + 2) * rows, HEAD:]
        both = jnp.concatenate([e, o], axis=1)
        for n in range(copies):
            out[n, :, p * LANES : (p + 1) * LANES] = both


def meet(parts, copies, rows, width):
    return pl.pallas_call(
        meet_kernel,
        out_shape=jax.ShapeDtypeStruct((copies, rows, width), bf16),
        compiler_params=params(),
        name="meet",
    )(*parts)


def around(value, axis):
    size = lax.axis_size(axis)
    return [lax.ppermute(value, axis, [(i, (i + d) % size) for i in range(size)]) for d in range(1, size)]


def local(
    q_light, k_light, v_light, q_heavy, k_heavy, v_heavy, enc_kv, dec_queries, query_ids, key_ids
):
    n_seq = lax.axis_size(TOKENS)
    n_fine = lax.axis_size("fine")
    here = lax.axis_index(TOKENS)
    group = lax.axis_index("coarse")
    place = lax.axis_index("fine")
    width = q_light.shape[2]

    kv_chunks, q_chunks = pack(q_heavy[0], k_heavy[0], v_heavy[0], enc_kv[0])
    kv_group = lax.all_to_all(kv_chunks, "fine", 0, 0, tiled=True)
    q_enc = lax.all_to_all(q_chunks, "fine", 0, 0, tiled=True)

    light_kv = jnp.concatenate([k_light[0], v_light[0]], axis=1)
    up = [(i, i + 1) for i in range(n_seq - 1)]
    prev = lax.ppermute(light_kv, TOKENS, up)
    after = lax.ppermute(light_kv, TOKENS, [(b, a) for a, b in up])

    ids = lax.dynamic_slice_in_dim(key_ids[0], group * KGRP, KGRP) - group * n_fine
    own = pick(ids, kv_group).reshape(KGRP * BLOCK, LANES)
    routed = [own] + around(own, "coarse")

    dec_rows = dec_queries.shape[1] // n_fine
    part = decode(place[None], dec_queries[0], q_enc, dec_rows)
    parts = [part] + around(part, "coarse")
    shares = meet(parts, n_fine, dec_rows, width)
    decoded = lax.all_to_all(shares, "fine", 0, 0, tiled=True).reshape(1, -1, width)

    heavy = heavy_attend(q_enc, routed, 4)
    heavy = lax.all_to_all(heavy, "fine", 0, 0, tiled=True)

    edge = jnp.stack([here > 0, here < n_seq - 1]).astype(jnp.int32)
    light = light_attend(edge, q_light[0], k_light[0], v_light[0], prev, after)
    query_group = lax.dynamic_slice_in_dim(query_ids[0], group * n_fine, n_fine)
    chosen = jnp.sum((query_group == here).astype(jnp.int32))[None]
    encoded = join(chosen, light, heavy)[None]
    return (encoded, decoded)


def solution(mesh):
    seq = P("doc", TOKENS, None)
    whole = P("doc", None, None)
    return jax.shard_map(
        local,
        mesh=mesh,
        in_specs=(seq,) * 7 + (whole, P("doc", None), P("doc", None)),
        out_specs=(seq, whole),
        check_vma=False,
    )
```

```python
import jax
import jax.numpy as jnp
from jax import lax
from jax.experimental import pallas as pl
from jax.experimental.pallas import tpu as pltpu
from jax.sharding import PartitionSpec as P

HEAD = 64
LANES = 2 * HEAD
BLOCK = 128
KGRP = 8
HALF = BLOCK // 2
SCALE = HEAD**-0.5
LOG2E = 1.4426950408889634
TOKENS = ("coarse", "fine")
VMEM = 48 * 1024 * 1024

f32 = jnp.float32
bf16 = jnp.bfloat16


def params(**kw):
    return pltpu.CompilerParams(vmem_limit_bytes=VMEM, **kw)


def lane_ids(shape):
    return lax.broadcasted_iota(jnp.int32, shape, len(shape) - 1)


def nt(a, b):
    return lax.dot_general(a, b, (((1,), (1,)), ((), ())), preferred_element_type=f32)


def nn(a, b):
    return jnp.dot(a, b, preferred_element_type=f32)


def pack_kernel(q_hbm, k_hbm, v_hbm, out, q, k, v, sem):
    copies = [
        pltpu.make_async_copy(src, dst, sem.at[n])
        for n, (src, dst) in enumerate(((k_hbm, k), (v_hbm, v), (q_hbm, q)))
    ]
    for c in copies:
        c.start()
    heads = out.shape[0]
    copies[0].wait()
    copies[1].wait()
    for h in range(heads):
        cols = slice(h * HEAD, (h + 1) * HEAD)
        out[h, :BLOCK] = jnp.concatenate([k[:, cols], v[:, cols]], axis=1)
    copies[2].wait()
    for h in range(heads):
        qh = q[:, h * HEAD : (h + 1) * HEAD]
        out[h, BLOCK:] = jnp.concatenate([qh[:HALF], qh[HALF:]], axis=1)


def pack(q, k, v):
    heads = q.shape[1] // HEAD
    hbm = pl.BlockSpec(memory_space=pltpu.HBM)
    return pl.pallas_call(
        pack_kernel,
        in_specs=[hbm] * 3,
        out_shape=jax.ShapeDtypeStruct((heads, BLOCK + HALF, LANES), bf16),
        scratch_shapes=[pltpu.VMEM(x.shape, bf16) for x in (q, k, v)]
        + [pltpu.SemaphoreType.DMA((3,))],
        compiler_params=params(),
        name="pack",
    )(q, k, v)


def pick_kernel(ids, kv, out):
    group = lax.axis_index("coarse")
    for s in range(KGRP):
        out[s] = kv[ids[0, group * KGRP + s] - group * kv.shape[0], :BLOCK]


def pick(ids, kv):
    return pl.pallas_call(
        pick_kernel,
        out_shape=jax.ShapeDtypeStruct((KGRP, BLOCK, LANES), bf16),
        in_specs=[pl.BlockSpec(memory_space=pltpu.SMEM), pl.BlockSpec(memory_space=pltpu.VMEM)],
        compiler_params=params(),
        name="pick",
    )(ids, kv)


def with_ones(kv):
    return jnp.where(lane_ids(kv.shape) < HEAD, jnp.ones_like(kv), kv)


def summed(q, keys, values):
    peak = total = None
    for k, v in zip(keys, values):
        s = nt(q, k)
        top = s.max(axis=1, keepdims=True)
        top = top if peak is None else jnp.maximum(peak, top)
        o = nn(jnp.exp2((s - top) * (SCALE * LOG2E)).astype(bf16), v)
        total = o if peak is None else total * jnp.exp2((peak - top) * (SCALE * LOG2E)) + o
        peak = top
    return total, peak


def heavy_kernel(part, q, kv0, kv1, kv2, kv3, *rest):
    out = rest[-1]
    rows = q.shape[0] * HALF
    both = q[:, BLOCK:].reshape(rows, LANES)
    zero = jnp.zeros((rows, HEAD), bf16)
    keys = [kv[...] for kv in (kv0, kv1, kv2, kv3)]
    vals = [with_ones(k) for k in keys]
    mine = jnp.concatenate([both[:, part * HEAD : (part + 1) * HEAD], zero], axis=1)
    o, _ = summed(mine, keys, vals)
    ratio = (o / pltpu.roll(o, HEAD, 1))[:, HEAD:].astype(bf16)
    if part == 0:
        out[...] = ratio.reshape(out.shape)
    else:
        out[...] = jnp.concatenate([rest[0][...].reshape(rows, HEAD), ratio], axis=1).reshape(out.shape)


def heavy_attend(part, q_kv, kvs, *first):
    blocks = q_kv.shape[0]
    lanes = (part + 1) * HEAD
    return pl.pallas_call(
        lambda *refs: heavy_kernel(part, *refs),
        out_shape=jax.ShapeDtypeStruct((blocks, HALF, lanes), bf16),
        compiler_params=params(),
        cost_estimate=pl.CostEstimate(flops=5_000_000_000, transcendentals=4_000_000, bytes_accessed=2_000_000),
        name=f"heavy{part}",
    )(q_kv, *kvs, *first)


def light_kernel(q, k, v, prev, after, out):
    here = lax.axis_index(TOKENS)
    last = lax.axis_size(TOKENS) - 1
    rows, width = q.shape
    low = lane_ids((rows, LANES)) < HEAD
    i = lax.broadcasted_iota(jnp.int32, (2 * rows, BLOCK), 0) % rows
    j = lax.broadcasted_iota(jnp.int32, (2 * rows, BLOCK), 1)
    sees_prev = (j > i) & (here > 0)
    sees_next = (j < i) & (here < last)
    for p in range(width // LANES):
        c = slice(p * LANES, (p + 1) * LANES)
        cv = slice(width + p * LANES, width + (p + 1) * LANES)
        qq = q[:, c]
        zero = jnp.zeros_like(qq)
        two = jnp.concatenate([jnp.where(low, qq, zero), jnp.where(low, zero, qq)], axis=0)
        own = nt(two, k[:, c])
        left = jnp.where(sees_prev, nt(two, prev[:, c]), f32(-1e30))
        right = jnp.where(sees_next, nt(two, after[:, c]), f32(-1e30))
        peak = jnp.maximum(jnp.maximum(own, left), right).max(axis=1, keepdims=True)
        po, pp, pn = (jnp.exp2((s - peak) * (SCALE * LOG2E)) for s in (own, left, right))
        total = (po + pp + pn).sum(axis=1, keepdims=True)
        o = nn(po.astype(bf16), v[:, c]) + nn(pp.astype(bf16), prev[:, cv]) + nn(pn.astype(bf16), after[:, cv])
        o = o / total
        out[:, c] = jnp.where(low, o[:rows], o[rows:])


def light_attend(q, k, v, prev, after):
    return pl.pallas_call(
        light_kernel,
        out_shape=jax.ShapeDtypeStruct(q.shape, f32),
        compiler_params=params(),
        cost_estimate=pl.CostEstimate(flops=3_000_000_000, transcendentals=800_000, bytes_accessed=2_000_000),
        name="light",
    )(q, k, v, prev, after)


def join_kernel(ids, light, heavy, out):
    here = lax.axis_index(TOKENS)
    count = jnp.int32(0)
    for n in range(ids.shape[1]):
        count = count + jnp.where(ids[0, n] == here, 1, 0)
    scale = count.astype(f32)
    for p in range(heavy.shape[0] // 2):
        e, o = heavy[2 * p], heavy[2 * p + 1]
        for n in range(2):
            rows, lanes = slice(n * HALF, (n + 1) * HALF), slice(n * HEAD, (n + 1) * HEAD)
            cols = slice(p * LANES, (p + 1) * LANES)
            both = jnp.concatenate([e[:, lanes], o[:, lanes]], axis=1)
            out[rows, cols] = (light[rows, cols] + both.astype(f32) * scale).astype(bf16)


def join(ids, light, heavy):
    vmem = pl.BlockSpec(memory_space=pltpu.VMEM)
    return pl.pallas_call(
        join_kernel,
        in_specs=[pl.BlockSpec(memory_space=pltpu.SMEM), vmem, vmem],
        out_shape=jax.ShapeDtypeStruct(light.shape, bf16),
        compiler_params=params(),
        name="join",
    )(ids, light, heavy)


def decode_kernel(q_hbm, e0, e1, e2, e3, out, q, sem):
    rows, width = q.shape
    at = pl.multiple_of(lax.axis_index("fine") * rows, rows)
    copy = pltpu.make_async_copy(q_hbm.at[pl.ds(at, rows)], q, sem)
    copy.start()
    copy.wait()
    zero = jnp.zeros((rows, HEAD), bf16)
    stack = jnp.concatenate(
        [
            jnp.concatenate([q[:, h * HEAD : (h + 1) * HEAD], zero], axis=1)
            for h in range(width // HEAD)
        ],
        axis=0,
    )
    keys = [e[...] for e in (e0, e1, e2, e3)]
    vals = [with_ones(k) for k in keys]
    total, peak = summed(stack, keys, vals)
    lane = lane_ids(total.shape)
    level = peak * SCALE + jnp.log(total)
    hi = level.astype(bf16).astype(f32)
    mid = (level - hi).astype(bf16).astype(f32)
    least = level - hi - mid
    parts = jnp.where(lane < 16, hi, jnp.where(lane < 32, mid, least))
    ratio = total / pltpu.roll(total, HEAD, 1)
    out[...] = jnp.where(lane < HEAD, parts, ratio).astype(bf16)


def decode(q, enc, rows):
    width = q.shape[1]
    vmem = pl.BlockSpec(memory_space=pltpu.VMEM)
    return pl.pallas_call(
        decode_kernel,
        in_specs=[pl.BlockSpec(memory_space=pltpu.HBM)] + [vmem] * len(enc),
        out_shape=jax.ShapeDtypeStruct((rows * (width // HEAD), LANES), bf16),
        scratch_shapes=[pltpu.VMEM((rows, width), bf16), pltpu.SemaphoreType.DMA(())],
        compiler_params=params(),
        cost_estimate=pl.CostEstimate(flops=1_000_000_000, transcendentals=1_000_000, bytes_accessed=1_000_000),
        name="decode",
    )(q, *enc)


def meet_kernel(a, b, c, d, out):
    parts = [x[...].astype(f32) for x in (a, b, c, d)]
    levels = [x[:, 0:1] + x[:, 16:17] + x[:, 32:33] for x in parts]
    peak = jnp.maximum(jnp.maximum(levels[0], levels[1]), jnp.maximum(levels[2], levels[3]))
    scales = [jnp.exp(n - peak) for n in levels]
    total = scales[0] + scales[1] + scales[2] + scales[3]
    value = parts[0] * scales[0]
    for x, s in zip(parts[1:], scales[1:]):
        value = value + x * s
    value = (value / total).astype(bf16)
    copies, rows, width = out.shape
    for p in range(width // LANES):
        e = value[2 * p * rows : (2 * p + 1) * rows, HEAD:]
        o = value[(2 * p + 1) * rows : (2 * p + 2) * rows, HEAD:]
        both = jnp.concatenate([e, o], axis=1)
        for n in range(copies):
            out[n, :, p * LANES : (p + 1) * LANES] = both


def meet(parts, copies, rows, width):
    return pl.pallas_call(
        meet_kernel,
        out_shape=jax.ShapeDtypeStruct((copies, rows, width), bf16),
        compiler_params=params(),
        name="meet",
    )(*parts)


def around(value, axis, stride=1, ring=None):
    size = lax.axis_size(axis)
    ring = ring or size

    def to(i, d):
        at = i // stride % ring
        return i + ((at + d) % ring - at) * stride

    return [lax.ppermute(value, axis, [(i, to(i, d)) for i in range(size)]) for d in range(1, ring)]


def after_all(value, *others):
    return lax.optimization_barrier((value, others))[0]


def local(
    q_light, k_light, v_light, q_heavy, k_heavy, v_heavy, enc_kv, dec_queries, query_ids, key_ids
):
    n_seq = lax.axis_size(TOKENS)
    n_fine = lax.axis_size("fine")
    side = 4
    width = q_light.shape[2]

    chunks = pack(q_heavy[0], k_heavy[0], v_heavy[0])
    group = lax.all_to_all(chunks, "fine", 0, 0, tiled=True)

    row = jnp.concatenate([enc_kv[0]] + around(enc_kv[0], "fine", 1, side), axis=0)
    enc = [row] + around(row, "fine", side, n_fine // side)
    dec_rows = dec_queries.shape[1] // n_fine
    part = decode(dec_queries[0], enc, dec_rows)
    parts = around(part, "coarse")

    own = pick(key_ids, after_all(group, part)).reshape(KGRP * BLOCK, LANES)
    routed = [own] + around(own, "coarse")

    shares = meet([after_all(part, own)] + parts, n_fine, dec_rows, width)
    decoded = lax.all_to_all(shares, "fine", 0, 0, tiled=True)

    light_kv = jnp.concatenate([k_light[0], v_light[0]], axis=1)
    light_kv = after_all(light_kv, own)
    up = [(i, i + 1) for i in range(n_seq - 1)]
    prev = lax.ppermute(light_kv, TOKENS, up)
    after = lax.ppermute(light_kv, TOKENS, [(b, a) for a, b in up])

    first = heavy_attend(0, after_all(group, shares), routed)
    heavy = heavy_attend(1, after_all(group, prev, after), routed, first)
    q_light = after_all(q_light, heavy)
    heavy, decoded = lax.optimization_barrier((heavy, decoded))
    heavy = lax.all_to_all(heavy, "fine", 0, 0, tiled=True)

    light = light_attend(q_light[0], k_light[0], v_light[0], prev, after)
    encoded = join(query_ids, light, heavy)[None]
    return (encoded, decoded.reshape(1, -1, width))


def solution(mesh):
    seq = P("doc", TOKENS, None)
    whole = P("doc", None, None)
    return jax.shard_map(
        local,
        mesh=mesh,
        in_specs=(seq,) * 7 + (whole, P("doc", None), P("doc", None)),
        out_specs=(seq, whole),
        check_vma=False,
    )
```

```python
import jax
import jax.numpy as jnp
from jax import lax
from jax.experimental import pallas as pl
from jax.experimental.pallas import tpu as pltpu
from jax.sharding import PartitionSpec as P

HEAD = 64
LANES = 2 * HEAD
BLOCK = 128
KGRP = 8
HALF = BLOCK // 2
SCALE = HEAD**-0.5
LOG2E = 1.4426950408889634
TOKENS = ("coarse", "fine")
VMEM = 48 * 1024 * 1024

f32 = jnp.float32
bf16 = jnp.bfloat16


def params(**kw):
    return pltpu.CompilerParams(vmem_limit_bytes=VMEM, **kw)


def lane_ids(shape):
    return lax.broadcasted_iota(jnp.int32, shape, len(shape) - 1)


def nt(a, b):
    return lax.dot_general(a, b, (((1,), (1,)), ((), ())), preferred_element_type=f32)


def nn(a, b):
    return jnp.dot(a, b, preferred_element_type=f32)


def pack_kernel(q_hbm, k_hbm, v_hbm, out, q, k, v, sem):
    copies = [
        pltpu.make_async_copy(src, dst, sem.at[n])
        for n, (src, dst) in enumerate(((k_hbm, k), (v_hbm, v), (q_hbm, q)))
    ]
    for c in copies:
        c.start()
    heads = out.shape[0]
    copies[0].wait()
    copies[1].wait()
    for h in range(heads):
        cols = slice(h * HEAD, (h + 1) * HEAD)
        out[h, :BLOCK] = jnp.concatenate([k[:, cols], v[:, cols]], axis=1)
    copies[2].wait()
    for h in range(heads):
        qh = q[:, h * HEAD : (h + 1) * HEAD]
        out[h, BLOCK:] = jnp.concatenate([qh[:HALF], qh[HALF:]], axis=1)


def pack(q, k, v):
    heads = q.shape[1] // HEAD
    hbm = pl.BlockSpec(memory_space=pltpu.HBM)
    return pl.pallas_call(
        pack_kernel,
        in_specs=[hbm] * 3,
        out_shape=jax.ShapeDtypeStruct((heads, BLOCK + HALF, LANES), bf16),
        scratch_shapes=[pltpu.VMEM(x.shape, bf16) for x in (q, k, v)]
        + [pltpu.SemaphoreType.DMA((3,))],
        compiler_params=params(),
        name="pack",
    )(*(pltpu.with_memory_space_constraint(x, pltpu.HBM) for x in (q, k, v)))


def pick_kernel(ids, kv, out):
    group = lax.axis_index("coarse")
    for s in range(KGRP):
        out[s] = kv[ids[0, group * KGRP + s] - group * kv.shape[0], :BLOCK]


def pick(ids, kv):
    return pl.pallas_call(
        pick_kernel,
        out_shape=jax.ShapeDtypeStruct((KGRP, BLOCK, LANES), bf16),
        in_specs=[pl.BlockSpec(memory_space=pltpu.SMEM), pl.BlockSpec(memory_space=pltpu.VMEM)],
        compiler_params=params(),
        name="pick",
    )(ids, kv)


def with_ones(kv):
    return jnp.where(lane_ids(kv.shape) < HEAD, jnp.ones_like(kv), kv)


def summed(q, keys, values):
    peak = total = None
    for k, v in zip(keys, values):
        s = nt(q, k)
        top = s.max(axis=1, keepdims=True)
        top = top if peak is None else jnp.maximum(peak, top)
        o = nn(jnp.exp2((s - top) * (SCALE * LOG2E)).astype(bf16), v)
        total = o if peak is None else total * jnp.exp2((peak - top) * (SCALE * LOG2E)) + o
        peak = top
    return total, peak


def heavy_kernel(q, kv0, kv1, kv2, kv3, out):
    rows = q.shape[0] * HALF
    both = q[:, BLOCK:].reshape(rows, LANES)
    zero = jnp.zeros((rows, HEAD), bf16)
    keys = [kv[...] for kv in (kv0, kv1, kv2, kv3)]
    vals = [with_ones(k) for k in keys]
    a, _ = summed(jnp.concatenate([both[:, :HEAD], zero], axis=1), keys, vals)
    b, _ = summed(jnp.concatenate([both[:, HEAD:], zero], axis=1), keys, vals)
    low = lane_ids(a.shape) < HEAD
    top = jnp.where(low, pltpu.roll(a, HEAD, 1), b)
    sums = jnp.where(low, a, pltpu.roll(b, HEAD, 1))
    out[...] = (top / sums).astype(bf16).reshape(out.shape)


def heavy_attend(q_kv, kvs):
    blocks = q_kv.shape[0]
    return pl.pallas_call(
        heavy_kernel,
        out_shape=jax.ShapeDtypeStruct((blocks, HALF, LANES), bf16),
        compiler_params=params(),
        cost_estimate=pl.CostEstimate(flops=10_000_000_000, transcendentals=8_000_000, bytes_accessed=2_000_000),
        name="heavy",
    )(q_kv, *kvs)


def light_kernel(q, k, v, prev, after, out):
    here = lax.axis_index(TOKENS)
    last = lax.axis_size(TOKENS) - 1
    rows, width = q.shape
    low = lane_ids((rows, LANES)) < HEAD
    i = lax.broadcasted_iota(jnp.int32, (2 * rows, BLOCK), 0) % rows
    j = lax.broadcasted_iota(jnp.int32, (2 * rows, BLOCK), 1)
    sees_prev = (j > i) & (here > 0)
    sees_next = (j < i) & (here < last)
    for p in range(width // LANES):
        c = slice(p * LANES, (p + 1) * LANES)
        cv = slice(width + p * LANES, width + (p + 1) * LANES)
        qq = q[:, c]
        zero = jnp.zeros_like(qq)
        two = jnp.concatenate([jnp.where(low, qq, zero), jnp.where(low, zero, qq)], axis=0)
        own = nt(two, k[:, c])
        left = jnp.where(sees_prev, nt(two, prev[:, c]), f32(-1e30))
        right = jnp.where(sees_next, nt(two, after[:, c]), f32(-1e30))
        peak = jnp.maximum(jnp.maximum(own, left), right).max(axis=1, keepdims=True)
        po, pp, pn = (jnp.exp2((s - peak) * (SCALE * LOG2E)) for s in (own, left, right))
        total = (po + pp + pn).sum(axis=1, keepdims=True)
        o = nn(po.astype(bf16), v[:, c]) + nn(pp.astype(bf16), prev[:, cv]) + nn(pn.astype(bf16), after[:, cv])
        o = o / total
        out[:, c] = jnp.where(low, o[:rows], o[rows:])


def light_attend(q, k, v, prev, after):
    return pl.pallas_call(
        light_kernel,
        out_shape=jax.ShapeDtypeStruct(q.shape, f32),
        compiler_params=params(),
        cost_estimate=pl.CostEstimate(flops=3_000_000_000, transcendentals=800_000, bytes_accessed=2_000_000),
        name="light",
    )(q, k, v, prev, after)


def join_kernel(ids, light, heavy, out):
    here = lax.axis_index(TOKENS)
    count = jnp.int32(0)
    for n in range(ids.shape[1]):
        count = count + jnp.where(ids[0, n] == here, 1, 0)
    scale = count.astype(f32)
    for p in range(heavy.shape[0] // 2):
        e, o = heavy[2 * p], heavy[2 * p + 1]
        for n in range(2):
            rows, lanes = slice(n * HALF, (n + 1) * HALF), slice(n * HEAD, (n + 1) * HEAD)
            cols = slice(p * LANES, (p + 1) * LANES)
            both = jnp.concatenate([e[:, lanes], o[:, lanes]], axis=1)
            out[rows, cols] = (light[rows, cols] + both.astype(f32) * scale).astype(bf16)


def join(ids, light, heavy):
    vmem = pl.BlockSpec(memory_space=pltpu.VMEM)
    return pl.pallas_call(
        join_kernel,
        in_specs=[pl.BlockSpec(memory_space=pltpu.SMEM), vmem, vmem],
        out_shape=jax.ShapeDtypeStruct(light.shape, bf16),
        compiler_params=params(),
        name="join",
    )(ids, light, heavy)


def decode_kernel(q_hbm, e0, e1, e2, e3, out, q, sem):
    rows, width = q.shape
    at = pl.multiple_of(lax.axis_index("fine") * rows, rows)
    copy = pltpu.make_async_copy(q_hbm.at[pl.ds(at, rows)], q, sem)
    copy.start()
    copy.wait()
    zero = jnp.zeros((rows, HEAD), bf16)
    stack = jnp.concatenate(
        [
            jnp.concatenate([q[:, h * HEAD : (h + 1) * HEAD], zero], axis=1)
            for h in range(width // HEAD)
        ],
        axis=0,
    )
    keys = [e[...] for e in (e0, e1, e2, e3)]
    vals = [with_ones(k) for k in keys]
    total, peak = summed(stack, keys, vals)
    lane = lane_ids(total.shape)
    level = peak * SCALE + jnp.log(total)
    hi = level.astype(bf16).astype(f32)
    mid = (level - hi).astype(bf16).astype(f32)
    least = level - hi - mid
    parts = jnp.where(lane < 16, hi, jnp.where(lane < 32, mid, least))
    ratio = total / pltpu.roll(total, HEAD, 1)
    out[...] = jnp.where(lane < HEAD, parts, ratio).astype(bf16)


def decode(q, enc, rows):
    width = q.shape[1]
    vmem = pl.BlockSpec(memory_space=pltpu.VMEM)
    return pl.pallas_call(
        decode_kernel,
        in_specs=[pl.BlockSpec(memory_space=pltpu.HBM)] + [vmem] * len(enc),
        out_shape=jax.ShapeDtypeStruct((rows * (width // HEAD), LANES), bf16),
        scratch_shapes=[pltpu.VMEM((rows, width), bf16), pltpu.SemaphoreType.DMA(())],
        compiler_params=params(),
        cost_estimate=pl.CostEstimate(flops=1_000_000_000, transcendentals=1_000_000, bytes_accessed=1_000_000),
        name="decode",
    )(q, *enc)


def meet_kernel(a, b, c, d, out):
    parts = [x[...].astype(f32) for x in (a, b, c, d)]
    levels = [x[:, 0:1] + x[:, 16:17] + x[:, 32:33] for x in parts]
    peak = jnp.maximum(jnp.maximum(levels[0], levels[1]), jnp.maximum(levels[2], levels[3]))
    scales = [jnp.exp(n - peak) for n in levels]
    total = scales[0] + scales[1] + scales[2] + scales[3]
    value = parts[0] * scales[0]
    for x, s in zip(parts[1:], scales[1:]):
        value = value + x * s
    value = (value / total).astype(bf16)
    rows, width = out.shape
    for p in range(width // LANES):
        e = value[2 * p * rows : (2 * p + 1) * rows, HEAD:]
        o = value[(2 * p + 1) * rows : (2 * p + 2) * rows, HEAD:]
        out[:, p * LANES : (p + 1) * LANES] = jnp.concatenate([e, o], axis=1)


def meet(parts, rows, width):
    return pl.pallas_call(
        meet_kernel,
        out_shape=jax.ShapeDtypeStruct((rows, width), bf16),
        compiler_params=params(),
        name="meet",
    )(*parts)


def around(value, axis, stride=1, ring=None):
    size = lax.axis_size(axis)
    ring = ring or size

    def to(i, d):
        at = i // stride % ring
        return i + ((at + d) % ring - at) * stride

    return [lax.ppermute(value, axis, [(i, to(i, d)) for i in range(size)]) for d in range(1, ring)]


def after_all(value, *others):
    return lax.optimization_barrier((value, others))[0]


def local(
    q_light, k_light, v_light, q_heavy, k_heavy, v_heavy, enc_kv, dec_queries, query_ids, key_ids
):
    n_seq = lax.axis_size(TOKENS)
    n_fine = lax.axis_size("fine")
    side = 4
    width = q_light.shape[2]

    row = jnp.concatenate([enc_kv[0]] + around(enc_kv[0], "fine", 1, side), axis=0)
    enc = [row] + around(row, "fine", side, n_fine // side)
    chunks = pack(q_heavy[0], k_heavy[0], v_heavy[0])
    group = lax.all_to_all(after_all(chunks, row), "fine", 0, 0, tiled=True)

    dec_rows = dec_queries.shape[1] // n_fine
    part = decode(dec_queries[0], enc, dec_rows)
    share = meet([part] + around(part, "coarse"), dec_rows, width)
    decoded = lax.all_gather(share, "fine", axis=0, tiled=True)[None]

    own = pick(key_ids, after_all(group, share)).reshape(KGRP * BLOCK, LANES)
    routed = [own] + around(own, "coarse")

    light_kv = jnp.concatenate([k_light[0], v_light[0]], axis=1)
    light_kv = after_all(light_kv, own)
    up = [(i, i + 1) for i in range(n_seq - 1)]
    prev = lax.ppermute(light_kv, TOKENS, up)
    after = lax.ppermute(light_kv, TOKENS, [(b, a) for a, b in up])

    heavy = heavy_attend(group, routed)
    q_light = after_all(q_light, heavy)
    heavy = lax.all_to_all(heavy, "fine", 0, 0, tiled=True)

    light = light_attend(q_light[0], k_light[0], v_light[0], prev, after)
    encoded = join(query_ids, light, heavy)[None]
    return (encoded, decoded)


def solution(mesh):
    seq = P("doc", TOKENS, None)
    whole = P("doc", None, None)
    return jax.shard_map(
        local,
        mesh=mesh,
        in_specs=(seq,) * 7 + (whole, P("doc", None), P("doc", None)),
        out_specs=(seq, whole),
        check_vma=False,
    )
```

```python
import jax
import jax.numpy as jnp
from jax import lax
from jax.experimental import pallas as pl
from jax.experimental.pallas import tpu as pltpu
from jax.sharding import PartitionSpec as P

HEAD = 64
LANES = 2 * HEAD
BLOCK = 128
KGRP = 8
HALF = BLOCK // 2
SCALE = HEAD**-0.5
LOG2E = 1.4426950408889634
TOKENS = ("coarse", "fine")
VMEM = 48 * 1024 * 1024

f32 = jnp.float32
bf16 = jnp.bfloat16


def params(**kw):
    return pltpu.CompilerParams(vmem_limit_bytes=VMEM, **kw)


def lane_ids(shape):
    return lax.broadcasted_iota(jnp.int32, shape, len(shape) - 1)


def nt(a, b):
    return lax.dot_general(a, b, (((1,), (1,)), ((), ())), preferred_element_type=f32)


def nn(a, b):
    return jnp.dot(a, b, preferred_element_type=f32)


def pack_kernel(q_hbm, k_hbm, v_hbm, out, q, k, v, sem):
    copies = [
        pltpu.make_async_copy(src, dst, sem.at[n])
        for n, (src, dst) in enumerate(((k_hbm, k), (v_hbm, v), (q_hbm, q)))
    ]
    for c in copies:
        c.start()
    heads = out.shape[0]
    copies[0].wait()
    copies[1].wait()
    for h in range(heads):
        cols = slice(h * HEAD, (h + 1) * HEAD)
        out[h, :BLOCK] = jnp.concatenate([k[:, cols], v[:, cols]], axis=1)
    copies[2].wait()
    for h in range(heads):
        qh = q[:, h * HEAD : (h + 1) * HEAD]
        out[h, BLOCK:] = jnp.concatenate([qh[:HALF], qh[HALF:]], axis=1)


def pack(q, k, v):
    heads = q.shape[1] // HEAD
    hbm = pl.BlockSpec(memory_space=pltpu.HBM)
    return pl.pallas_call(
        pack_kernel,
        in_specs=[hbm] * 3,
        out_shape=jax.ShapeDtypeStruct((heads, BLOCK + HALF, LANES), bf16),
        scratch_shapes=[pltpu.VMEM(x.shape, bf16) for x in (q, k, v)]
        + [pltpu.SemaphoreType.DMA((3,))],
        compiler_params=params(),
        name="pack",
    )(*(pltpu.with_memory_space_constraint(x, pltpu.HBM) for x in (q, k, v)))


def pick_kernel(ids, kv, out):
    group = lax.axis_index("coarse")
    for s in range(KGRP):
        out[s] = kv[ids[0, group * KGRP + s] - group * kv.shape[0], :BLOCK]


def pick(ids, kv):
    return pl.pallas_call(
        pick_kernel,
        out_shape=jax.ShapeDtypeStruct((KGRP, BLOCK, LANES), bf16),
        in_specs=[pl.BlockSpec(memory_space=pltpu.SMEM), pl.BlockSpec(memory_space=pltpu.VMEM)],
        compiler_params=params(),
        name="pick",
    )(ids, kv)


def with_ones(kv):
    return jnp.where(lane_ids(kv.shape) < HEAD, jnp.ones_like(kv), kv)


def summed(q, keys, values):
    peak = total = None
    for k, v in zip(keys, values):
        s = nt(q, k)
        top = s.max(axis=1, keepdims=True)
        top = top if peak is None else jnp.maximum(peak, top)
        o = nn(jnp.exp2((s - top) * (SCALE * LOG2E)).astype(bf16), v)
        total = o if peak is None else total * jnp.exp2((peak - top) * (SCALE * LOG2E)) + o
        peak = top
    return total, peak


def heavy_kernel(q, kv0, kv1, kv2, kv3, out):
    rows = q.shape[0] * HALF
    both = q[:, BLOCK:].reshape(rows, LANES)
    zero = jnp.zeros((rows, HEAD), bf16)
    keys = [kv[...] for kv in (kv0, kv1, kv2, kv3)]
    vals = [with_ones(k) for k in keys]
    a, _ = summed(jnp.concatenate([both[:, :HEAD], zero], axis=1), keys, vals)
    b, _ = summed(jnp.concatenate([both[:, HEAD:], zero], axis=1), keys, vals)
    low = lane_ids(a.shape) < HEAD
    top = jnp.where(low, pltpu.roll(a, HEAD, 1), b)
    sums = jnp.where(low, a, pltpu.roll(b, HEAD, 1))
    out[...] = (top / sums).astype(bf16).reshape(out.shape)


def heavy_attend(q_kv, kvs):
    blocks = q_kv.shape[0]
    return pl.pallas_call(
        heavy_kernel,
        out_shape=jax.ShapeDtypeStruct((blocks, HALF, LANES), bf16),
        compiler_params=params(),
        cost_estimate=pl.CostEstimate(flops=10_000_000_000, transcendentals=8_000_000, bytes_accessed=2_000_000),
        name="heavy",
    )(q_kv, *kvs)


def light_kernel(q, k, v, prev, after, out):
    here = lax.axis_index(TOKENS)
    last = lax.axis_size(TOKENS) - 1
    rows, width = q.shape
    low = lane_ids((rows, LANES)) < HEAD
    i = lax.broadcasted_iota(jnp.int32, (2 * rows, BLOCK), 0) % rows
    j = lax.broadcasted_iota(jnp.int32, (2 * rows, BLOCK), 1)
    sees_prev = (j > i) & (here > 0)
    sees_next = (j < i) & (here < last)
    for p in range(width // LANES):
        c = slice(p * LANES, (p + 1) * LANES)
        cv = slice(width + p * LANES, width + (p + 1) * LANES)
        qq = q[:, c]
        zero = jnp.zeros_like(qq)
        two = jnp.concatenate([jnp.where(low, qq, zero), jnp.where(low, zero, qq)], axis=0)
        own = nt(two, k[:, c])
        left = jnp.where(sees_prev, nt(two, prev[:, c]), f32(-1e30))
        right = jnp.where(sees_next, nt(two, after[:, c]), f32(-1e30))
        peak = jnp.maximum(jnp.maximum(own, left), right).max(axis=1, keepdims=True)
        po, pp, pn = (jnp.exp2((s - peak) * (SCALE * LOG2E)) for s in (own, left, right))
        total = (po + pp + pn).sum(axis=1, keepdims=True)
        o = nn(po.astype(bf16), v[:, c]) + nn(pp.astype(bf16), prev[:, cv]) + nn(pn.astype(bf16), after[:, cv])
        o = o / total
        out[:, c] = jnp.where(low, o[:rows], o[rows:])


def light_attend(q, k, v, prev, after):
    return pl.pallas_call(
        light_kernel,
        out_shape=jax.ShapeDtypeStruct(q.shape, f32),
        compiler_params=params(),
        cost_estimate=pl.CostEstimate(flops=3_000_000_000, transcendentals=800_000, bytes_accessed=2_000_000),
        name="light",
    )(q, k, v, prev, after)


def join_kernel(ids, light, heavy, out):
    here = lax.axis_index(TOKENS)
    count = jnp.int32(0)
    for n in range(ids.shape[1]):
        count = count + jnp.where(ids[0, n] == here, 1, 0)
    scale = count.astype(f32)
    for p in range(heavy.shape[0] // 2):
        e, o = heavy[2 * p], heavy[2 * p + 1]
        for n in range(2):
            rows, lanes = slice(n * HALF, (n + 1) * HALF), slice(n * HEAD, (n + 1) * HEAD)
            cols = slice(p * LANES, (p + 1) * LANES)
            both = jnp.concatenate([e[:, lanes], o[:, lanes]], axis=1)
            out[rows, cols] = (light[rows, cols] + both.astype(f32) * scale).astype(bf16)


def join(ids, light, heavy):
    vmem = pl.BlockSpec(memory_space=pltpu.VMEM)
    return pl.pallas_call(
        join_kernel,
        in_specs=[pl.BlockSpec(memory_space=pltpu.SMEM), vmem, vmem],
        out_shape=jax.ShapeDtypeStruct(light.shape, bf16),
        compiler_params=params(),
        name="join",
    )(ids, light, heavy)


def decode_kernel(q_hbm, e0, e1, e2, e3, out, q, sem):
    rows, width = q.shape
    at = pl.multiple_of(lax.axis_index("fine") * rows, rows)
    copy = pltpu.make_async_copy(q_hbm.at[pl.ds(at, rows)], q, sem)
    copy.start()
    copy.wait()
    zero = jnp.zeros((rows, HEAD), bf16)
    stack = jnp.concatenate(
        [
            jnp.concatenate([q[:, h * HEAD : (h + 1) * HEAD], zero], axis=1)
            for h in range(width // HEAD)
        ],
        axis=0,
    )
    keys = [e[...] for e in (e0, e1, e2, e3)]
    vals = [with_ones(k) for k in keys]
    total, peak = summed(stack, keys, vals)
    lane = lane_ids(total.shape)
    level = peak * SCALE + jnp.log(total)
    hi = level.astype(bf16).astype(f32)
    mid = (level - hi).astype(bf16).astype(f32)
    least = level - hi - mid
    parts = jnp.where(lane < 16, hi, jnp.where(lane < 32, mid, least))
    ratio = total / pltpu.roll(total, HEAD, 1)
    out[...] = jnp.where(lane < HEAD, parts, ratio).astype(bf16)


def decode(q, enc, rows):
    width = q.shape[1]
    vmem = pl.BlockSpec(memory_space=pltpu.VMEM)
    return pl.pallas_call(
        decode_kernel,
        in_specs=[pl.BlockSpec(memory_space=pltpu.HBM)] + [vmem] * len(enc),
        out_shape=jax.ShapeDtypeStruct((rows * (width // HEAD), LANES), bf16),
        scratch_shapes=[pltpu.VMEM((rows, width), bf16), pltpu.SemaphoreType.DMA(())],
        compiler_params=params(),
        cost_estimate=pl.CostEstimate(flops=1_000_000_000, transcendentals=1_000_000, bytes_accessed=1_000_000),
        name="decode",
    )(q, *enc)


def meet_kernel(a, b, c, d, out):
    parts = [x[...].astype(f32) for x in (a, b, c, d)]
    levels = [x[:, 0:1] + x[:, 16:17] + x[:, 32:33] for x in parts]
    peak = jnp.maximum(jnp.maximum(levels[0], levels[1]), jnp.maximum(levels[2], levels[3]))
    scales = [jnp.exp(n - peak) for n in levels]
    total = scales[0] + scales[1] + scales[2] + scales[3]
    value = parts[0] * scales[0]
    for x, s in zip(parts[1:], scales[1:]):
        value = value + x * s
    value = (value / total).astype(bf16)
    rows, width = out.shape
    for p in range(width // LANES):
        e = value[2 * p * rows : (2 * p + 1) * rows, HEAD:]
        o = value[(2 * p + 1) * rows : (2 * p + 2) * rows, HEAD:]
        out[:, p * LANES : (p + 1) * LANES] = jnp.concatenate([e, o], axis=1)


def meet(parts, rows, width):
    return pl.pallas_call(
        meet_kernel,
        out_shape=jax.ShapeDtypeStruct((rows, width), bf16),
        compiler_params=params(),
        name="meet",
    )(*parts)


def spread_kernel(own, down1, down2, down3, out):
    place = lax.axis_index("fine")
    side = own.shape[0]
    row, col = place // side, place % side
    for dr, got in enumerate((own, down1, down2, down3)):
        at = (row + side - dr) % side * side
        for dc in range(side):
            out[at + (col + side - dc) % side] = got[dc]


def spread(rows):
    side, count, width = rows[0].shape
    return pl.pallas_call(
        spread_kernel,
        out_shape=jax.ShapeDtypeStruct((len(rows) * side, count, width), bf16),
        compiler_params=params(),
        name="spread",
    )(*rows)


def around(value, axis, stride=1, ring=None):
    size = lax.axis_size(axis)
    ring = ring or size

    def to(i, d):
        at = i // stride % ring
        return i + ((at + d) % ring - at) * stride

    return [lax.ppermute(value, axis, [(i, to(i, d)) for i in range(size)]) for d in range(1, ring)]


def after_all(value, *others):
    return lax.optimization_barrier((value, others))[0]


def local(
    q_light, k_light, v_light, q_heavy, k_heavy, v_heavy, enc_kv, dec_queries, query_ids, key_ids
):
    n_seq = lax.axis_size(TOKENS)
    n_fine = lax.axis_size("fine")
    side = 4
    width = q_light.shape[2]

    light_kv = jnp.concatenate([k_light[0], v_light[0]], axis=1)
    up = [(i, i + 1) for i in range(n_seq - 1)]
    prev = lax.ppermute(light_kv, TOKENS, up)
    after = lax.ppermute(light_kv, TOKENS, [(b, a) for a, b in up])

    def rows_of(value):
        return jnp.concatenate([value] + around(value, "fine", 1, side), axis=0)

    def square(row):
        return [row] + around(row, "fine", side, n_fine // side)

    row = rows_of(enc_kv[0])
    enc = square(row)
    chunks = pack(q_heavy[0], k_heavy[0], v_heavy[0])
    group = lax.all_to_all(after_all(chunks, enc[1]), "fine", 0, 0, tiled=True)

    dec_rows = dec_queries.shape[1] // n_fine
    part = decode(dec_queries[0], enc, dec_rows)
    light = light_attend(after_all(q_light[0], part), k_light[0], v_light[0], prev, after)
    share = meet([after_all(part, light)] + around(part, "coarse"), dec_rows, width)

    own = pick(key_ids, after_all(group, share)).reshape(KGRP * BLOCK, LANES)
    routed = [own] + around(own, "coarse")
    shares = square(rows_of(after_all(share, own)[None]))

    heavy = heavy_attend(group, routed)
    shares = after_all(shares, heavy)
    heavy = lax.all_to_all(heavy, "fine", 0, 0, tiled=True)
    decoded = spread(shares).reshape(1, -1, width)
    encoded = join(query_ids, light, heavy)[None]
    return (encoded, decoded)


def solution(mesh):
    seq = P("doc", TOKENS, None)
    whole = P("doc", None, None)
    return jax.shard_map(
        local,
        mesh=mesh,
        in_specs=(seq,) * 7 + (whole, P("doc", None), P("doc", None)),
        out_specs=(seq, whole),
        check_vma=False,
    )
```

```python
import jax
import jax.numpy as jnp
from jax import lax
from jax.experimental import pallas as pl
from jax.experimental.pallas import tpu as pltpu
from jax.sharding import PartitionSpec as P

HEAD = 64
LANES = 2 * HEAD
BLOCK = 128
KGRP = 8
HALF = BLOCK // 2
SCALE = HEAD**-0.5
LOG2E = 1.4426950408889634
TOKENS = ("coarse", "fine")
VMEM = 48 * 1024 * 1024

f32 = jnp.float32
bf16 = jnp.bfloat16


def params(**kw):
    return pltpu.CompilerParams(vmem_limit_bytes=VMEM, **kw)


def lane_ids(shape):
    return lax.broadcasted_iota(jnp.int32, shape, len(shape) - 1)


def nt(a, b):
    return lax.dot_general(a, b, (((1,), (1,)), ((), ())), preferred_element_type=f32)


def nn(a, b):
    return jnp.dot(a, b, preferred_element_type=f32)


def pack_kernel(q_hbm, k_hbm, v_hbm, out, q, k, v, sem):
    copies = [
        pltpu.make_async_copy(src, dst, sem.at[n])
        for n, (src, dst) in enumerate(((k_hbm, k), (v_hbm, v), (q_hbm, q)))
    ]
    for c in copies:
        c.start()
    heads = out.shape[0]
    copies[0].wait()
    copies[1].wait()
    for h in range(heads):
        cols = slice(h * HEAD, (h + 1) * HEAD)
        out[h, :BLOCK] = jnp.concatenate([k[:, cols], v[:, cols]], axis=1)
    copies[2].wait()
    for h in range(heads):
        qh = q[:, h * HEAD : (h + 1) * HEAD]
        out[h, BLOCK:] = jnp.concatenate([qh[:HALF], qh[HALF:]], axis=1)


def pack(q, k, v):
    heads = q.shape[1] // HEAD
    hbm = pl.BlockSpec(memory_space=pltpu.HBM)
    return pl.pallas_call(
        pack_kernel,
        in_specs=[hbm] * 3,
        out_shape=jax.ShapeDtypeStruct((heads, BLOCK + HALF, LANES), bf16),
        scratch_shapes=[pltpu.VMEM(x.shape, bf16) for x in (q, k, v)]
        + [pltpu.SemaphoreType.DMA((3,))],
        compiler_params=params(),
        name="pack",
    )(*(pltpu.with_memory_space_constraint(x, pltpu.HBM) for x in (q, k, v)))


def pick_kernel(ids, kv, out):
    group = lax.axis_index("coarse")
    for s in range(KGRP):
        out[s] = kv[ids[0, group * KGRP + s] - group * kv.shape[0], :BLOCK]


def pick(ids, kv):
    return pl.pallas_call(
        pick_kernel,
        out_shape=jax.ShapeDtypeStruct((KGRP, BLOCK, LANES), bf16),
        in_specs=[pl.BlockSpec(memory_space=pltpu.SMEM), pl.BlockSpec(memory_space=pltpu.VMEM)],
        compiler_params=params(),
        name="pick",
    )(ids, kv)


def with_ones(kv):
    return jnp.where(lane_ids(kv.shape) < HEAD, jnp.ones_like(kv), kv)


def summed(q, keys, values):
    peak = total = None
    for k, v in zip(keys, values):
        s = nt(q, k)
        top = s.max(axis=1, keepdims=True)
        top = top if peak is None else jnp.maximum(peak, top)
        o = nn(jnp.exp2((s - top) * (SCALE * LOG2E)).astype(bf16), v)
        total = o if peak is None else total * jnp.exp2((peak - top) * (SCALE * LOG2E)) + o
        peak = top
    return total, peak


def heavy_kernel(q, kv0, kv1, kv2, kv3, out):
    rows = q.shape[0] * HALF
    both = q[:, BLOCK:].reshape(rows, LANES)
    zero = jnp.zeros((rows, HEAD), bf16)
    keys = [kv[...] for kv in (kv0, kv1, kv2, kv3)]
    vals = [with_ones(k) for k in keys]
    a, _ = summed(jnp.concatenate([both[:, :HEAD], zero], axis=1), keys, vals)
    b, _ = summed(jnp.concatenate([both[:, HEAD:], zero], axis=1), keys, vals)
    low = lane_ids(a.shape) < HEAD
    top = jnp.where(low, pltpu.roll(a, HEAD, 1), b)
    sums = jnp.where(low, a, pltpu.roll(b, HEAD, 1))
    out[...] = (top / sums).astype(bf16).reshape(out.shape)


def heavy_attend(q_kv, kvs):
    blocks = q_kv.shape[0]
    return pl.pallas_call(
        heavy_kernel,
        out_shape=jax.ShapeDtypeStruct((blocks, HALF, LANES), bf16),
        compiler_params=params(),
        cost_estimate=pl.CostEstimate(flops=10_000_000_000, transcendentals=8_000_000, bytes_accessed=2_000_000),
        name="heavy",
    )(q_kv, *kvs)


def light_kernel(q, k, v, prev, after, out):
    here = lax.axis_index(TOKENS)
    last = lax.axis_size(TOKENS) - 1
    rows, width = q.shape
    low = lane_ids((rows, LANES)) < HEAD
    i = lax.broadcasted_iota(jnp.int32, (2 * rows, BLOCK), 0) % rows
    j = lax.broadcasted_iota(jnp.int32, (2 * rows, BLOCK), 1)
    sees_prev = (j > i) & (here > 0)
    sees_next = (j < i) & (here < last)
    for p in range(width // LANES):
        c = slice(p * LANES, (p + 1) * LANES)
        cv = slice(width + p * LANES, width + (p + 1) * LANES)
        qq = q[:, c]
        zero = jnp.zeros_like(qq)
        two = jnp.concatenate([jnp.where(low, qq, zero), jnp.where(low, zero, qq)], axis=0)
        own = nt(two, k[:, c])
        left = jnp.where(sees_prev, nt(two, prev[:, c]), f32(-1e30))
        right = jnp.where(sees_next, nt(two, after[:, c]), f32(-1e30))
        peak = jnp.maximum(jnp.maximum(own, left), right).max(axis=1, keepdims=True)
        po, pp, pn = (jnp.exp2((s - peak) * (SCALE * LOG2E)) for s in (own, left, right))
        total = (po + pp + pn).sum(axis=1, keepdims=True)
        o = nn(po.astype(bf16), v[:, c]) + nn(pp.astype(bf16), prev[:, cv]) + nn(pn.astype(bf16), after[:, cv])
        o = o / total
        out[:, c] = jnp.where(low, o[:rows], o[rows:])


def light_attend(q, k, v, prev, after):
    return pl.pallas_call(
        light_kernel,
        out_shape=jax.ShapeDtypeStruct(q.shape, f32),
        compiler_params=params(),
        cost_estimate=pl.CostEstimate(flops=3_000_000_000, transcendentals=800_000, bytes_accessed=2_000_000),
        name="light",
    )(q, k, v, prev, after)


def join_kernel(ids, light, heavy, out):
    here = lax.axis_index(TOKENS)
    count = jnp.int32(0)
    for n in range(ids.shape[1]):
        count = count + jnp.where(ids[0, n] == here, 1, 0)
    scale = count.astype(f32)
    for p in range(heavy.shape[0] // 2):
        e, o = heavy[2 * p], heavy[2 * p + 1]
        for n in range(2):
            rows, lanes = slice(n * HALF, (n + 1) * HALF), slice(n * HEAD, (n + 1) * HEAD)
            cols = slice(p * LANES, (p + 1) * LANES)
            both = jnp.concatenate([e[:, lanes], o[:, lanes]], axis=1)
            out[rows, cols] = (light[rows, cols] + both.astype(f32) * scale).astype(bf16)


def join(ids, light, heavy):
    vmem = pl.BlockSpec(memory_space=pltpu.VMEM)
    return pl.pallas_call(
        join_kernel,
        in_specs=[pl.BlockSpec(memory_space=pltpu.SMEM), vmem, vmem],
        out_shape=jax.ShapeDtypeStruct(light.shape, bf16),
        compiler_params=params(),
        name="join",
    )(ids, light, heavy)


def decode_kernel(q_hbm, e0, e1, e2, e3, out, q, sem):
    rows, width = q.shape
    at = pl.multiple_of(lax.axis_index("fine") * rows, rows)
    copy = pltpu.make_async_copy(q_hbm.at[pl.ds(at, rows)], q, sem)
    copy.start()
    copy.wait()
    zero = jnp.zeros((rows, HEAD), bf16)
    stack = jnp.concatenate(
        [
            jnp.concatenate([q[:, h * HEAD : (h + 1) * HEAD], zero], axis=1)
            for h in range(width // HEAD)
        ],
        axis=0,
    )
    keys = [e[...] for e in (e0, e1, e2, e3)]
    vals = [with_ones(k) for k in keys]
    total, peak = summed(stack, keys, vals)
    lane = lane_ids(total.shape)
    level = peak * SCALE + jnp.log(total)
    hi = level.astype(bf16).astype(f32)
    mid = (level - hi).astype(bf16).astype(f32)
    least = level - hi - mid
    parts = jnp.where(lane < 16, hi, jnp.where(lane < 32, mid, least))
    ratio = total / pltpu.roll(total, HEAD, 1)
    out[...] = jnp.where(lane < HEAD, parts, ratio).astype(bf16)


def decode(q, enc, rows):
    width = q.shape[1]
    vmem = pl.BlockSpec(memory_space=pltpu.VMEM)
    return pl.pallas_call(
        decode_kernel,
        in_specs=[pl.BlockSpec(memory_space=pltpu.HBM)] + [vmem] * len(enc),
        out_shape=jax.ShapeDtypeStruct((rows * (width // HEAD), LANES), bf16),
        scratch_shapes=[pltpu.VMEM((rows, width), bf16), pltpu.SemaphoreType.DMA(())],
        compiler_params=params(),
        cost_estimate=pl.CostEstimate(flops=1_000_000_000, transcendentals=1_000_000, bytes_accessed=1_000_000),
        name="decode",
    )(q, *enc)


def meet_kernel(a, b, c, d, out):
    parts = [x[...].astype(f32) for x in (a, b, c, d)]
    levels = [x[:, 0:1] + x[:, 16:17] + x[:, 32:33] for x in parts]
    peak = jnp.maximum(jnp.maximum(levels[0], levels[1]), jnp.maximum(levels[2], levels[3]))
    scales = [jnp.exp(n - peak) for n in levels]
    total = scales[0] + scales[1] + scales[2] + scales[3]
    value = parts[0] * scales[0]
    for x, s in zip(parts[1:], scales[1:]):
        value = value + x * s
    value = (value / total).astype(bf16)
    rows, width = out.shape
    for p in range(width // LANES):
        e = value[2 * p * rows : (2 * p + 1) * rows, HEAD:]
        o = value[(2 * p + 1) * rows : (2 * p + 2) * rows, HEAD:]
        out[:, p * LANES : (p + 1) * LANES] = jnp.concatenate([e, o], axis=1)


def meet(parts, rows, width):
    return pl.pallas_call(
        meet_kernel,
        out_shape=jax.ShapeDtypeStruct((rows, width), bf16),
        compiler_params=params(),
        name="meet",
    )(*parts)


def stack_kernel(*refs):
    parts, out = refs[:4], refs[-1]
    size = parts[0].shape[0]
    for n, part in enumerate(parts):
        out[n * size : (n + 1) * size] = part[...]


def stack(parts, *others):
    first = parts[0]
    specs = [pl.BlockSpec(memory_space=pltpu.VMEM)] * len(parts)
    return pl.pallas_call(
        stack_kernel,
        in_specs=specs + [pl.BlockSpec(memory_space=pl.ANY)] * len(others),
        out_shape=jax.ShapeDtypeStruct((len(parts) * first.shape[0],) + first.shape[1:], first.dtype),
        compiler_params=params(),
        name="stack",
    )(*parts, *others)


def spread_kernel(own, down1, down2, down3, out):
    place = lax.axis_index("fine")
    side = own.shape[0]
    row, col = place // side, place % side
    for dr, got in enumerate((own, down1, down2, down3)):
        at = (row + side - dr) % side * side
        for dc in range(side):
            out[at + (col + side - dc) % side] = got[dc]


def spread(rows):
    side, count, width = rows[0].shape
    return pl.pallas_call(
        spread_kernel,
        out_shape=jax.ShapeDtypeStruct((len(rows) * side, count, width), bf16),
        compiler_params=params(),
        name="spread",
    )(*rows)


def around(value, axis, stride=1, ring=None):
    size = lax.axis_size(axis)
    ring = ring or size

    def to(i, d):
        at = i // stride % ring
        return i + ((at + d) % ring - at) * stride

    return [lax.ppermute(value, axis, [(i, to(i, d)) for i in range(size)]) for d in range(1, ring)]


def after_all(value, *others):
    return lax.optimization_barrier((value, others))[0]


def local(
    q_light, k_light, v_light, q_heavy, k_heavy, v_heavy, enc_kv, dec_queries, query_ids, key_ids
):
    n_seq = lax.axis_size(TOKENS)
    n_fine = lax.axis_size("fine")
    side = 4
    width = q_light.shape[2]

    light_kv = jnp.concatenate([k_light[0], v_light[0]], axis=1)

    def rows_of(value):
        return [value] + around(value, "fine", 1, side)

    def square(row):
        return [row] + around(row, "fine", side, n_fine // side)

    enc = square(stack(rows_of(enc_kv[0]), light_kv))
    chunks = pack(q_heavy[0], k_heavy[0], v_heavy[0])
    group = lax.all_to_all(after_all(chunks, enc[1], enc[2], enc[3]), "fine", 0, 0, tiled=True)

    dec_rows = dec_queries.shape[1] // n_fine
    part = decode(dec_queries[0], enc, dec_rows)
    share = meet([part] + around(part, "coarse"), dec_rows, width)

    own = pick(key_ids, after_all(group, share)).reshape(KGRP * BLOCK, LANES)
    routed = [own] + around(own, "coarse")
    shares = square(stack(rows_of(after_all(share, own)[None])))

    light_kv = after_all(light_kv, routed)
    up = [(i, i + 1) for i in range(n_seq - 1)]
    prev = lax.ppermute(light_kv, TOKENS, up)
    after = lax.ppermute(light_kv, TOKENS, [(b, a) for a, b in up])

    heavy = heavy_attend(group, routed)
    shares, q_light = after_all((shares, q_light), heavy)
    heavy = lax.all_to_all(heavy, "fine", 0, 0, tiled=True)
    light = light_attend(q_light[0], k_light[0], v_light[0], prev, after)
    decoded = spread(shares).reshape(1, -1, width)
    encoded = join(query_ids, light, heavy)[None]
    return (encoded, decoded)


def solution(mesh):
    seq = P("doc", TOKENS, None)
    whole = P("doc", None, None)
    return jax.shard_map(
        local,
        mesh=mesh,
        in_specs=(seq,) * 7 + (whole, P("doc", None), P("doc", None)),
        out_specs=(seq, whole),
        check_vma=False,
    )
```

```python
import jax
import jax.numpy as jnp
from jax import lax
from jax.experimental import pallas as pl
from jax.experimental.pallas import tpu as pltpu
from jax.sharding import PartitionSpec as P

HEAD = 64
LANES = 2 * HEAD
BLOCK = 128
KGRP = 8
HALF = BLOCK // 2
SCALE = HEAD**-0.5
LOG2E = 1.4426950408889634
TOKENS = ("coarse", "fine")
VMEM = 48 * 1024 * 1024

f32 = jnp.float32
bf16 = jnp.bfloat16


def params(**kw):
    return pltpu.CompilerParams(vmem_limit_bytes=VMEM, **kw)


def lane_ids(shape):
    return lax.broadcasted_iota(jnp.int32, shape, len(shape) - 1)


def nt(a, b):
    return lax.dot_general(a, b, (((1,), (1,)), ((), ())), preferred_element_type=f32)


def nn(a, b):
    return jnp.dot(a, b, preferred_element_type=f32)


def pack_kernel(q_hbm, k_hbm, v_hbm, out, q, k, v, sem):
    copies = [
        pltpu.make_async_copy(src, dst, sem.at[n])
        for n, (src, dst) in enumerate(((k_hbm, k), (v_hbm, v), (q_hbm, q)))
    ]
    for c in copies:
        c.start()
    heads = out.shape[0]
    copies[0].wait()
    copies[1].wait()
    for h in range(heads):
        cols = slice(h * HEAD, (h + 1) * HEAD)
        out[h, :BLOCK] = jnp.concatenate([k[:, cols], v[:, cols]], axis=1)
    copies[2].wait()
    for h in range(heads):
        qh = q[:, h * HEAD : (h + 1) * HEAD]
        out[h, BLOCK:] = jnp.concatenate([qh[:HALF], qh[HALF:]], axis=1)


def pack(q, k, v):
    heads = q.shape[1] // HEAD
    hbm = pl.BlockSpec(memory_space=pltpu.HBM)
    return pl.pallas_call(
        pack_kernel,
        in_specs=[hbm] * 3,
        out_shape=jax.ShapeDtypeStruct((heads, BLOCK + HALF, LANES), bf16),
        scratch_shapes=[pltpu.VMEM(x.shape, bf16) for x in (q, k, v)]
        + [pltpu.SemaphoreType.DMA((3,))],
        compiler_params=params(),
        name="pack",
    )(*(pltpu.with_memory_space_constraint(x, pltpu.HBM) for x in (q, k, v)))


def pick_kernel(ids, kv, out):
    group = lax.axis_index("coarse")
    for s in range(KGRP):
        out[s] = kv[ids[0, group * KGRP + s] - group * kv.shape[0], :BLOCK]


def pick(ids, kv):
    return pl.pallas_call(
        pick_kernel,
        out_shape=jax.ShapeDtypeStruct((KGRP, BLOCK, LANES), bf16),
        in_specs=[pl.BlockSpec(memory_space=pltpu.SMEM), pl.BlockSpec(memory_space=pltpu.VMEM)],
        compiler_params=params(),
        name="pick",
    )(ids, kv)


def with_ones(kv):
    return jnp.where(lane_ids(kv.shape) < HEAD, jnp.ones_like(kv), kv)


def summed(q, keys, values):
    peak = total = None
    for k, v in zip(keys, values):
        s = nt(q, k)
        top = s.max(axis=1, keepdims=True)
        top = top if peak is None else jnp.maximum(peak, top)
        o = nn(jnp.exp2((s - top) * (SCALE * LOG2E)).astype(bf16), v)
        total = o if peak is None else total * jnp.exp2((peak - top) * (SCALE * LOG2E)) + o
        peak = top
    return total, peak


def heavy_kernel(q, kv0, kv1, kv2, kv3, out):
    rows = q.shape[0] * HALF
    both = q[:, BLOCK:].reshape(rows, LANES)
    zero = jnp.zeros((rows, HEAD), bf16)
    keys = [kv[...] for kv in (kv0, kv1, kv2, kv3)]
    vals = [with_ones(k) for k in keys]
    a, _ = summed(jnp.concatenate([both[:, :HEAD], zero], axis=1), keys, vals)
    b, _ = summed(jnp.concatenate([both[:, HEAD:], zero], axis=1), keys, vals)
    low = lane_ids(a.shape) < HEAD
    top = jnp.where(low, pltpu.roll(a, HEAD, 1), b)
    sums = jnp.where(low, a, pltpu.roll(b, HEAD, 1))
    out[...] = (top / sums).astype(bf16).reshape(out.shape)


def heavy_attend(q_kv, kvs):
    blocks = q_kv.shape[0]
    return pl.pallas_call(
        heavy_kernel,
        out_shape=jax.ShapeDtypeStruct((blocks, HALF, LANES), bf16),
        compiler_params=params(),
        cost_estimate=pl.CostEstimate(flops=10_000_000_000, transcendentals=8_000_000, bytes_accessed=2_000_000),
        name="heavy",
    )(q_kv, *kvs)


def light_kernel(q, k, v, even, odd, out):
    here = lax.axis_index(TOKENS)
    last = lax.axis_size(TOKENS) - 1
    rows, width = q.shape
    low = lane_ids((rows, LANES)) < HEAD
    i = lax.broadcasted_iota(jnp.int32, (2 * rows, BLOCK), 0) % rows
    j = lax.broadcasted_iota(jnp.int32, (2 * rows, BLOCK), 1)
    ahead = (j - i) * (1 - 2 * (here % 2))
    sees_even = ahead < 0
    sees_odd = (ahead > 0) & (here > 0) & (here < last)
    for p in range(width // LANES):
        c = slice(p * LANES, (p + 1) * LANES)
        cv = slice(width + p * LANES, width + (p + 1) * LANES)
        qq = q[:, c]
        zero = jnp.zeros_like(qq)
        two = jnp.concatenate([jnp.where(low, qq, zero), jnp.where(low, zero, qq)], axis=0)
        own = nt(two, k[:, c])
        first = jnp.where(sees_even, nt(two, even[:, c]), f32(-1e30))
        second = jnp.where(sees_odd, nt(two, odd[:, c]), f32(-1e30))
        peak = jnp.maximum(jnp.maximum(own, first), second).max(axis=1, keepdims=True)
        po, pe, pd = (jnp.exp2((s - peak) * (SCALE * LOG2E)) for s in (own, first, second))
        total = (po + pe + pd).sum(axis=1, keepdims=True)
        o = nn(po.astype(bf16), v[:, c]) + nn(pe.astype(bf16), even[:, cv]) + nn(pd.astype(bf16), odd[:, cv])
        o = o / total
        out[:, c] = jnp.where(low, o[:rows], o[rows:])


def light_attend(q, k, v, even, odd):
    return pl.pallas_call(
        light_kernel,
        out_shape=jax.ShapeDtypeStruct(q.shape, f32),
        compiler_params=params(),
        cost_estimate=pl.CostEstimate(flops=3_000_000_000, transcendentals=800_000, bytes_accessed=2_000_000),
        name="light",
    )(q, k, v, even, odd)


def join_kernel(ids, light, heavy, out):
    here = lax.axis_index(TOKENS)
    count = jnp.int32(0)
    for n in range(ids.shape[1]):
        count = count + jnp.where(ids[0, n] == here, 1, 0)
    scale = count.astype(f32)
    for p in range(heavy.shape[0] // 2):
        e, o = heavy[2 * p], heavy[2 * p + 1]
        for n in range(2):
            rows, lanes = slice(n * HALF, (n + 1) * HALF), slice(n * HEAD, (n + 1) * HEAD)
            cols = slice(p * LANES, (p + 1) * LANES)
            both = jnp.concatenate([e[:, lanes], o[:, lanes]], axis=1)
            out[rows, cols] = (light[rows, cols] + both.astype(f32) * scale).astype(bf16)


def join(ids, light, heavy):
    vmem = pl.BlockSpec(memory_space=pltpu.VMEM)
    return pl.pallas_call(
        join_kernel,
        in_specs=[pl.BlockSpec(memory_space=pltpu.SMEM), vmem, vmem],
        out_shape=jax.ShapeDtypeStruct(light.shape, bf16),
        compiler_params=params(),
        name="join",
    )(ids, light, heavy)


def decode_kernel(q_hbm, e0, e1, e2, e3, out, q, sem):
    rows, width = q.shape
    at = pl.multiple_of(lax.axis_index("fine") * rows, rows)
    copy = pltpu.make_async_copy(q_hbm.at[pl.ds(at, rows)], q, sem)
    copy.start()
    copy.wait()
    zero = jnp.zeros((rows, HEAD), bf16)
    stack = jnp.concatenate(
        [
            jnp.concatenate([q[:, h * HEAD : (h + 1) * HEAD], zero], axis=1)
            for h in range(width // HEAD)
        ],
        axis=0,
    )
    keys = [e[...] for e in (e0, e1, e2, e3)]
    vals = [with_ones(k) for k in keys]
    total, peak = summed(stack, keys, vals)
    lane = lane_ids(total.shape)
    level = peak * SCALE + jnp.log(total)
    hi = level.astype(bf16).astype(f32)
    mid = (level - hi).astype(bf16).astype(f32)
    least = level - hi - mid
    parts = jnp.where(lane < 16, hi, jnp.where(lane < 32, mid, least))
    ratio = total / pltpu.roll(total, HEAD, 1)
    out[...] = jnp.where(lane < HEAD, parts, ratio).astype(bf16)


def decode(q, enc, rows):
    width = q.shape[1]
    vmem = pl.BlockSpec(memory_space=pltpu.VMEM)
    return pl.pallas_call(
        decode_kernel,
        in_specs=[pl.BlockSpec(memory_space=pltpu.HBM)] + [vmem] * len(enc),
        out_shape=jax.ShapeDtypeStruct((rows * (width // HEAD), LANES), bf16),
        scratch_shapes=[pltpu.VMEM((rows, width), bf16), pltpu.SemaphoreType.DMA(())],
        compiler_params=params(),
        cost_estimate=pl.CostEstimate(flops=1_000_000_000, transcendentals=1_000_000, bytes_accessed=1_000_000),
        name="decode",
    )(q, *enc)


def meet_kernel(a, b, c, d, out):
    parts = [x[...].astype(f32) for x in (a, b, c, d)]
    levels = [x[:, 0:1] + x[:, 16:17] + x[:, 32:33] for x in parts]
    peak = jnp.maximum(jnp.maximum(levels[0], levels[1]), jnp.maximum(levels[2], levels[3]))
    scales = [jnp.exp(n - peak) for n in levels]
    total = scales[0] + scales[1] + scales[2] + scales[3]
    value = parts[0] * scales[0]
    for x, s in zip(parts[1:], scales[1:]):
        value = value + x * s
    value = (value / total).astype(bf16)
    rows, width = out.shape
    for p in range(width // LANES):
        e = value[2 * p * rows : (2 * p + 1) * rows, HEAD:]
        o = value[(2 * p + 1) * rows : (2 * p + 2) * rows, HEAD:]
        out[:, p * LANES : (p + 1) * LANES] = jnp.concatenate([e, o], axis=1)


def meet(parts, rows, width):
    return pl.pallas_call(
        meet_kernel,
        out_shape=jax.ShapeDtypeStruct((rows, width), bf16),
        compiler_params=params(),
        name="meet",
    )(*parts)


def stack_kernel(*refs):
    parts, out = refs[:4], refs[-1]
    size = parts[0].shape[0]
    for n, part in enumerate(parts):
        out[n * size : (n + 1) * size] = part[...]


def stack(parts, *others):
    first = parts[0]
    specs = [pl.BlockSpec(memory_space=pltpu.VMEM)] * len(parts)
    return pl.pallas_call(
        stack_kernel,
        in_specs=specs + [pl.BlockSpec(memory_space=pl.ANY)] * len(others),
        out_shape=jax.ShapeDtypeStruct((len(parts) * first.shape[0],) + first.shape[1:], first.dtype),
        compiler_params=params(),
        name="stack",
    )(*parts, *others)


def spread_kernel(own, other1, other2, other3, out):
    place = lax.axis_index("fine")
    side = own.shape[0]
    for dr, got in enumerate((own, other1, other2, other3)):
        for dc in range(side):
            out[place ^ (dr * side + dc)] = got[dc]


def spread(rows):
    side, count, width = rows[0].shape
    return pl.pallas_call(
        spread_kernel,
        out_shape=jax.ShapeDtypeStruct((len(rows) * side, count, width), bf16),
        compiler_params=params(),
        name="spread",
    )(*rows)


def around(value, axis, stride=1, ring=None):
    size = lax.axis_size(axis)
    ring = ring or size

    def pairs(d):
        return [(i, i + ((i // stride % ring ^ d) - i // stride % ring) * stride) for i in range(size)]

    return [lax.ppermute(value, axis, pairs(d)) for d in range(1, ring)]


def after_all(value, *others):
    return lax.optimization_barrier((value, others))[0]


def local(
    q_light, k_light, v_light, q_heavy, k_heavy, v_heavy, enc_kv, dec_queries, query_ids, key_ids
):
    n_seq = lax.axis_size(TOKENS)
    n_fine = lax.axis_size("fine")
    side = 4
    width = q_light.shape[2]

    light_kv = jnp.concatenate([k_light[0], v_light[0]], axis=1)

    def rows_of(value):
        return [value] + around(value, "fine", 1, side)

    def square(row):
        return [row] + around(row, "fine", side, n_fine // side)

    enc = square(stack(rows_of(enc_kv[0]), light_kv))
    chunks = pack(q_heavy[0], k_heavy[0], v_heavy[0])
    group = lax.all_to_all(after_all(chunks, enc[1], enc[2], enc[3]), "fine", 0, 0, tiled=True)

    dec_rows = dec_queries.shape[1] // n_fine
    part = decode(dec_queries[0], enc, dec_rows)
    share = meet([part] + around(part, "coarse"), dec_rows, width)

    own = pick(key_ids, after_all(group, share)).reshape(KGRP * BLOCK, LANES)
    routed = [own] + around(own, "coarse")
    shares = square(stack(rows_of(after_all(share, own)[None])))

    light_kv = after_all(light_kv, routed)
    even = lax.ppermute(light_kv, TOKENS, [(i, i ^ 1) for i in range(n_seq)])
    odd = lax.ppermute(light_kv, TOKENS, [(i, (i - 1 ^ 1) + 1) for i in range(1, n_seq - 1)])

    heavy = heavy_attend(group, routed)
    shares, q_light = after_all((shares, q_light), heavy)
    heavy = lax.all_to_all(heavy, "fine", 0, 0, tiled=True)
    light = light_attend(q_light[0], k_light[0], v_light[0], even, odd)
    decoded = spread(shares).reshape(1, -1, width)
    encoded = join(query_ids, light, heavy)[None]
    return (encoded, decoded)


def solution(mesh):
    seq = P("doc", TOKENS, None)
    whole = P("doc", None, None)
    return jax.shard_map(
        local,
        mesh=mesh,
        in_specs=(seq,) * 7 + (whole, P("doc", None), P("doc", None)),
        out_specs=(seq, whole),
        check_vma=False,
    )
```

```python
import jax
import jax.numpy as jnp
from jax import lax
from jax.experimental import pallas as pl
from jax.experimental.pallas import tpu as pltpu
from jax.sharding import PartitionSpec as P

HEAD = 64
LANES = 2 * HEAD
BLOCK = 128
KGRP = 8
HALF = BLOCK // 2
SCALE = HEAD**-0.5
LOG2E = 1.4426950408889634
TOKENS = ("coarse", "fine")
VMEM = 48 * 1024 * 1024

f32 = jnp.float32
bf16 = jnp.bfloat16


def params(**kw):
    return pltpu.CompilerParams(vmem_limit_bytes=VMEM, **kw)


def lane_ids(shape):
    return lax.broadcasted_iota(jnp.int32, shape, len(shape) - 1)


def nt(a, b):
    return lax.dot_general(a, b, (((1,), (1,)), ((), ())), preferred_element_type=f32)


def nn(a, b):
    return jnp.dot(a, b, preferred_element_type=f32)


def pack_kernel(q_hbm, k_hbm, v_hbm, out, q, k, v, sem):
    copies = [
        pltpu.make_async_copy(src, dst, sem.at[n])
        for n, (src, dst) in enumerate(((k_hbm, k), (v_hbm, v), (q_hbm, q)))
    ]
    for c in copies:
        c.start()
    heads = out.shape[0]
    copies[0].wait()
    copies[1].wait()
    for h in range(heads):
        cols = slice(h * HEAD, (h + 1) * HEAD)
        out[h, :BLOCK] = jnp.concatenate([k[:, cols], v[:, cols]], axis=1)
    copies[2].wait()
    for h in range(heads):
        qh = q[:, h * HEAD : (h + 1) * HEAD]
        out[h, BLOCK:] = jnp.concatenate([qh[:HALF], qh[HALF:]], axis=1)


def pack(q, k, v):
    heads = q.shape[1] // HEAD
    hbm = pl.BlockSpec(memory_space=pltpu.HBM)
    return pl.pallas_call(
        pack_kernel,
        in_specs=[hbm] * 3,
        out_shape=jax.ShapeDtypeStruct((heads, BLOCK + HALF, LANES), bf16),
        scratch_shapes=[pltpu.VMEM(x.shape, bf16) for x in (q, k, v)]
        + [pltpu.SemaphoreType.DMA((3,))],
        compiler_params=params(),
        name="pack",
    )(*(pltpu.with_memory_space_constraint(x, pltpu.HBM) for x in (q, k, v)))


def pick_kernel(ids, kv, out):
    group = lax.axis_index("coarse")
    for s in range(KGRP):
        out[s] = kv[ids[0, group * KGRP + s] - group * kv.shape[0], :BLOCK]


def pick(ids, kv):
    return pl.pallas_call(
        pick_kernel,
        out_shape=jax.ShapeDtypeStruct((KGRP, BLOCK, LANES), bf16),
        in_specs=[pl.BlockSpec(memory_space=pltpu.SMEM), pl.BlockSpec(memory_space=pltpu.VMEM)],
        compiler_params=params(),
        name="pick",
    )(ids, kv)


def with_ones(kv):
    return jnp.where(lane_ids(kv.shape) < HEAD, jnp.ones_like(kv), kv)


def summed(q, keys, values):
    peak = total = None
    for k, v in zip(keys, values):
        s = nt(q, k)
        top = s.max(axis=1, keepdims=True)
        top = top if peak is None else jnp.maximum(peak, top)
        o = nn(jnp.exp2((s - top) * (SCALE * LOG2E)).astype(bf16), v)
        total = o if peak is None else total * jnp.exp2((peak - top) * (SCALE * LOG2E)) + o
        peak = top
    return total, peak


def heavy_kernel(q, kv0, kv1, kv2, kv3, out):
    rows = q.shape[0] * HALF
    both = q[:, BLOCK:].reshape(rows, LANES)
    zero = jnp.zeros((rows, HEAD), bf16)
    keys = [kv[...] for kv in (kv0, kv1, kv2, kv3)]
    vals = [with_ones(k) for k in keys]
    a, _ = summed(jnp.concatenate([both[:, :HEAD], zero], axis=1), keys, vals)
    b, _ = summed(jnp.concatenate([both[:, HEAD:], zero], axis=1), keys, vals)
    low = lane_ids(a.shape) < HEAD
    top = jnp.where(low, pltpu.roll(a, HEAD, 1), b)
    sums = jnp.where(low, a, pltpu.roll(b, HEAD, 1))
    out[...] = (top / sums).astype(bf16).reshape(out.shape)


def heavy_attend(q_kv, kvs):
    blocks = q_kv.shape[0]
    return pl.pallas_call(
        heavy_kernel,
        out_shape=jax.ShapeDtypeStruct((blocks, HALF, LANES), bf16),
        compiler_params=params(),
        cost_estimate=pl.CostEstimate(flops=10_000_000_000, transcendentals=8_000_000, bytes_accessed=2_000_000),
        name="heavy",
    )(q_kv, *kvs)


def light_kernel(q, k, v, even, odd, out):
    here = lax.axis_index(TOKENS)
    last = lax.axis_size(TOKENS) - 1
    rows, width = q.shape
    low = lane_ids((rows, LANES)) < HEAD
    i = lax.broadcasted_iota(jnp.int32, (2 * rows, BLOCK), 0) % rows
    j = lax.broadcasted_iota(jnp.int32, (2 * rows, BLOCK), 1)
    ahead = (j - i) * (1 - 2 * (here % 2))
    sees_even = ahead < 0
    sees_odd = (ahead > 0) & (here > 0) & (here < last)
    for p in range(width // LANES):
        c = slice(p * LANES, (p + 1) * LANES)
        cv = slice(width + p * LANES, width + (p + 1) * LANES)
        qq = q[:, c]
        zero = jnp.zeros_like(qq)
        two = jnp.concatenate([jnp.where(low, qq, zero), jnp.where(low, zero, qq)], axis=0)
        own = nt(two, k[:, c])
        first = jnp.where(sees_even, nt(two, even[:, c]), f32(-1e30))
        second = jnp.where(sees_odd, nt(two, odd[:, c]), f32(-1e30))
        peak = jnp.maximum(jnp.maximum(own, first), second).max(axis=1, keepdims=True)
        po, pe, pd = (jnp.exp2((s - peak) * (SCALE * LOG2E)) for s in (own, first, second))
        total = (po + pe + pd).sum(axis=1, keepdims=True)
        o = nn(po.astype(bf16), v[:, c]) + nn(pe.astype(bf16), even[:, cv]) + nn(pd.astype(bf16), odd[:, cv])
        o = o / total
        out[:, c] = jnp.where(low, o[:rows], o[rows:])


def light_attend(q, k, v, even, odd):
    return pl.pallas_call(
        light_kernel,
        out_shape=jax.ShapeDtypeStruct(q.shape, f32),
        compiler_params=params(),
        cost_estimate=pl.CostEstimate(flops=3_000_000_000, transcendentals=800_000, bytes_accessed=2_000_000),
        name="light",
    )(q, k, v, even, odd)


def join_kernel(ids, light, heavy, out):
    here = lax.axis_index(TOKENS)
    count = jnp.int32(0)
    for n in range(ids.shape[1]):
        count = count + jnp.where(ids[0, n] == here, 1, 0)
    scale = count.astype(f32)
    for p in range(heavy.shape[0] // 2):
        e, o = heavy[2 * p], heavy[2 * p + 1]
        for n in range(2):
            rows, lanes = slice(n * HALF, (n + 1) * HALF), slice(n * HEAD, (n + 1) * HEAD)
            cols = slice(p * LANES, (p + 1) * LANES)
            both = jnp.concatenate([e[:, lanes], o[:, lanes]], axis=1)
            out[rows, cols] = (light[rows, cols] + both.astype(f32) * scale).astype(bf16)


def join(ids, light, heavy):
    vmem = pl.BlockSpec(memory_space=pltpu.VMEM)
    return pl.pallas_call(
        join_kernel,
        in_specs=[pl.BlockSpec(memory_space=pltpu.SMEM), vmem, vmem],
        out_shape=jax.ShapeDtypeStruct(light.shape, bf16),
        compiler_params=params(),
        name="join",
    )(ids, light, heavy)


def partial(level, ratio):
    lane = lane_ids(ratio.shape)
    hi = level.astype(bf16).astype(f32)
    mid = (level - hi).astype(bf16).astype(f32)
    least = level - hi - mid
    parts = jnp.where(lane < 16, hi, jnp.where(lane < 32, mid, least))
    return jnp.where(lane < HEAD, parts, ratio).astype(bf16)


def decode_kernel(q_hbm, e0, e1, out, q, sem):
    rows, width = q.shape
    at = pl.multiple_of(lax.axis_index("fine") * rows, rows)
    copy = pltpu.make_async_copy(q_hbm.at[pl.ds(at, rows)], q, sem)
    copy.start()
    copy.wait()
    zero = jnp.zeros((rows, HEAD), bf16)
    stack = jnp.concatenate(
        [
            jnp.concatenate([q[:, h * HEAD : (h + 1) * HEAD], zero], axis=1)
            for h in range(width // HEAD)
        ],
        axis=0,
    )
    keys = [e[...] for e in (e0, e1)]
    vals = [with_ones(k) for k in keys]
    total, peak = summed(stack, keys, vals)
    out[...] = partial(peak * SCALE + jnp.log(total), total / pltpu.roll(total, HEAD, 1))


def decode(q, enc, rows):
    width = q.shape[1]
    vmem = pl.BlockSpec(memory_space=pltpu.VMEM)
    return pl.pallas_call(
        decode_kernel,
        in_specs=[pl.BlockSpec(memory_space=pltpu.HBM)] + [vmem] * len(enc),
        out_shape=jax.ShapeDtypeStruct((rows * (width // HEAD), LANES), bf16),
        scratch_shapes=[pltpu.VMEM((rows, width), bf16), pltpu.SemaphoreType.DMA(())],
        compiler_params=params(),
        cost_estimate=pl.CostEstimate(flops=1_000_000_000, transcendentals=1_000_000, bytes_accessed=1_000_000),
        name="decode",
    )(q, *enc)


def meet_kernel(a, b, out, *, last):
    parts = [x[...].astype(f32) for x in (a, b)]
    levels = [x[:, 0:1] + x[:, 16:17] + x[:, 32:33] for x in parts]
    peak = jnp.maximum(*levels)
    scales = [jnp.exp(n - peak) for n in levels]
    total = scales[0] + scales[1]
    value = (parts[0] * scales[0] + parts[1] * scales[1]) / total
    if not last:
        out[...] = partial(jnp.broadcast_to(peak + jnp.log(total), value.shape), value)
        return
    value = value.astype(bf16)
    rows, width = out.shape
    for p in range(width // LANES):
        e = value[2 * p * rows : (2 * p + 1) * rows, HEAD:]
        o = value[(2 * p + 1) * rows : (2 * p + 2) * rows, HEAD:]
        out[:, p * LANES : (p + 1) * LANES] = jnp.concatenate([e, o], axis=1)


def meet(a, b, shape, last):
    return pl.pallas_call(
        lambda *refs: meet_kernel(*refs, last=last),
        out_shape=jax.ShapeDtypeStruct(shape, bf16),
        compiler_params=params(),
        name="meet",
    )(a, b)


def stack_kernel(a, b, *rest):
    out = rest[-1]
    size = a.shape[0]
    out[:size] = a[...]
    out[size:] = b[...]


def stack(a, b, *others):
    return pl.pallas_call(
        stack_kernel,
        in_specs=[pl.BlockSpec(memory_space=pltpu.VMEM)] * 2
        + [pl.BlockSpec(memory_space=pl.ANY)] * len(others),
        out_shape=jax.ShapeDtypeStruct((2 * a.shape[0],) + a.shape[1:], a.dtype),
        compiler_params=params(),
        name="stack",
    )(a, b, *others)


def spread_kernel(own, other, out):
    place = lax.axis_index("fine")
    order = (0, 1, 3, 2)
    for r, dr in enumerate(order):
        got = own if r < 2 else other
        for c, dc in enumerate(order):
            out[place ^ (dr * 4 + dc)] = got[r % 2 * 4 + c]


def spread(own, other):
    side, count, width = own.shape
    return pl.pallas_call(
        spread_kernel,
        out_shape=jax.ShapeDtypeStruct((2 * side, count, width), bf16),
        compiler_params=params(),
        name="spread",
    )(own, other)


def swap(value, axis, d, stride=1, ring=4):
    size = lax.axis_size(axis)
    pairs = [(i, i + ((i // stride % ring ^ d) - i // stride % ring) * stride) for i in range(size)]
    return lax.ppermute(value, axis, pairs)


def after_all(value, *others):
    return lax.optimization_barrier((value, others))[0]


def local(
    q_light, k_light, v_light, q_heavy, k_heavy, v_heavy, enc_kv, dec_queries, query_ids, key_ids
):
    n_seq = lax.axis_size(TOKENS)
    n_fine = lax.axis_size("fine")
    width = q_light.shape[2]

    light_kv = jnp.concatenate([k_light[0], v_light[0]], axis=1)

    def across(value, d):
        return swap(value, "fine", d, 1)

    def down(value, d):
        return swap(value, "fine", d, 4)

    enc = enc_kv[0]
    enc = stack(enc, across(enc, 1), light_kv)
    enc = stack(enc, across(enc, 3))
    enc = stack(enc, down(enc, 1))
    enc = (enc, down(enc, 3))
    chunks = pack(q_heavy[0], k_heavy[0], v_heavy[0])
    group = lax.all_to_all(after_all(chunks, enc[1]), "fine", 0, 0, tiled=True)

    dec_rows = dec_queries.shape[1] // n_fine
    part = decode(dec_queries[0], enc, dec_rows)
    part = meet(part, swap(part, "coarse", 1), part.shape, False)
    share = meet(part, swap(part, "coarse", 3), (dec_rows, width), True)

    own = pick(key_ids, after_all(group, share)).reshape(KGRP * BLOCK, LANES)
    near, far = swap(own, "coarse", 1), swap(own, "coarse", 3)
    routed = [own, near, far, swap(near, "coarse", 3)]
    share = share[None]
    share = stack(share, across(share, 1), near, far)
    share = stack(share, across(share, 3))
    share = stack(share, down(share, 1))
    shares = (share, down(share, 3))

    light_kv = after_all(light_kv, routed)
    even = lax.ppermute(light_kv, TOKENS, [(i, i ^ 1) for i in range(n_seq)])
    odd = lax.ppermute(light_kv, TOKENS, [(i, (i - 1 ^ 1) + 1) for i in range(1, n_seq - 1)])

    heavy = heavy_attend(group, routed)
    shares, q_light = after_all((shares, q_light), heavy)
    heavy = lax.all_to_all(heavy, "fine", 0, 0, tiled=True)
    light = light_attend(q_light[0], k_light[0], v_light[0], even, odd)
    decoded = spread(*shares).reshape(1, -1, width)
    encoded = join(query_ids, light, heavy)[None]
    return (encoded, decoded)


def solution(mesh):
    seq = P("doc", TOKENS, None)
    whole = P("doc", None, None)
    return jax.shard_map(
        local,
        mesh=mesh,
        in_specs=(seq,) * 7 + (whole, P("doc", None), P("doc", None)),
        out_specs=(seq, whole),
        check_vma=False,
    )
```

```python
import jax
import jax.numpy as jnp
from jax import lax
from jax.experimental import pallas as pl
from jax.experimental.pallas import tpu as pltpu
from jax.sharding import PartitionSpec as P

HEAD = 64
LANES = 2 * HEAD
BLOCK = 128
KGRP = 8
HALF = BLOCK // 2
SCALE = HEAD**-0.5
LOG2E = 1.4426950408889634
TOKENS = ("coarse", "fine")
VMEM = 48 * 1024 * 1024

f32 = jnp.float32
bf16 = jnp.bfloat16


def params(**kw):
    return pltpu.CompilerParams(vmem_limit_bytes=VMEM, **kw)


def lane_ids(shape):
    return lax.broadcasted_iota(jnp.int32, shape, len(shape) - 1)


def nt(a, b):
    return lax.dot_general(a, b, (((1,), (1,)), ((), ())), preferred_element_type=f32)


def nn(a, b):
    return jnp.dot(a, b, preferred_element_type=f32)


def pack_kernel(q_hbm, k_hbm, v_hbm, out, q, k, v, sem):
    copies = [
        pltpu.make_async_copy(src, dst, sem.at[n])
        for n, (src, dst) in enumerate(((k_hbm, k), (v_hbm, v), (q_hbm, q)))
    ]
    for c in copies:
        c.start()
    heads = out.shape[0]
    copies[0].wait()
    copies[1].wait()
    for h in range(heads):
        cols = slice(h * HEAD, (h + 1) * HEAD)
        out[h, :BLOCK] = jnp.concatenate([k[:, cols], v[:, cols]], axis=1)
    copies[2].wait()
    for h in range(heads):
        qh = q[:, h * HEAD : (h + 1) * HEAD]
        out[h, BLOCK:] = jnp.concatenate([qh[:HALF], qh[HALF:]], axis=1)


def pack(q, k, v):
    heads = q.shape[1] // HEAD
    hbm = pl.BlockSpec(memory_space=pltpu.HBM)
    return pl.pallas_call(
        pack_kernel,
        in_specs=[hbm] * 3,
        out_shape=jax.ShapeDtypeStruct((heads, BLOCK + HALF, LANES), bf16),
        scratch_shapes=[pltpu.VMEM(x.shape, bf16) for x in (q, k, v)]
        + [pltpu.SemaphoreType.DMA((3,))],
        compiler_params=params(),
        name="pack",
    )(*(pltpu.with_memory_space_constraint(x, pltpu.HBM) for x in (q, k, v)))


def pick_kernel(ids, kv, out):
    group = lax.axis_index("coarse")
    for s in range(KGRP):
        out[s] = kv[ids[0, group * KGRP + s] - group * kv.shape[0], :BLOCK]


def pick(ids, kv):
    return pl.pallas_call(
        pick_kernel,
        out_shape=jax.ShapeDtypeStruct((KGRP, BLOCK, LANES), bf16),
        in_specs=[pl.BlockSpec(memory_space=pltpu.SMEM), pl.BlockSpec(memory_space=pltpu.VMEM)],
        compiler_params=params(),
        name="pick",
    )(ids, kv)


def with_ones(kv):
    return jnp.where(lane_ids(kv.shape) < HEAD, jnp.ones_like(kv), kv)


def summed(q, keys, values):
    peak = total = None
    for k, v in zip(keys, values):
        s = nt(q, k)
        top = s.max(axis=1, keepdims=True)
        top = top if peak is None else jnp.maximum(peak, top)
        o = nn(jnp.exp2((s - top) * (SCALE * LOG2E)).astype(bf16), v)
        total = o if peak is None else total * jnp.exp2((peak - top) * (SCALE * LOG2E)) + o
        peak = top
    return total, peak


def heavy_kernel(q, kv0, kv1, kv2, kv3, out):
    rows = q.shape[0] * HALF
    both = q[:, BLOCK:].reshape(rows, LANES)
    zero = jnp.zeros((rows, HEAD), bf16)
    keys = [kv[...] for kv in (kv0, kv1, kv2, kv3)]
    vals = [with_ones(k) for k in keys]
    a, _ = summed(jnp.concatenate([both[:, :HEAD], zero], axis=1), keys, vals)
    b, _ = summed(jnp.concatenate([both[:, HEAD:], zero], axis=1), keys, vals)
    low = lane_ids(a.shape) < HEAD
    top = jnp.where(low, pltpu.roll(a, HEAD, 1), b)
    sums = jnp.where(low, a, pltpu.roll(b, HEAD, 1))
    out[...] = (top / sums).astype(bf16).reshape(out.shape)


def heavy_attend(q_kv, kvs):
    blocks = q_kv.shape[0]
    return pl.pallas_call(
        heavy_kernel,
        out_shape=jax.ShapeDtypeStruct((blocks, HALF, LANES), bf16),
        compiler_params=params(),
        cost_estimate=pl.CostEstimate(flops=10_000_000_000, transcendentals=8_000_000, bytes_accessed=2_000_000),
        name="heavy",
    )(q_kv, *kvs)


def light_kernel(q, k, v, even, odd, rows_in, out, rows_out, sem):
    copy = pltpu.make_async_copy(rows_in, rows_out, sem)
    copy.start()
    here = lax.axis_index(TOKENS)
    last = lax.axis_size(TOKENS) - 1
    rows, width = q.shape
    low = lane_ids((rows, LANES)) < HEAD
    i = lax.broadcasted_iota(jnp.int32, (2 * rows, BLOCK), 0) % rows
    j = lax.broadcasted_iota(jnp.int32, (2 * rows, BLOCK), 1)
    ahead = (j - i) * (1 - 2 * (here % 2))
    sees_even = ahead < 0
    sees_odd = (ahead > 0) & (here > 0) & (here < last)
    for p in range(width // LANES):
        c = slice(p * LANES, (p + 1) * LANES)
        cv = slice(width + p * LANES, width + (p + 1) * LANES)
        qq = q[:, c]
        zero = jnp.zeros_like(qq)
        two = jnp.concatenate([jnp.where(low, qq, zero), jnp.where(low, zero, qq)], axis=0)
        own = nt(two, k[:, c])
        first = jnp.where(sees_even, nt(two, even[:, c]), f32(-1e30))
        second = jnp.where(sees_odd, nt(two, odd[:, c]), f32(-1e30))
        peak = jnp.maximum(jnp.maximum(own, first), second).max(axis=1, keepdims=True)
        po, pe, pd = (jnp.exp2((s - peak) * (SCALE * LOG2E)) for s in (own, first, second))
        total = (po + pe + pd).sum(axis=1, keepdims=True)
        o = nn(po.astype(bf16), v[:, c]) + nn(pe.astype(bf16), even[:, cv]) + nn(pd.astype(bf16), odd[:, cv])
        o = o / total
        out[:, c] = jnp.where(low, o[:rows], o[rows:])
    copy.wait()


def light_attend(q, k, v, even, odd, decoded):
    vmem = pl.BlockSpec(memory_space=pltpu.VMEM)
    hbm = pl.BlockSpec(memory_space=pl.ANY)
    return pl.pallas_call(
        light_kernel,
        in_specs=[vmem] * 5 + [hbm],
        out_specs=(vmem, hbm),
        out_shape=(jax.ShapeDtypeStruct(q.shape, f32), jax.ShapeDtypeStruct(decoded.shape, bf16)),
        scratch_shapes=[pltpu.SemaphoreType.DMA(())],
        compiler_params=params(),
        cost_estimate=pl.CostEstimate(flops=3_000_000_000, transcendentals=800_000, bytes_accessed=2_000_000),
        name="light",
    )(q, k, v, even, odd, decoded)


def join_kernel(ids, light, heavy, out):
    here = lax.axis_index(TOKENS)
    count = jnp.int32(0)
    for n in range(ids.shape[1]):
        count = count + jnp.where(ids[0, n] == here, 1, 0)
    scale = count.astype(f32)
    for p in range(heavy.shape[0] // 2):
        e, o = heavy[2 * p], heavy[2 * p + 1]
        for n in range(2):
            rows, lanes = slice(n * HALF, (n + 1) * HALF), slice(n * HEAD, (n + 1) * HEAD)
            cols = slice(p * LANES, (p + 1) * LANES)
            both = jnp.concatenate([e[:, lanes], o[:, lanes]], axis=1)
            out[rows, cols] = (light[rows, cols] + both.astype(f32) * scale).astype(bf16)


def join(ids, light, heavy):
    vmem = pl.BlockSpec(memory_space=pltpu.VMEM)
    return pl.pallas_call(
        join_kernel,
        in_specs=[pl.BlockSpec(memory_space=pltpu.SMEM), vmem, vmem],
        out_shape=jax.ShapeDtypeStruct(light.shape, bf16),
        compiler_params=params(),
        name="join",
    )(ids, light, heavy)


def decode_kernel(q_hbm, e0, e1, e2, e3, out, q, sem):
    rows, width = q.shape
    at = pl.multiple_of(lax.axis_index("fine") * rows, rows)
    copy = pltpu.make_async_copy(q_hbm.at[pl.ds(at, rows)], q, sem)
    copy.start()
    copy.wait()
    zero = jnp.zeros((rows, HEAD), bf16)
    stack = jnp.concatenate(
        [
            jnp.concatenate([q[:, h * HEAD : (h + 1) * HEAD], zero], axis=1)
            for h in range(width // HEAD)
        ],
        axis=0,
    )
    keys = [e[...] for e in (e0, e1, e2, e3)]
    vals = [with_ones(k) for k in keys]
    total, peak = summed(stack, keys, vals)
    lane = lane_ids(total.shape)
    level = peak * SCALE + jnp.log(total)
    hi = level.astype(bf16).astype(f32)
    mid = (level - hi).astype(bf16).astype(f32)
    least = level - hi - mid
    parts = jnp.where(lane < 16, hi, jnp.where(lane < 32, mid, least))
    ratio = total / pltpu.roll(total, HEAD, 1)
    out[...] = jnp.where(lane < HEAD, parts, ratio).astype(bf16)


def decode(q, enc, rows):
    width = q.shape[1]
    vmem = pl.BlockSpec(memory_space=pltpu.VMEM)
    return pl.pallas_call(
        decode_kernel,
        in_specs=[pl.BlockSpec(memory_space=pltpu.HBM)] + [vmem] * len(enc),
        out_shape=jax.ShapeDtypeStruct((rows * (width // HEAD), LANES), bf16),
        scratch_shapes=[pltpu.VMEM((rows, width), bf16), pltpu.SemaphoreType.DMA(())],
        compiler_params=params(),
        cost_estimate=pl.CostEstimate(flops=30_000_000_000, transcendentals=1_000_000, bytes_accessed=1_000_000),
        name="decode",
    )(q, *enc)


def meet_kernel(a, b, c, d, out):
    parts = [x[...].astype(f32) for x in (a, b, c, d)]
    levels = [x[:, 0:1] + x[:, 16:17] + x[:, 32:33] for x in parts]
    peak = jnp.maximum(jnp.maximum(levels[0], levels[1]), jnp.maximum(levels[2], levels[3]))
    scales = [jnp.exp(n - peak) for n in levels]
    total = scales[0] + scales[1] + scales[2] + scales[3]
    value = parts[0] * scales[0]
    for x, s in zip(parts[1:], scales[1:]):
        value = value + x * s
    value = (value / total).astype(bf16)
    copies, rows, width = out.shape
    for p in range(width // LANES):
        e = value[2 * p * rows : (2 * p + 1) * rows, HEAD:]
        o = value[(2 * p + 1) * rows : (2 * p + 2) * rows, HEAD:]
        both = jnp.concatenate([e, o], axis=1)
        for n in range(copies):
            out[n, :, p * LANES : (p + 1) * LANES] = both


def meet(parts, copies, rows, width):
    return pl.pallas_call(
        meet_kernel,
        out_shape=jax.ShapeDtypeStruct((copies, rows, width), bf16),
        compiler_params=params(),
        name="meet",
    )(*parts)


def stack_kernel(*refs):
    parts, out = refs[:4], refs[-1]
    size = parts[0].shape[0]
    for n, part in enumerate(parts):
        out[n * size : (n + 1) * size] = part[...]


def stack(parts, *others):
    first = parts[0]
    specs = [pl.BlockSpec(memory_space=pltpu.VMEM)] * len(parts)
    return pl.pallas_call(
        stack_kernel,
        in_specs=specs + [pl.BlockSpec(memory_space=pl.ANY)] * len(others),
        out_shape=jax.ShapeDtypeStruct((len(parts) * first.shape[0],) + first.shape[1:], first.dtype),
        compiler_params=params(),
        name="stack",
    )(*parts, *others)


def around(value, axis, stride=1, ring=None):
    size = lax.axis_size(axis)
    ring = ring or size

    def pairs(d):
        return [(i, i + ((i // stride % ring ^ d) - i // stride % ring) * stride) for i in range(size)]

    return [lax.ppermute(value, axis, pairs(d)) for d in range(1, ring)]


def after_all(value, *others):
    return lax.optimization_barrier((value, others))[0]


def local(
    q_light, k_light, v_light, q_heavy, k_heavy, v_heavy, enc_kv, dec_queries, query_ids, key_ids
):
    n_seq = lax.axis_size(TOKENS)
    n_fine = lax.axis_size("fine")
    side = 4
    width = q_light.shape[2]

    light_kv = jnp.concatenate([k_light[0], v_light[0]], axis=1)

    def rows_of(value):
        return [value] + around(value, "fine", 1, side)

    def square(row):
        return [row] + around(row, "fine", side, n_fine // side)

    enc = square(stack(rows_of(enc_kv[0]), light_kv))
    chunks = pack(q_heavy[0], k_heavy[0], v_heavy[0])
    group = lax.all_to_all(after_all(chunks, enc[0]), "fine", 0, 0, tiled=True)

    dec_rows = dec_queries.shape[1] // n_fine
    part = decode(dec_queries[0], enc, dec_rows)
    share = meet([part] + around(part, "coarse"), n_fine, dec_rows, width)

    own = pick(key_ids, after_all(group, share)).reshape(KGRP * BLOCK, LANES)
    routed = [own] + around(own, "coarse")
    decoded = lax.all_to_all(after_all(share, own), "fine", 0, 0, tiled=True)

    light_kv = after_all(light_kv, routed)
    even = lax.ppermute(light_kv, TOKENS, [(i, i ^ 1) for i in range(n_seq)])
    odd = lax.ppermute(light_kv, TOKENS, [(i, (i - 1 ^ 1) + 1) for i in range(1, n_seq - 1)])

    heavy = heavy_attend(group, routed)
    q_light = after_all(q_light, heavy)
    heavy, decoded = lax.optimization_barrier((heavy, decoded))
    heavy = lax.all_to_all(heavy, "fine", 0, 0, tiled=True)
    light, decoded = light_attend(
        q_light[0], k_light[0], v_light[0], even, odd, decoded.reshape(-1, width)
    )
    encoded = join(query_ids, light, heavy)[None]
    return (encoded, decoded[None])


def solution(mesh):
    seq = P("doc", TOKENS, None)
    whole = P("doc", None, None)
    return jax.shard_map(
        local,
        mesh=mesh,
        in_specs=(seq,) * 7 + (whole, P("doc", None), P("doc", None)),
        out_specs=(seq, whole),
        check_vma=False,
    )
```

```python
import jax
import jax.numpy as jnp
from jax import lax
from jax.experimental import pallas as pl
from jax.experimental.pallas import tpu as pltpu
from jax.sharding import PartitionSpec as P

HEAD = 64
LANES = 2 * HEAD
BLOCK = 128
KGRP = 8
HALF = BLOCK // 2
SCALE = HEAD**-0.5
LOG2E = 1.4426950408889634
TOKENS = ("coarse", "fine")
MIB = 1024 * 1024

f32 = jnp.float32
bf16 = jnp.bfloat16


def params(mib):
    return pltpu.CompilerParams(vmem_limit_bytes=mib * MIB)


def lane_ids(shape):
    return lax.broadcasted_iota(jnp.int32, shape, len(shape) - 1)


def nt(a, b):
    return lax.dot_general(a, b, (((1,), (1,)), ((), ())), preferred_element_type=f32)


def nn(a, b):
    return jnp.dot(a, b, preferred_element_type=f32)


def pack_kernel(q_hbm, k_hbm, v_hbm, out, q, k, v, sem):
    copies = [
        pltpu.make_async_copy(src, dst, sem.at[n])
        for n, (src, dst) in enumerate(((k_hbm, k), (v_hbm, v), (q_hbm, q)))
    ]
    for c in copies:
        c.start()
    heads = out.shape[0]
    copies[0].wait()
    copies[1].wait()
    for h in range(heads):
        cols = slice(h * HEAD, (h + 1) * HEAD)
        out[h, :BLOCK] = jnp.concatenate([k[:, cols], v[:, cols]], axis=1)
    copies[2].wait()
    for h in range(heads):
        qh = q[:, h * HEAD : (h + 1) * HEAD]
        out[h, BLOCK:] = jnp.concatenate([qh[:HALF], qh[HALF:]], axis=1)


def pack(q, k, v):
    heads = q.shape[1] // HEAD
    hbm = pl.BlockSpec(memory_space=pltpu.HBM)
    return pl.pallas_call(
        pack_kernel,
        in_specs=[hbm] * 3,
        out_shape=jax.ShapeDtypeStruct((heads, BLOCK + HALF, LANES), bf16),
        scratch_shapes=[pltpu.VMEM(x.shape, bf16) for x in (q, k, v)]
        + [pltpu.SemaphoreType.DMA((3,))],
        compiler_params=params(8),
        name="pack",
    )(*(pltpu.with_memory_space_constraint(x, pltpu.HBM) for x in (q, k, v)))


def pick_kernel(ids, kv, out):
    group = lax.axis_index("coarse")
    for s in range(KGRP):
        out[s] = kv[ids[0, group * KGRP + s] - group * kv.shape[0], :BLOCK]


def pick(ids, kv):
    return pl.pallas_call(
        pick_kernel,
        out_shape=jax.ShapeDtypeStruct((KGRP, BLOCK, LANES), bf16),
        in_specs=[pl.BlockSpec(memory_space=pltpu.SMEM), pl.BlockSpec(memory_space=pltpu.VMEM)],
        compiler_params=params(4),
        name="pick",
    )(ids, kv)


def with_ones(kv):
    return jnp.where(lane_ids(kv.shape) < HEAD, jnp.ones_like(kv), kv)


def summed(q, keys):
    peak = total = None
    for k in keys:
        s = nt(q, k)
        top = s.max(axis=1, keepdims=True)
        top = top if peak is None else jnp.maximum(peak, top)
        o = nn(jnp.exp2((s - top) * (SCALE * LOG2E)).astype(bf16), with_ones(k))
        total = o if peak is None else total * jnp.exp2((peak - top) * (SCALE * LOG2E)) + o
        peak = top
    return total, peak


def heavy_kernel(q, kv0, kv1, kv2, kv3, out, others, sem):
    copies = [pltpu.make_async_copy(kv, others.at[n], sem.at[n]) for n, kv in enumerate((kv1, kv2, kv3))]
    for copy in copies:
        copy.start()

    def arriving():
        yield kv0[...]
        for n, copy in enumerate(copies):
            copy.wait()
            yield others[n]

    rows = q.shape[0] * HALF
    both = q[:, BLOCK:].reshape(rows, LANES)
    zero = jnp.zeros((rows, HEAD), bf16)
    a, _ = summed(jnp.concatenate([both[:, :HEAD], zero], axis=1), arriving())
    keys = [kv0[...]] + [others[n] for n in range(len(copies))]
    b, _ = summed(jnp.concatenate([both[:, HEAD:], zero], axis=1), keys)
    low = lane_ids(a.shape) < HEAD
    top = jnp.where(low, pltpu.roll(a, HEAD, 1), b)
    sums = jnp.where(low, a, pltpu.roll(b, HEAD, 1))
    out[...] = (top / sums).astype(bf16).reshape(out.shape)


def heavy_attend(q_kv, kvs):
    blocks = q_kv.shape[0]
    vmem = pl.BlockSpec(memory_space=pltpu.VMEM)
    hbm = pl.BlockSpec(memory_space=pl.ANY)
    others = kvs[1:]
    return pl.pallas_call(
        heavy_kernel,
        in_specs=[vmem] * 2 + [hbm] * len(others),
        out_shape=jax.ShapeDtypeStruct((blocks, HALF, LANES), bf16),
        scratch_shapes=[
            pltpu.VMEM((len(others),) + kvs[0].shape, bf16),
            pltpu.SemaphoreType.DMA((len(others),)),
        ],
        compiler_params=params(28),
        cost_estimate=pl.CostEstimate(flops=10_000_000_000, transcendentals=8_000_000, bytes_accessed=2_000_000),
        name="heavy",
    )(q_kv, kvs[0], *others)


def light_kernel(q, k, v, even, odd, rows_in, out, rows_out, sem):
    count = rows_in.shape[0] // 4
    copies = [
        pltpu.make_async_copy(rows_in.at[pl.ds(n * count, count)], rows_out.at[pl.ds(n * count, count)], sem.at[n])
        for n in range(4)
    ]
    for copy in copies:
        copy.start()
    here = lax.axis_index(TOKENS)
    last = lax.axis_size(TOKENS) - 1
    rows, width = q.shape
    low = lane_ids((rows, LANES)) < HEAD
    i = lax.broadcasted_iota(jnp.int32, (2 * rows, BLOCK), 0) % rows
    j = lax.broadcasted_iota(jnp.int32, (2 * rows, BLOCK), 1)
    ahead = (j - i) * (1 - 2 * (here % 2))
    sees_even = ahead < 0
    sees_odd = (ahead > 0) & (here > 0) & (here < last)
    for p in range(width // LANES):
        c = slice(p * LANES, (p + 1) * LANES)
        cv = slice(width + p * LANES, width + (p + 1) * LANES)
        qq = q[:, c]
        zero = jnp.zeros_like(qq)
        two = jnp.concatenate([jnp.where(low, qq, zero), jnp.where(low, zero, qq)], axis=0)
        own = nt(two, k[:, c])
        first = jnp.where(sees_even, nt(two, even[:, c]), f32(-1e30))
        second = jnp.where(sees_odd, nt(two, odd[:, c]), f32(-1e30))
        peak = jnp.maximum(jnp.maximum(own, first), second).max(axis=1, keepdims=True)
        po, pe, pd = (jnp.exp2((s - peak) * (SCALE * LOG2E)) for s in (own, first, second))
        total = (po + pe + pd).sum(axis=1, keepdims=True)
        o = nn(po.astype(bf16), v[:, c]) + nn(pe.astype(bf16), even[:, cv]) + nn(pd.astype(bf16), odd[:, cv])
        o = o / total
        out[:, c] = jnp.where(low, o[:rows], o[rows:])
    for copy in copies:
        copy.wait()


def light_attend(q, k, v, even, odd, decoded):
    vmem = pl.BlockSpec(memory_space=pltpu.VMEM)
    hbm = pl.BlockSpec(memory_space=pl.ANY)
    return pl.pallas_call(
        light_kernel,
        in_specs=[vmem] * 5 + [hbm],
        out_specs=(vmem, hbm),
        out_shape=(jax.ShapeDtypeStruct(q.shape, f32), jax.ShapeDtypeStruct(decoded.shape, bf16)),
        scratch_shapes=[pltpu.SemaphoreType.DMA((4,))],
        compiler_params=params(12),
        cost_estimate=pl.CostEstimate(flops=3_000_000_000, transcendentals=800_000, bytes_accessed=2_000_000),
        name="light",
    )(q, k, v, even, odd, decoded)


def join_kernel(ids, light, heavy, out):
    here = lax.axis_index(TOKENS)
    count = jnp.int32(0)
    for n in range(ids.shape[1]):
        count = count + jnp.where(ids[0, n] == here, 1, 0)
    scale = count.astype(f32)
    for p in range(heavy.shape[0] // 2):
        e, o = heavy[2 * p], heavy[2 * p + 1]
        for n in range(2):
            rows, lanes = slice(n * HALF, (n + 1) * HALF), slice(n * HEAD, (n + 1) * HEAD)
            cols = slice(p * LANES, (p + 1) * LANES)
            both = jnp.concatenate([e[:, lanes], o[:, lanes]], axis=1)
            out[rows, cols] = (light[rows, cols] + both.astype(f32) * scale).astype(bf16)


def join(ids, light, heavy):
    vmem = pl.BlockSpec(memory_space=pltpu.VMEM)
    return pl.pallas_call(
        join_kernel,
        in_specs=[pl.BlockSpec(memory_space=pltpu.SMEM), vmem, vmem],
        out_shape=jax.ShapeDtypeStruct(light.shape, bf16),
        compiler_params=params(6),
        name="join",
    )(ids, light, heavy)


def decode_kernel(q_hbm, e0, e1, e2, e3, out, q, sem):
    rows, width = q.shape
    at = pl.multiple_of(lax.axis_index("fine") * rows, rows)
    copy = pltpu.make_async_copy(q_hbm.at[pl.ds(at, rows)], q, sem)
    copy.start()
    copy.wait()
    zero = jnp.zeros((rows, HEAD), bf16)
    stack = jnp.concatenate(
        [
            jnp.concatenate([q[:, h * HEAD : (h + 1) * HEAD], zero], axis=1)
            for h in range(width // HEAD)
        ],
        axis=0,
    )
    keys = [e[...] for e in (e0, e1, e2, e3)]
    total, peak = summed(stack, keys)
    lane = lane_ids(total.shape)
    level = peak * SCALE + jnp.log(total)
    hi = level.astype(bf16).astype(f32)
    mid = (level - hi).astype(bf16).astype(f32)
    least = level - hi - mid
    parts = jnp.where(lane < 16, hi, jnp.where(lane < 32, mid, least))
    ratio = total / pltpu.roll(total, HEAD, 1)
    out[...] = jnp.where(lane < HEAD, parts, ratio).astype(bf16)


def decode(q, enc, rows):
    width = q.shape[1]
    vmem = pl.BlockSpec(memory_space=pltpu.VMEM)
    return pl.pallas_call(
        decode_kernel,
        in_specs=[pl.BlockSpec(memory_space=pltpu.HBM)] + [vmem] * len(enc),
        out_shape=jax.ShapeDtypeStruct((rows * (width // HEAD), LANES), bf16),
        scratch_shapes=[pltpu.VMEM((rows, width), bf16), pltpu.SemaphoreType.DMA(())],
        compiler_params=params(16),
        cost_estimate=pl.CostEstimate(flops=30_000_000_000, transcendentals=1_000_000, bytes_accessed=1_000_000),
        name="decode",
    )(q, *enc)


def meet_kernel(a, b, c, d, out):
    parts = [x[...].astype(f32) for x in (a, b, c, d)]
    levels = [x[:, 0:1] + x[:, 16:17] + x[:, 32:33] for x in parts]
    peak = jnp.maximum(jnp.maximum(levels[0], levels[1]), jnp.maximum(levels[2], levels[3]))
    scales = [jnp.exp(n - peak) for n in levels]
    total = scales[0] + scales[1] + scales[2] + scales[3]
    value = parts[0] * scales[0]
    for x, s in zip(parts[1:], scales[1:]):
        value = value + x * s
    value = (value / total).astype(bf16)
    copies, rows, width = out.shape
    for p in range(width // LANES):
        e = value[2 * p * rows : (2 * p + 1) * rows, HEAD:]
        o = value[(2 * p + 1) * rows : (2 * p + 2) * rows, HEAD:]
        both = jnp.concatenate([e, o], axis=1)
        for n in range(copies):
            out[n, :, p * LANES : (p + 1) * LANES] = both


def meet(parts, copies, rows, width):
    return pl.pallas_call(
        meet_kernel,
        out_shape=jax.ShapeDtypeStruct((copies, rows, width), bf16),
        compiler_params=params(8),
        cost_estimate=pl.CostEstimate(flops=30_000_000_000, transcendentals=0, bytes_accessed=2_000_000),
        name="meet",
    )(*parts)


def stack_kernel(*refs):
    parts, out = refs[:4], refs[-1]
    size = parts[0].shape[0]
    for n, part in enumerate(parts):
        out[n * size : (n + 1) * size] = part[...]


def stack(parts, *others):
    first = parts[0]
    specs = [pl.BlockSpec(memory_space=pltpu.VMEM)] * len(parts)
    return pl.pallas_call(
        stack_kernel,
        in_specs=specs + [pl.BlockSpec(memory_space=pl.ANY)] * len(others),
        out_shape=jax.ShapeDtypeStruct((len(parts) * first.shape[0],) + first.shape[1:], first.dtype),
        compiler_params=params(4),
        name="stack",
    )(*parts, *others)


def around(value, axis, stride=1, ring=None):
    size = lax.axis_size(axis)
    ring = ring or size

    def pairs(d):
        return [(i, i + ((i // stride % ring ^ d) - i // stride % ring) * stride) for i in range(size)]

    return [lax.ppermute(value, axis, pairs(d)) for d in range(1, ring)]


def after_all(value, *others):
    return lax.optimization_barrier((value, others))[0]


def local(
    q_light, k_light, v_light, q_heavy, k_heavy, v_heavy, enc_kv, dec_queries, query_ids, key_ids
):
    n_seq = lax.axis_size(TOKENS)
    n_fine = lax.axis_size("fine")
    side = 4
    width = q_light.shape[2]

    light_kv = jnp.concatenate([k_light[0], v_light[0]], axis=1)

    def rows_of(value):
        return [value] + around(value, "fine", 1, side)

    def square(row):
        return [row] + around(row, "fine", side, n_fine // side)

    chunks = pack(q_heavy[0], k_heavy[0], v_heavy[0])
    enc = square(stack(rows_of(enc_kv[0]), chunks))
    group = lax.all_to_all(after_all(chunks, enc[0]), "fine", 0, 0, tiled=True)

    dec_rows = dec_queries.shape[1] // n_fine
    part = decode(dec_queries[0], enc, dec_rows)

    parts = around(part, "coarse")
    own = pick(key_ids, after_all(group, part, light_kv)).reshape(KGRP * BLOCK, LANES)
    routed = [own] + around(own, "coarse")
    share = meet([after_all(part, own)] + parts, n_fine, dec_rows, width)
    decoded = lax.all_to_all(share, "fine", 0, 0, tiled=True)

    light_kv = after_all(light_kv, share)
    even = lax.ppermute(light_kv, TOKENS, [(i, i ^ 1) for i in range(n_seq)])
    odd = lax.ppermute(light_kv, TOKENS, [(i, (i - 1 ^ 1) + 1) for i in range(1, n_seq - 1)])

    heavy = heavy_attend(group, routed)
    heavy, decoded = lax.optimization_barrier((heavy, decoded))
    heavy = lax.all_to_all(heavy, "fine", 0, 0, tiled=True)
    light, decoded = light_attend(
        q_light[0], k_light[0], v_light[0], even, odd, decoded.reshape(-1, width)
    )
    encoded = join(query_ids, light, heavy)[None]
    return (encoded, decoded[None])


def solution(mesh):
    seq = P("doc", TOKENS, None)
    whole = P("doc", None, None)
    return jax.shard_map(
        local,
        mesh=mesh,
        in_specs=(seq,) * 7 + (whole, P("doc", None), P("doc", None)),
        out_specs=(seq, whole),
        check_vma=False,
    )
```

```python
import jax
import jax.numpy as jnp
from jax import lax
from jax.experimental import pallas as pl
from jax.experimental.pallas import tpu as pltpu
from jax.sharding import PartitionSpec as P

HEAD = 64
LANES = 2 * HEAD
BLOCK = 128
KGRP = 8
HALF = BLOCK // 2
SCALE = HEAD**-0.5
LOG2E = 1.4426950408889634
TOKENS = ("coarse", "fine")
MIB = 1024 * 1024

f32 = jnp.float32
bf16 = jnp.bfloat16


def params(mib):
    return pltpu.CompilerParams(vmem_limit_bytes=mib * MIB)


def lane_ids(shape):
    return lax.broadcasted_iota(jnp.int32, shape, len(shape) - 1)


def nt(a, b):
    return lax.dot_general(a, b, (((1,), (1,)), ((), ())), preferred_element_type=f32)


def nn(a, b):
    return jnp.dot(a, b, preferred_element_type=f32)


def pack_kernel(q_hbm, k_hbm, v_hbm, out, q, k, v, sem):
    copies = [
        pltpu.make_async_copy(src, dst, sem.at[n])
        for n, (src, dst) in enumerate(((k_hbm, k), (v_hbm, v), (q_hbm, q)))
    ]
    for c in copies:
        c.start()
    heads = out.shape[0]
    copies[0].wait()
    copies[1].wait()
    for h in range(heads):
        cols = slice(h * HEAD, (h + 1) * HEAD)
        out[h, :BLOCK] = jnp.concatenate([k[:, cols], v[:, cols]], axis=1)
    copies[2].wait()
    for h in range(heads):
        qh = q[:, h * HEAD : (h + 1) * HEAD]
        out[h, BLOCK:] = jnp.concatenate([qh[:HALF], qh[HALF:]], axis=1)


def pack(q, k, v):
    heads = q.shape[1] // HEAD
    hbm = pl.BlockSpec(memory_space=pltpu.HBM)
    return pl.pallas_call(
        pack_kernel,
        in_specs=[hbm] * 3,
        out_shape=jax.ShapeDtypeStruct((heads, BLOCK + HALF, LANES), bf16),
        scratch_shapes=[pltpu.VMEM(x.shape, bf16) for x in (q, k, v)]
        + [pltpu.SemaphoreType.DMA((3,))],
        compiler_params=params(8),
        name="pack",
    )(*(pltpu.with_memory_space_constraint(x, pltpu.HBM) for x in (q, k, v)))


def pick_kernel(ids, kv, out):
    group = lax.axis_index("coarse")
    for s in range(KGRP):
        out[s] = kv[ids[0, group * KGRP + s] - group * kv.shape[0], :BLOCK]


def pick(ids, kv):
    return pl.pallas_call(
        pick_kernel,
        out_shape=jax.ShapeDtypeStruct((KGRP, BLOCK, LANES), bf16),
        in_specs=[pl.BlockSpec(memory_space=pltpu.SMEM), pl.BlockSpec(memory_space=pltpu.VMEM)],
        compiler_params=params(4),
        name="pick",
    )(ids, kv)


def with_ones(kv):
    return jnp.where(lane_ids(kv.shape) < HEAD, jnp.ones_like(kv), kv)


def summed(q, keys):
    peak = total = None
    for k in keys:
        s = nt(q, k)
        top = s.max(axis=1, keepdims=True)
        top = top if peak is None else jnp.maximum(peak, top)
        o = nn(jnp.exp2((s - top) * (SCALE * LOG2E)).astype(bf16), with_ones(k))
        total = o if peak is None else total * jnp.exp2((peak - top) * (SCALE * LOG2E)) + o
        peak = top
    return total, peak


def heavy_kernel(q, kv0, kv1, kv2, kv3, out):
    rows = q.shape[0] * HALF
    both = q[:, BLOCK:].reshape(rows, LANES)
    zero = jnp.zeros((rows, HEAD), bf16)
    keys = [kv[...] for kv in (kv0, kv1, kv2, kv3)]
    a, _ = summed(jnp.concatenate([both[:, :HEAD], zero], axis=1), keys)
    b, _ = summed(jnp.concatenate([both[:, HEAD:], zero], axis=1), keys)
    low = lane_ids(a.shape) < HEAD
    top = jnp.where(low, pltpu.roll(a, HEAD, 1), b)
    sums = jnp.where(low, a, pltpu.roll(b, HEAD, 1))
    out[...] = (top / sums).astype(bf16).reshape(out.shape)


def heavy_attend(q_kv, kvs):
    return pl.pallas_call(
        heavy_kernel,
        out_shape=jax.ShapeDtypeStruct((q_kv.shape[0], HALF, LANES), bf16),
        compiler_params=params(28),
        cost_estimate=pl.CostEstimate(flops=10_000_000_000, transcendentals=8_000_000, bytes_accessed=2_000_000),
        name="heavy",
    )(q_kv, *kvs)


def light_kernel(q, k, v, even, odd, rows_in, out, rows_out, sem):
    count = rows_in.shape[0] // 4
    copies = [
        pltpu.make_async_copy(rows_in.at[pl.ds(n * count, count)], rows_out.at[pl.ds(n * count, count)], sem.at[n])
        for n in range(4)
    ]
    for copy in copies:
        copy.start()
    here = lax.axis_index(TOKENS)
    last = lax.axis_size(TOKENS) - 1
    rows, width = q.shape
    low = lane_ids((rows, LANES)) < HEAD
    i = lax.broadcasted_iota(jnp.int32, (2 * rows, BLOCK), 0) % rows
    j = lax.broadcasted_iota(jnp.int32, (2 * rows, BLOCK), 1)
    ahead = (j - i) * (1 - 2 * (here % 2))
    sees_even = ahead < 0
    sees_odd = (ahead > 0) & (here > 0) & (here < last)
    for p in range(width // LANES):
        c = slice(p * LANES, (p + 1) * LANES)
        cv = slice(width + p * LANES, width + (p + 1) * LANES)
        qq = q[:, c]
        zero = jnp.zeros_like(qq)
        two = jnp.concatenate([jnp.where(low, qq, zero), jnp.where(low, zero, qq)], axis=0)
        own = nt(two, k[:, c])
        first = jnp.where(sees_even, nt(two, even[:, c]), f32(-1e30))
        second = jnp.where(sees_odd, nt(two, odd[:, c]), f32(-1e30))
        peak = jnp.maximum(jnp.maximum(own, first), second).max(axis=1, keepdims=True)
        po, pe, pd = (jnp.exp2((s - peak) * (SCALE * LOG2E)) for s in (own, first, second))
        total = (po + pe + pd).sum(axis=1, keepdims=True)
        o = nn(po.astype(bf16), v[:, c]) + nn(pe.astype(bf16), even[:, cv]) + nn(pd.astype(bf16), odd[:, cv])
        o = o / total
        out[:, c] = jnp.where(low, o[:rows], o[rows:])
    for copy in copies:
        copy.wait()


def light_attend(q, k, v, even, odd, decoded):
    vmem = pl.BlockSpec(memory_space=pltpu.VMEM)
    hbm = pl.BlockSpec(memory_space=pl.ANY)
    return pl.pallas_call(
        light_kernel,
        in_specs=[vmem] * 5 + [hbm],
        out_specs=(vmem, hbm),
        out_shape=(jax.ShapeDtypeStruct(q.shape, f32), jax.ShapeDtypeStruct(decoded.shape, bf16)),
        scratch_shapes=[pltpu.SemaphoreType.DMA((4,))],
        compiler_params=params(12),
        cost_estimate=pl.CostEstimate(flops=3_000_000_000, transcendentals=800_000, bytes_accessed=2_000_000),
        name="light",
    )(q, k, v, even, odd, decoded)


def join_kernel(ids, light, heavy, out, both, sem):
    here = lax.axis_index(TOKENS)
    count = jnp.int32(0)
    for n in range(ids.shape[1]):
        count = count + jnp.where(ids[0, n] == here, 1, 0)
    scale = count.astype(f32)
    pairs = heavy.shape[0] // 2
    step = pairs // 4
    copies = []
    for p in range(pairs):
        e, o = heavy[2 * p], heavy[2 * p + 1]
        cols = slice(p * LANES, (p + 1) * LANES)
        for n in range(2):
            rows, lanes = slice(n * HALF, (n + 1) * HALF), slice(n * HEAD, (n + 1) * HEAD)
            added = jnp.concatenate([e[:, lanes], o[:, lanes]], axis=1)
            both[rows, cols] = (light[rows, cols] + added.astype(f32) * scale).astype(bf16)
        if p % step == step - 1:
            part = pl.ds((p + 1 - step) * LANES, step * LANES)
            copies.append(pltpu.make_async_copy(both.at[:, part], out.at[:, part], sem.at[p // step]))
            copies[-1].start()
    for copy in copies:
        copy.wait()


def join(ids, light, heavy):
    vmem = pl.BlockSpec(memory_space=pltpu.VMEM)
    return pl.pallas_call(
        join_kernel,
        in_specs=[pl.BlockSpec(memory_space=pltpu.SMEM), vmem, vmem],
        out_specs=pl.BlockSpec(memory_space=pl.ANY),
        out_shape=jax.ShapeDtypeStruct(light.shape, bf16),
        scratch_shapes=[pltpu.VMEM(light.shape, bf16), pltpu.SemaphoreType.DMA((4,))],
        compiler_params=params(6),
        name="join",
    )(ids, light, heavy)


def decode_kernel(q_hbm, e0, e1, e2, e3, out, q, sem):
    rows, width = q.shape
    at = pl.multiple_of(lax.axis_index("fine") * rows, rows)
    copy = pltpu.make_async_copy(q_hbm.at[pl.ds(at, rows)], q, sem)
    copy.start()
    copy.wait()
    zero = jnp.zeros((rows, HEAD), bf16)
    stack = jnp.concatenate(
        [
            jnp.concatenate([q[:, h * HEAD : (h + 1) * HEAD], zero], axis=1)
            for h in range(width // HEAD)
        ],
        axis=0,
    )
    keys = [e[...] for e in (e0, e1, e2, e3)]
    total, peak = summed(stack, keys)
    lane = lane_ids(total.shape)
    level = peak * SCALE + jnp.log(total)
    hi = level.astype(bf16).astype(f32)
    mid = (level - hi).astype(bf16).astype(f32)
    least = level - hi - mid
    parts = jnp.where(lane < 16, hi, jnp.where(lane < 32, mid, least))
    ratio = total / pltpu.roll(total, HEAD, 1)
    out[...] = jnp.where(lane < HEAD, parts, ratio).astype(bf16)


def decode(q, enc, rows):
    width = q.shape[1]
    vmem = pl.BlockSpec(memory_space=pltpu.VMEM)
    return pl.pallas_call(
        decode_kernel,
        in_specs=[pl.BlockSpec(memory_space=pltpu.HBM)] + [vmem] * len(enc),
        out_shape=jax.ShapeDtypeStruct((rows * (width // HEAD), LANES), bf16),
        scratch_shapes=[pltpu.VMEM((rows, width), bf16), pltpu.SemaphoreType.DMA(())],
        compiler_params=params(16),
        cost_estimate=pl.CostEstimate(flops=30_000_000_000, transcendentals=1_000_000, bytes_accessed=1_000_000),
        name="decode",
    )(q, *enc)


def meet_kernel(a, b, c, d, out):
    parts = [x[...].astype(f32) for x in (a, b, c, d)]
    levels = [x[:, 0:1] + x[:, 16:17] + x[:, 32:33] for x in parts]
    peak = jnp.maximum(jnp.maximum(levels[0], levels[1]), jnp.maximum(levels[2], levels[3]))
    scales = [jnp.exp(n - peak) for n in levels]
    total = scales[0] + scales[1] + scales[2] + scales[3]
    value = parts[0] * scales[0]
    for x, s in zip(parts[1:], scales[1:]):
        value = value + x * s
    value = (value / total).astype(bf16)
    copies, rows, width = out.shape
    for p in range(width // LANES):
        e = value[2 * p * rows : (2 * p + 1) * rows, HEAD:]
        o = value[(2 * p + 1) * rows : (2 * p + 2) * rows, HEAD:]
        both = jnp.concatenate([e, o], axis=1)
        for n in range(copies):
            out[n, :, p * LANES : (p + 1) * LANES] = both


def meet(parts, copies, rows, width):
    return pl.pallas_call(
        meet_kernel,
        out_shape=jax.ShapeDtypeStruct((copies, rows, width), bf16),
        compiler_params=params(8),
        cost_estimate=pl.CostEstimate(flops=30_000_000_000, transcendentals=0, bytes_accessed=2_000_000),
        name="meet",
    )(*parts)


def stack_kernel(*refs):
    parts, out = refs[:4], refs[-1]
    size = parts[0].shape[0]
    for n, part in enumerate(parts):
        out[n * size : (n + 1) * size] = part[...]


def stack(parts, *others):
    first = parts[0]
    specs = [pl.BlockSpec(memory_space=pltpu.VMEM)] * len(parts)
    return pl.pallas_call(
        stack_kernel,
        in_specs=specs + [pl.BlockSpec(memory_space=pl.ANY)] * len(others),
        out_shape=jax.ShapeDtypeStruct((len(parts) * first.shape[0],) + first.shape[1:], first.dtype),
        compiler_params=params(4),
        name="stack",
    )(*parts, *others)


def around(value, axis, stride=1, ring=None):
    size = lax.axis_size(axis)
    ring = ring or size

    def pairs(d):
        return [(i, i + ((i // stride % ring ^ d) - i // stride % ring) * stride) for i in range(size)]

    return [lax.ppermute(value, axis, pairs(d)) for d in range(1, ring)]


def after_all(value, *others):
    return lax.optimization_barrier((value, others))[0]


def local(
    q_light, k_light, v_light, q_heavy, k_heavy, v_heavy, enc_kv, dec_queries, query_ids, key_ids
):
    n_seq = lax.axis_size(TOKENS)
    n_fine = lax.axis_size("fine")
    side = 4
    width = q_light.shape[2]

    light_kv = jnp.concatenate([k_light[0], v_light[0]], axis=1)

    def rows_of(value):
        return [value] + around(value, "fine", 1, side)

    def square(row):
        return [row] + around(row, "fine", side, n_fine // side)

    chunks = pack(q_heavy[0], k_heavy[0], v_heavy[0])
    enc = square(stack(rows_of(enc_kv[0]), chunks))
    group = lax.all_to_all(after_all(chunks, enc[0]), "fine", 0, 0, tiled=True)

    dec_rows = dec_queries.shape[1] // n_fine
    part = decode(dec_queries[0], enc, dec_rows)

    parts = around(part, "coarse")
    own = pick(key_ids, after_all(group, part, light_kv)).reshape(KGRP * BLOCK, LANES)
    routed = [own] + around(own, "coarse")
    share = meet([after_all(part, own)] + parts, n_fine, dec_rows, width)
    decoded = lax.all_to_all(share, "fine", 0, 0, tiled=True)

    even = lax.ppermute(light_kv, TOKENS, [(i, i ^ 1) for i in range(n_seq)])
    odd = lax.ppermute(after_all(light_kv, share), TOKENS, [(i, (i - 1 ^ 1) + 1) for i in range(1, n_seq - 1)])

    heavy = heavy_attend(after_all(group, even), routed)
    heavy, decoded = lax.optimization_barrier((heavy, decoded))
    heavy = lax.all_to_all(heavy, "fine", 0, 0, tiled=True)
    light, decoded = light_attend(
        q_light[0], k_light[0], v_light[0], even, odd, decoded.reshape(-1, width)
    )
    encoded = join(query_ids, light, heavy)[None]
    return (encoded, decoded[None])


def solution(mesh):
    seq = P("doc", TOKENS, None)
    whole = P("doc", None, None)
    return jax.shard_map(
        local,
        mesh=mesh,
        in_specs=(seq,) * 7 + (whole, P("doc", None), P("doc", None)),
        out_specs=(seq, whole),
        check_vma=False,
    )
```

```python
import jax
import jax.numpy as jnp
from jax import lax
from jax.experimental import pallas as pl
from jax.experimental.pallas import tpu as pltpu
from jax.sharding import PartitionSpec as P

HEAD = 64
LANES = 2 * HEAD
BLOCK = 128
KGRP = 8
HALF = BLOCK // 2
SCALE = HEAD**-0.5
LOG2E = 1.4426950408889634
TOKENS = ("coarse", "fine")
MIB = 1024 * 1024

f32 = jnp.float32
bf16 = jnp.bfloat16


def params(mib):
    return pltpu.CompilerParams(vmem_limit_bytes=mib * MIB)


def lane_ids(shape):
    return lax.broadcasted_iota(jnp.int32, shape, len(shape) - 1)


def nt(a, b):
    return lax.dot_general(a, b, (((1,), (1,)), ((), ())), preferred_element_type=f32)


def nn(a, b):
    return jnp.dot(a, b, preferred_element_type=f32)


def pack_kernel(q_hbm, k_hbm, v_hbm, out, q, k, v, sem):
    copies = [
        pltpu.make_async_copy(src, dst, sem.at[n])
        for n, (src, dst) in enumerate(((k_hbm, k), (v_hbm, v), (q_hbm, q)))
    ]
    for c in copies:
        c.start()
    heads = out.shape[0]
    copies[0].wait()
    copies[1].wait()
    for h in range(heads):
        cols = slice(h * HEAD, (h + 1) * HEAD)
        out[h, :BLOCK] = jnp.concatenate([k[:, cols], v[:, cols]], axis=1)
    copies[2].wait()
    for h in range(heads):
        qh = q[:, h * HEAD : (h + 1) * HEAD]
        out[h, BLOCK:] = jnp.concatenate([qh[:HALF], qh[HALF:]], axis=1)


def pack(q, k, v):
    heads = q.shape[1] // HEAD
    hbm = pl.BlockSpec(memory_space=pltpu.HBM)
    return pl.pallas_call(
        pack_kernel,
        in_specs=[hbm] * 3,
        out_shape=jax.ShapeDtypeStruct((heads, BLOCK + HALF, LANES), bf16),
        scratch_shapes=[pltpu.VMEM(x.shape, bf16) for x in (q, k, v)]
        + [pltpu.SemaphoreType.DMA((3,))],
        compiler_params=params(8),
        name="pack",
    )(*(pltpu.with_memory_space_constraint(x, pltpu.HBM) for x in (q, k, v)))


def pick_kernel(ids, kv, out):
    group = lax.axis_index("coarse")
    for s in range(KGRP):
        out[s] = kv[ids[0, group * KGRP + s] - group * kv.shape[0], :BLOCK]


def pick(ids, kv):
    return pl.pallas_call(
        pick_kernel,
        out_shape=jax.ShapeDtypeStruct((KGRP, BLOCK, LANES), bf16),
        in_specs=[pl.BlockSpec(memory_space=pltpu.SMEM), pl.BlockSpec(memory_space=pltpu.VMEM)],
        compiler_params=params(4),
        name="pick",
    )(ids, kv)


def with_ones(kv):
    return jnp.where(lane_ids(kv.shape) < HEAD, jnp.ones_like(kv), kv)


def summed(q, keys):
    peak = total = None
    for k in keys:
        s = nt(q, k)
        top = s.max(axis=1, keepdims=True)
        top = top if peak is None else jnp.maximum(peak, top)
        o = nn(jnp.exp2((s - top) * (SCALE * LOG2E)).astype(bf16), with_ones(k))
        total = o if peak is None else total * jnp.exp2((peak - top) * (SCALE * LOG2E)) + o
        peak = top
    return total, peak


def heavy_kernel(q, kv0, kv1, kv2, kv3, out, late, sem):
    copies = [pltpu.make_async_copy(kv, late.at[n], sem.at[n]) for n, kv in enumerate((kv1, kv2))]
    for copy in copies:
        copy.start()

    def arriving():
        yield kv0[...]
        yield kv3[...]
        for n, copy in enumerate(copies):
            copy.wait()
            yield late[n]

    rows = q.shape[0] * HALF
    both = q[:, BLOCK:].reshape(rows, LANES)
    zero = jnp.zeros((rows, HEAD), bf16)
    a, _ = summed(jnp.concatenate([both[:, :HEAD], zero], axis=1), arriving())
    keys = [kv0[...], kv3[...]] + [late[n] for n in range(len(copies))]
    b, _ = summed(jnp.concatenate([both[:, HEAD:], zero], axis=1), keys)
    low = lane_ids(a.shape) < HEAD
    top = jnp.where(low, pltpu.roll(a, HEAD, 1), b)
    sums = jnp.where(low, a, pltpu.roll(b, HEAD, 1))
    out[...] = (top / sums).astype(bf16).reshape(out.shape)


def heavy_attend(q_kv, kvs):
    vmem = pl.BlockSpec(memory_space=pltpu.VMEM)
    own = kvs[0]
    return pl.pallas_call(
        heavy_kernel,
        in_specs=[vmem] * 2 + [pl.BlockSpec(memory_space=pl.ANY)] * 2 + [vmem],
        out_shape=jax.ShapeDtypeStruct((q_kv.shape[0], HALF, LANES), bf16),
        scratch_shapes=[pltpu.VMEM((2,) + own.shape, bf16), pltpu.SemaphoreType.DMA((2,))],
        compiler_params=params(28),
        cost_estimate=pl.CostEstimate(flops=10_000_000_000, transcendentals=8_000_000, bytes_accessed=2_000_000),
        name="heavy",
    )(q_kv, *kvs)


def light_kernel(q, k, v, even, odd, rows_in, out, rows_out, sem):
    count = rows_in.shape[0] // 4
    copies = [
        pltpu.make_async_copy(rows_in.at[pl.ds(n * count, count)], rows_out.at[pl.ds(n * count, count)], sem.at[n])
        for n in range(4)
    ]
    for copy in copies:
        copy.start()
    here = lax.axis_index(TOKENS)
    last = lax.axis_size(TOKENS) - 1
    rows, width = q.shape
    low = lane_ids((rows, LANES)) < HEAD
    i = lax.broadcasted_iota(jnp.int32, (2 * rows, BLOCK), 0) % rows
    j = lax.broadcasted_iota(jnp.int32, (2 * rows, BLOCK), 1)
    ahead = (j - i) * (1 - 2 * (here % 2))
    sees_even = ahead < 0
    sees_odd = (ahead > 0) & (here > 0) & (here < last)
    for p in range(width // LANES):
        c = slice(p * LANES, (p + 1) * LANES)
        cv = slice(width + p * LANES, width + (p + 1) * LANES)
        qq = q[:, c]
        zero = jnp.zeros_like(qq)
        two = jnp.concatenate([jnp.where(low, qq, zero), jnp.where(low, zero, qq)], axis=0)
        own = nt(two, k[:, c])
        first = jnp.where(sees_even, nt(two, even[:, c]), f32(-1e30))
        second = jnp.where(sees_odd, nt(two, odd[:, c]), f32(-1e30))
        peak = jnp.maximum(jnp.maximum(own, first), second).max(axis=1, keepdims=True)
        po, pe, pd = (jnp.exp2((s - peak) * (SCALE * LOG2E)) for s in (own, first, second))
        total = (po + pe + pd).sum(axis=1, keepdims=True)
        o = nn(po.astype(bf16), v[:, c]) + nn(pe.astype(bf16), even[:, cv]) + nn(pd.astype(bf16), odd[:, cv])
        o = o / total
        out[:, c] = jnp.where(low, o[:rows], o[rows:])
    for copy in copies:
        copy.wait()


def light_attend(q, k, v, even, odd, decoded):
    vmem = pl.BlockSpec(memory_space=pltpu.VMEM)
    hbm = pl.BlockSpec(memory_space=pl.ANY)
    return pl.pallas_call(
        light_kernel,
        in_specs=[vmem] * 5 + [hbm],
        out_specs=(vmem, hbm),
        out_shape=(jax.ShapeDtypeStruct(q.shape, f32), jax.ShapeDtypeStruct(decoded.shape, bf16)),
        scratch_shapes=[pltpu.SemaphoreType.DMA((4,))],
        compiler_params=params(12),
        cost_estimate=pl.CostEstimate(flops=3_000_000_000, transcendentals=800_000, bytes_accessed=2_000_000),
        name="light",
    )(q, k, v, even, odd, decoded)


def join_kernel(ids, light, heavy, out, both, sem):
    here = lax.axis_index(TOKENS)
    count = jnp.int32(0)
    for n in range(ids.shape[1]):
        count = count + jnp.where(ids[0, n] == here, 1, 0)
    scale = count.astype(f32)
    pairs = heavy.shape[0] // 2
    step = pairs // 4
    copies = []
    for p in range(pairs):
        e, o = heavy[2 * p], heavy[2 * p + 1]
        cols = slice(p * LANES, (p + 1) * LANES)
        for n in range(2):
            rows, lanes = slice(n * HALF, (n + 1) * HALF), slice(n * HEAD, (n + 1) * HEAD)
            added = jnp.concatenate([e[:, lanes], o[:, lanes]], axis=1)
            both[rows, cols] = (light[rows, cols] + added.astype(f32) * scale).astype(bf16)
        if p % step == step - 1:
            part = pl.ds((p + 1 - step) * LANES, step * LANES)
            copies.append(pltpu.make_async_copy(both.at[:, part], out.at[:, part], sem.at[p // step]))
            copies[-1].start()
    for copy in copies:
        copy.wait()


def join(ids, light, heavy):
    vmem = pl.BlockSpec(memory_space=pltpu.VMEM)
    return pl.pallas_call(
        join_kernel,
        in_specs=[pl.BlockSpec(memory_space=pltpu.SMEM), vmem, vmem],
        out_specs=pl.BlockSpec(memory_space=pl.ANY),
        out_shape=jax.ShapeDtypeStruct(light.shape, bf16),
        scratch_shapes=[pltpu.VMEM(light.shape, bf16), pltpu.SemaphoreType.DMA((4,))],
        compiler_params=params(6),
        name="join",
    )(ids, light, heavy)


def decode_kernel(q_hbm, e0, e1, e2, e3, out, q, sem):
    rows, width = q.shape
    at = pl.multiple_of(lax.axis_index("fine") * rows, rows)
    copy = pltpu.make_async_copy(q_hbm.at[pl.ds(at, rows)], q, sem)
    copy.start()
    copy.wait()
    zero = jnp.zeros((rows, HEAD), bf16)
    stack = jnp.concatenate(
        [
            jnp.concatenate([q[:, h * HEAD : (h + 1) * HEAD], zero], axis=1)
            for h in range(width // HEAD)
        ],
        axis=0,
    )
    keys = [e[...] for e in (e0, e1, e2, e3)]
    total, peak = summed(stack, keys)
    lane = lane_ids(total.shape)
    level = peak * SCALE + jnp.log(total)
    hi = level.astype(bf16).astype(f32)
    mid = (level - hi).astype(bf16).astype(f32)
    least = level - hi - mid
    parts = jnp.where(lane < 16, hi, jnp.where(lane < 32, mid, least))
    ratio = total / pltpu.roll(total, HEAD, 1)
    out[...] = jnp.where(lane < HEAD, parts, ratio).astype(bf16)


def decode(q, enc, rows):
    width = q.shape[1]
    vmem = pl.BlockSpec(memory_space=pltpu.VMEM)
    return pl.pallas_call(
        decode_kernel,
        in_specs=[pl.BlockSpec(memory_space=pltpu.HBM)] + [vmem] * len(enc),
        out_shape=jax.ShapeDtypeStruct((rows * (width // HEAD), LANES), bf16),
        scratch_shapes=[pltpu.VMEM((rows, width), bf16), pltpu.SemaphoreType.DMA(())],
        compiler_params=params(16),
        cost_estimate=pl.CostEstimate(flops=30_000_000_000, transcendentals=1_000_000, bytes_accessed=1_000_000),
        name="decode",
    )(q, *enc)


def meet_kernel(a, b, c, d, out):
    parts = [x[...].astype(f32) for x in (a, b, c, d)]
    levels = [x[:, 0:1] + x[:, 16:17] + x[:, 32:33] for x in parts]
    peak = jnp.maximum(jnp.maximum(levels[0], levels[1]), jnp.maximum(levels[2], levels[3]))
    scales = [jnp.exp(n - peak) for n in levels]
    total = scales[0] + scales[1] + scales[2] + scales[3]
    value = parts[0] * scales[0]
    for x, s in zip(parts[1:], scales[1:]):
        value = value + x * s
    value = (value / total).astype(bf16)
    copies, rows, width = out.shape
    for p in range(width // LANES):
        e = value[2 * p * rows : (2 * p + 1) * rows, HEAD:]
        o = value[(2 * p + 1) * rows : (2 * p + 2) * rows, HEAD:]
        both = jnp.concatenate([e, o], axis=1)
        for n in range(copies):
            out[n, :, p * LANES : (p + 1) * LANES] = both


def meet(parts, copies, rows, width):
    return pl.pallas_call(
        meet_kernel,
        out_shape=jax.ShapeDtypeStruct((copies, rows, width), bf16),
        compiler_params=params(8),
        cost_estimate=pl.CostEstimate(flops=30_000_000_000, transcendentals=0, bytes_accessed=2_000_000),
        name="meet",
    )(*parts)


def stack_kernel(*refs):
    parts, out = refs[:4], refs[-1]
    size = parts[0].shape[0]
    for n, part in enumerate(parts):
        out[n * size : (n + 1) * size] = part[...]


def stack(parts, *others):
    first = parts[0]
    specs = [pl.BlockSpec(memory_space=pltpu.VMEM)] * len(parts)
    return pl.pallas_call(
        stack_kernel,
        in_specs=specs + [pl.BlockSpec(memory_space=pl.ANY)] * len(others),
        out_shape=jax.ShapeDtypeStruct((len(parts) * first.shape[0],) + first.shape[1:], first.dtype),
        compiler_params=params(4),
        name="stack",
    )(*parts, *others)


def around(value, axis, stride=1, ring=None):
    size = lax.axis_size(axis)
    ring = ring or size

    def pairs(d):
        return [(i, i + ((i // stride % ring ^ d) - i // stride % ring) * stride) for i in range(size)]

    return [lax.ppermute(value, axis, pairs(d)) for d in range(1, ring)]


def after_all(value, *others):
    return lax.optimization_barrier((value, others))[0]


def local(
    q_light, k_light, v_light, q_heavy, k_heavy, v_heavy, enc_kv, dec_queries, query_ids, key_ids
):
    n_seq = lax.axis_size(TOKENS)
    n_fine = lax.axis_size("fine")
    side = 4
    width = q_light.shape[2]

    light_kv = jnp.concatenate([k_light[0], v_light[0]], axis=1)

    def rows_of(value):
        return [value] + around(value, "fine", 1, side)

    def square(row):
        return [row] + around(row, "fine", side, n_fine // side)

    chunks = pack(q_heavy[0], k_heavy[0], v_heavy[0])
    enc = square(stack(rows_of(enc_kv[0]), chunks))
    group = lax.all_to_all(after_all(chunks, enc[0]), "fine", 0, 0, tiled=True)

    dec_rows = dec_queries.shape[1] // n_fine
    part = decode(dec_queries[0], enc, dec_rows)

    parts = around(part, "coarse")
    own = pick(key_ids, after_all(group, part, light_kv)).reshape(KGRP * BLOCK, LANES)
    routed = [own] + around(own, "coarse")
    share = meet([after_all(part, own)] + parts, n_fine, dec_rows, width)
    decoded = lax.all_to_all(share, "fine", 0, 0, tiled=True)

    even = lax.ppermute(light_kv, TOKENS, [(i, i ^ 1) for i in range(n_seq)])
    odd = lax.ppermute(after_all(light_kv, share), TOKENS, [(i, (i - 1 ^ 1) + 1) for i in range(1, n_seq - 1)])

    heavy = heavy_attend(after_all(group, even), routed)
    heavy, decoded = lax.optimization_barrier((heavy, decoded))
    heavy = lax.all_to_all(heavy, "fine", 0, 0, tiled=True)
    light, decoded = light_attend(
        q_light[0], k_light[0], v_light[0], even, odd, decoded.reshape(-1, width)
    )
    encoded = join(query_ids, light, heavy)[None]
    return (encoded, decoded[None])


def solution(mesh):
    seq = P("doc", TOKENS, None)
    whole = P("doc", None, None)
    return jax.shard_map(
        local,
        mesh=mesh,
        in_specs=(seq,) * 7 + (whole, P("doc", None), P("doc", None)),
        out_specs=(seq, whole),
        check_vma=False,
    )
```

```python
import jax
import jax.numpy as jnp
from jax import lax
from jax.experimental import pallas as pl
from jax.experimental.pallas import tpu as pltpu
from jax.sharding import PartitionSpec as P

HEAD = 64
LANES = 2 * HEAD
BLOCK = 128
KGRP = 8
HALF = BLOCK // 2
SCALE = HEAD**-0.5
LOG2E = 1.4426950408889634
TOKENS = ("coarse", "fine")
MIB = 1024 * 1024

f32 = jnp.float32
bf16 = jnp.bfloat16


def params(mib):
    return pltpu.CompilerParams(vmem_limit_bytes=mib * MIB)


def lane_ids(shape):
    return lax.broadcasted_iota(jnp.int32, shape, len(shape) - 1)


def nt(a, b):
    return lax.dot_general(a, b, (((1,), (1,)), ((), ())), preferred_element_type=f32)


def nn(a, b):
    return jnp.dot(a, b, preferred_element_type=f32)


def pack_kernel(q_hbm, k_hbm, v_hbm, out, q, k, v, sem):
    copies = [
        pltpu.make_async_copy(src, dst, sem.at[n])
        for n, (src, dst) in enumerate(((k_hbm, k), (v_hbm, v), (q_hbm, q)))
    ]
    for c in copies:
        c.start()
    heads = out.shape[0]
    copies[0].wait()
    copies[1].wait()
    for h in range(heads):
        cols = slice(h * HEAD, (h + 1) * HEAD)
        out[h, :BLOCK] = jnp.concatenate([k[:, cols], v[:, cols]], axis=1)
    copies[2].wait()
    for h in range(heads):
        qh = q[:, h * HEAD : (h + 1) * HEAD]
        out[h, BLOCK:] = jnp.concatenate([qh[:HALF], qh[HALF:]], axis=1)


def pack(q, k, v):
    heads = q.shape[1] // HEAD
    hbm = pl.BlockSpec(memory_space=pltpu.HBM)
    return pl.pallas_call(
        pack_kernel,
        in_specs=[hbm] * 3,
        out_shape=jax.ShapeDtypeStruct((heads, BLOCK + HALF, LANES), bf16),
        scratch_shapes=[pltpu.VMEM(x.shape, bf16) for x in (q, k, v)]
        + [pltpu.SemaphoreType.DMA((3,))],
        compiler_params=params(8),
        name="pack",
    )(*(pltpu.with_memory_space_constraint(x, pltpu.HBM) for x in (q, k, v)))


def pick_kernel(ids, kv, out):
    group = lax.axis_index("coarse")
    for s in range(KGRP):
        out[s] = kv[ids[0, group * KGRP + s] - group * kv.shape[0], :BLOCK]


def pick(ids, kv):
    return pl.pallas_call(
        pick_kernel,
        out_shape=jax.ShapeDtypeStruct((KGRP, BLOCK, LANES), bf16),
        in_specs=[pl.BlockSpec(memory_space=pltpu.SMEM), pl.BlockSpec(memory_space=pltpu.VMEM)],
        compiler_params=params(4),
        name="pick",
    )(ids, kv)


def with_ones(kv):
    return jnp.where(lane_ids(kv.shape) < HEAD, jnp.ones_like(kv), kv)


def summed(q, keys):
    peak = total = None
    for k in keys:
        s = nt(q, k)
        top = s.max(axis=1, keepdims=True)
        top = top if peak is None else jnp.maximum(peak, top)
        o = nn(jnp.exp2((s - top) * (SCALE * LOG2E)).astype(bf16), with_ones(k))
        total = o if peak is None else total * jnp.exp2((peak - top) * (SCALE * LOG2E)) + o
        peak = top
    return total, peak


def heavy_kernel(q, kv0, kv1, kv2, kv3, out, late, sem):
    copies = [pltpu.make_async_copy(kv, late.at[n], sem.at[n]) for n, kv in enumerate((kv1, kv2))]
    for copy in copies:
        copy.start()

    def arriving():
        yield kv0[...]
        yield kv3[...]
        for n, copy in enumerate(copies):
            copy.wait()
            yield late[n]

    rows = q.shape[0] * HALF
    both = q[:, BLOCK:].reshape(rows, LANES)
    zero = jnp.zeros((rows, HEAD), bf16)
    a, _ = summed(jnp.concatenate([both[:, :HEAD], zero], axis=1), arriving())
    keys = [kv0[...], kv3[...]] + [late[n] for n in range(len(copies))]
    b, _ = summed(jnp.concatenate([both[:, HEAD:], zero], axis=1), keys)
    low = lane_ids(a.shape) < HEAD
    top = jnp.where(low, pltpu.roll(a, HEAD, 1), b)
    sums = jnp.where(low, a, pltpu.roll(b, HEAD, 1))
    out[...] = (top / sums).astype(bf16).reshape(out.shape)


def heavy_attend(q_kv, kvs):
    vmem = pl.BlockSpec(memory_space=pltpu.VMEM)
    own = kvs[0]
    return pl.pallas_call(
        heavy_kernel,
        in_specs=[vmem] * 2 + [pl.BlockSpec(memory_space=pl.ANY)] * 2 + [vmem],
        out_shape=jax.ShapeDtypeStruct((q_kv.shape[0], HALF, LANES), bf16),
        scratch_shapes=[pltpu.VMEM((2,) + own.shape, bf16), pltpu.SemaphoreType.DMA((2,))],
        compiler_params=params(28),
        cost_estimate=pl.CostEstimate(flops=10_000_000_000, transcendentals=8_000_000, bytes_accessed=2_000_000),
        name="heavy",
    )(q_kv, *kvs)


def light_kernel(q, k, v, even, odd, cross, rows_in, out, rows_out, sem):
    count = rows_in.shape[0] // 4
    copies = [
        pltpu.make_async_copy(rows_in.at[pl.ds(n * count, count)], rows_out.at[pl.ds(n * count, count)], sem.at[n])
        for n in range(4)
    ]
    for copy in copies:
        copy.start()
    here = lax.axis_index(TOKENS)
    last = lax.axis_size(TOKENS) - 1
    rows, width = q.shape
    low = lane_ids((rows, LANES)) < HEAD
    i = lax.broadcasted_iota(jnp.int32, (2 * rows, BLOCK), 0) % rows
    j = lax.broadcasted_iota(jnp.int32, (2 * rows, BLOCK), 1)
    ahead = (j - i) * (1 - 2 * (here % 2))
    sees_even = ahead < 0
    sees_odd = (ahead > 0) & (here > 0) & (here < last)
    for p in range(width // LANES):
        c = slice(p * LANES, (p + 1) * LANES)
        cv = slice(width + p * LANES, width + (p + 1) * LANES)
        qq = q[:, c]
        zero = jnp.zeros_like(qq)
        two = jnp.concatenate([jnp.where(low, qq, zero), jnp.where(low, zero, qq)], axis=0)
        own = nt(two, k[:, c])
        first = jnp.where(sees_even, nt(two, even[:, c]), f32(-1e30))
        second = jnp.where(sees_odd, nt(two, odd[:, c] + cross[:, c]), f32(-1e30))
        peak = jnp.maximum(jnp.maximum(own, first), second).max(axis=1, keepdims=True)
        po, pe, pd = (jnp.exp2((s - peak) * (SCALE * LOG2E)) for s in (own, first, second))
        total = (po + pe + pd).sum(axis=1, keepdims=True)
        o = nn(po.astype(bf16), v[:, c]) + nn(pe.astype(bf16), even[:, cv]) + nn(pd.astype(bf16), odd[:, cv] + cross[:, cv])
        o = o / total
        out[:, c] = jnp.where(low, o[:rows], o[rows:])
    for copy in copies:
        copy.wait()


def light_attend(q, k, v, even, odd, cross, decoded):
    vmem = pl.BlockSpec(memory_space=pltpu.VMEM)
    hbm = pl.BlockSpec(memory_space=pl.ANY)
    return pl.pallas_call(
        light_kernel,
        in_specs=[vmem] * 6 + [hbm],
        out_specs=(vmem, hbm),
        out_shape=(jax.ShapeDtypeStruct(q.shape, f32), jax.ShapeDtypeStruct(decoded.shape, bf16)),
        scratch_shapes=[pltpu.SemaphoreType.DMA((4,))],
        compiler_params=params(12),
        cost_estimate=pl.CostEstimate(flops=3_000_000_000, transcendentals=800_000, bytes_accessed=2_000_000),
        name="light",
    )(q, k, v, even, odd, cross, decoded)


def join_kernel(ids, light, heavy, out, both, sem):
    here = lax.axis_index(TOKENS)
    count = jnp.int32(0)
    for n in range(ids.shape[1]):
        count = count + jnp.where(ids[0, n] == here, 1, 0)
    scale = count.astype(f32)
    pairs = heavy.shape[0] // 2
    step = pairs // 4
    copies = []
    for p in range(pairs):
        e, o = heavy[2 * p], heavy[2 * p + 1]
        cols = slice(p * LANES, (p + 1) * LANES)
        for n in range(2):
            rows, lanes = slice(n * HALF, (n + 1) * HALF), slice(n * HEAD, (n + 1) * HEAD)
            added = jnp.concatenate([e[:, lanes], o[:, lanes]], axis=1)
            both[rows, cols] = (light[rows, cols] + added.astype(f32) * scale).astype(bf16)
        if p % step == step - 1:
            part = pl.ds((p + 1 - step) * LANES, step * LANES)
            copies.append(pltpu.make_async_copy(both.at[:, part], out.at[:, part], sem.at[p // step]))
            copies[-1].start()
    for copy in copies:
        copy.wait()


def join(ids, light, heavy):
    vmem = pl.BlockSpec(memory_space=pltpu.VMEM)
    return pl.pallas_call(
        join_kernel,
        in_specs=[pl.BlockSpec(memory_space=pltpu.SMEM), vmem, vmem],
        out_specs=pl.BlockSpec(memory_space=pl.ANY),
        out_shape=jax.ShapeDtypeStruct(light.shape, bf16),
        scratch_shapes=[pltpu.VMEM(light.shape, bf16), pltpu.SemaphoreType.DMA((4,))],
        compiler_params=params(6),
        name="join",
    )(ids, light, heavy)


def decode_kernel(q_hbm, e0, e1, e2, e3, out, q, sem):
    rows, width = q.shape
    at = pl.multiple_of(lax.axis_index("fine") * rows, rows)
    copy = pltpu.make_async_copy(q_hbm.at[pl.ds(at, rows)], q, sem)
    copy.start()
    copy.wait()
    zero = jnp.zeros((rows, HEAD), bf16)
    stack = jnp.concatenate(
        [
            jnp.concatenate([q[:, h * HEAD : (h + 1) * HEAD], zero], axis=1)
            for h in range(width // HEAD)
        ],
        axis=0,
    )
    keys = [e[...] for e in (e0, e1, e2, e3)]
    total, peak = summed(stack, keys)
    lane = lane_ids(total.shape)
    level = peak * SCALE + jnp.log(total)
    hi = level.astype(bf16).astype(f32)
    mid = (level - hi).astype(bf16).astype(f32)
    least = level - hi - mid
    parts = jnp.where(lane < 16, hi, jnp.where(lane < 32, mid, least))
    ratio = total / pltpu.roll(total, HEAD, 1)
    out[...] = jnp.where(lane < HEAD, parts, ratio).astype(bf16)


def decode(q, enc, rows):
    width = q.shape[1]
    vmem = pl.BlockSpec(memory_space=pltpu.VMEM)
    return pl.pallas_call(
        decode_kernel,
        in_specs=[pl.BlockSpec(memory_space=pltpu.HBM)] + [vmem] * len(enc),
        out_shape=jax.ShapeDtypeStruct((rows * (width // HEAD), LANES), bf16),
        scratch_shapes=[pltpu.VMEM((rows, width), bf16), pltpu.SemaphoreType.DMA(())],
        compiler_params=params(16),
        cost_estimate=pl.CostEstimate(flops=30_000_000_000, transcendentals=1_000_000, bytes_accessed=1_000_000),
        name="decode",
    )(q, *enc)


def meet_kernel(a, b, c, d, out):
    parts = [x[...].astype(f32) for x in (a, b, c, d)]
    levels = [x[:, 0:1] + x[:, 16:17] + x[:, 32:33] for x in parts]
    peak = jnp.maximum(jnp.maximum(levels[0], levels[1]), jnp.maximum(levels[2], levels[3]))
    scales = [jnp.exp(n - peak) for n in levels]
    total = scales[0] + scales[1] + scales[2] + scales[3]
    value = parts[0] * scales[0]
    for x, s in zip(parts[1:], scales[1:]):
        value = value + x * s
    value = (value / total).astype(bf16)
    copies, rows, width = out.shape
    for p in range(width // LANES):
        e = value[2 * p * rows : (2 * p + 1) * rows, HEAD:]
        o = value[(2 * p + 1) * rows : (2 * p + 2) * rows, HEAD:]
        both = jnp.concatenate([e, o], axis=1)
        for n in range(copies):
            out[n, :, p * LANES : (p + 1) * LANES] = both


def meet(parts, copies, rows, width):
    return pl.pallas_call(
        meet_kernel,
        out_shape=jax.ShapeDtypeStruct((copies, rows, width), bf16),
        compiler_params=params(8),
        cost_estimate=pl.CostEstimate(flops=30_000_000_000, transcendentals=0, bytes_accessed=2_000_000),
        name="meet",
    )(*parts)


def stack_kernel(*refs):
    parts, out = refs[:4], refs[-1]
    size = parts[0].shape[0]
    for n, part in enumerate(parts):
        out[n * size : (n + 1) * size] = part[...]


def stack(parts, *others):
    first = parts[0]
    specs = [pl.BlockSpec(memory_space=pltpu.VMEM)] * len(parts)
    return pl.pallas_call(
        stack_kernel,
        in_specs=specs + [pl.BlockSpec(memory_space=pl.ANY)] * len(others),
        out_shape=jax.ShapeDtypeStruct((len(parts) * first.shape[0],) + first.shape[1:], first.dtype),
        compiler_params=params(4),
        name="stack",
    )(*parts, *others)


def around(value, axis, stride=1, ring=None):
    size = lax.axis_size(axis)
    ring = ring or size

    def pairs(d):
        return [(i, i + ((i // stride % ring ^ d) - i // stride % ring) * stride) for i in range(size)]

    return [lax.ppermute(value, axis, pairs(d)) for d in range(1, ring)]


def after_all(value, *others):
    return lax.optimization_barrier((value, others))[0]


def local(
    q_light, k_light, v_light, q_heavy, k_heavy, v_heavy, enc_kv, dec_queries, query_ids, key_ids
):
    n_seq = lax.axis_size(TOKENS)
    n_fine = lax.axis_size("fine")
    side = 4
    width = q_light.shape[2]

    def rows_of(value):
        return [value] + around(value, "fine", 1, side)

    def square(row):
        return [row] + around(row, "fine", side, n_fine // side)

    chunks = pack(q_heavy[0], k_heavy[0], v_heavy[0])
    enc = square(stack(rows_of(enc_kv[0]), chunks))
    light_kv = jnp.concatenate([after_all(k_light[0], enc[0]), v_light[0]], axis=1)
    odd_pairs = [(i, (i - 1 ^ 1) + 1) for i in range(1, n_seq - 1)]
    even = lax.ppermute(light_kv, TOKENS, [(i, i ^ 1) for i in range(n_seq)])
    odd = lax.ppermute(light_kv, TOKENS, [(i, j) for i, j in odd_pairs if i // n_fine == j // n_fine])
    cross = lax.ppermute(light_kv, TOKENS, [(i, j) for i, j in odd_pairs if i // n_fine != j // n_fine])

    group = lax.all_to_all(after_all(chunks, enc[0]), "fine", 0, 0, tiled=True)

    dec_rows = dec_queries.shape[1] // n_fine
    part = decode(dec_queries[0], enc, dec_rows)

    parts = around(part, "coarse")
    own = pick(key_ids, after_all(group, part, cross)).reshape(KGRP * BLOCK, LANES)
    routed = [own] + around(own, "coarse")
    share = meet([after_all(part, own)] + parts, n_fine, dec_rows, width)
    decoded = lax.all_to_all(share, "fine", 0, 0, tiled=True)

    heavy = heavy_attend(after_all(group, even, odd), routed)
    heavy, decoded = lax.optimization_barrier((heavy, decoded))
    heavy = lax.all_to_all(heavy, "fine", 0, 0, tiled=True)
    light, decoded = light_attend(
        q_light[0], k_light[0], v_light[0], even, odd, cross, decoded.reshape(-1, width)
    )
    encoded = join(query_ids, light, heavy)[None]
    return (encoded, decoded[None])


def solution(mesh):
    seq = P("doc", TOKENS, None)
    whole = P("doc", None, None)
    return jax.shard_map(
        local,
        mesh=mesh,
        in_specs=(seq,) * 7 + (whole, P("doc", None), P("doc", None)),
        out_specs=(seq, whole),
        check_vma=False,
    )
```

```python
import jax
import jax.numpy as jnp
from jax import lax
from jax.experimental import pallas as pl
from jax.experimental.pallas import tpu as pltpu
from jax.sharding import PartitionSpec as P

HEAD = 64
LANES = 2 * HEAD
BLOCK = 128
KGRP = 8
HALF = BLOCK // 2
SCALE = HEAD**-0.5
LOG2E = 1.4426950408889634
TOKENS = ("coarse", "fine")
MIB = 1024 * 1024

f32 = jnp.float32
bf16 = jnp.bfloat16


def params(mib):
    return pltpu.CompilerParams(vmem_limit_bytes=mib * MIB)


def lane_ids(shape):
    return lax.broadcasted_iota(jnp.int32, shape, len(shape) - 1)


def nt(a, b):
    return lax.dot_general(a, b, (((1,), (1,)), ((), ())), preferred_element_type=f32)


def nn(a, b):
    return jnp.dot(a, b, preferred_element_type=f32)


def pack_kernel(q_hbm, k_hbm, v_hbm, out, q, k, v, sem):
    copies = [
        pltpu.make_async_copy(src, dst, sem.at[n])
        for n, (src, dst) in enumerate(((k_hbm, k), (v_hbm, v), (q_hbm, q)))
    ]
    for c in copies:
        c.start()
    heads = out.shape[0]
    copies[0].wait()
    copies[1].wait()
    for h in range(heads):
        cols = slice(h * HEAD, (h + 1) * HEAD)
        out[h, :BLOCK] = jnp.concatenate([k[:, cols], v[:, cols]], axis=1)
    copies[2].wait()
    for h in range(heads):
        qh = q[:, h * HEAD : (h + 1) * HEAD]
        out[h, BLOCK:] = jnp.concatenate([qh[:HALF], qh[HALF:]], axis=1)


def pack(q, k, v):
    heads = q.shape[1] // HEAD
    hbm = pl.BlockSpec(memory_space=pltpu.HBM)
    return pl.pallas_call(
        pack_kernel,
        in_specs=[hbm] * 3,
        out_shape=jax.ShapeDtypeStruct((heads, BLOCK + HALF, LANES), bf16),
        scratch_shapes=[pltpu.VMEM(x.shape, bf16) for x in (q, k, v)]
        + [pltpu.SemaphoreType.DMA((3,))],
        compiler_params=params(8),
        name="pack",
    )(*(pltpu.with_memory_space_constraint(x, pltpu.HBM) for x in (q, k, v)))


def pick_kernel(ids, kv, out):
    group = lax.axis_index("coarse")
    for s in range(KGRP):
        out[s] = kv[ids[0, group * KGRP + s] - group * kv.shape[0], :BLOCK]


def pick(ids, kv):
    return pl.pallas_call(
        pick_kernel,
        out_shape=jax.ShapeDtypeStruct((KGRP, BLOCK, LANES), bf16),
        in_specs=[pl.BlockSpec(memory_space=pltpu.SMEM), pl.BlockSpec(memory_space=pltpu.VMEM)],
        compiler_params=params(4),
        name="pick",
    )(ids, kv)


def with_ones(kv):
    return jnp.where(lane_ids(kv.shape) < HEAD, jnp.ones_like(kv), kv)


def summed(q, keys):
    peak = total = None
    for k in keys:
        s = nt(q, k)
        top = s.max(axis=1, keepdims=True)
        top = top if peak is None else jnp.maximum(peak, top)
        o = nn(jnp.exp2((s - top) * (SCALE * LOG2E)).astype(bf16), with_ones(k))
        total = o if peak is None else total * jnp.exp2((peak - top) * (SCALE * LOG2E)) + o
        peak = top
    return total, peak


def heavy_kernel(q, kv0, kv1, kv2, kv3, out, late, sem):
    copies = [pltpu.make_async_copy(kv, late.at[n], sem.at[n]) for n, kv in enumerate((kv1, kv2))]
    for copy in copies:
        copy.start()

    def arriving():
        yield kv0[...]
        yield kv3[...]
        for n, copy in enumerate(copies):
            copy.wait()
            yield late[n]

    rows = q.shape[0] * HALF
    both = q[:, BLOCK:].reshape(rows, LANES)
    zero = jnp.zeros((rows, HEAD), bf16)
    a, _ = summed(jnp.concatenate([both[:, :HEAD], zero], axis=1), arriving())
    keys = [kv0[...], kv3[...]] + [late[n] for n in range(len(copies))]
    b, _ = summed(jnp.concatenate([both[:, HEAD:], zero], axis=1), keys)
    low = lane_ids(a.shape) < HEAD
    top = jnp.where(low, pltpu.roll(a, HEAD, 1), b)
    sums = jnp.where(low, a, pltpu.roll(b, HEAD, 1))
    out[...] = (top / sums).astype(bf16).reshape(out.shape)


def heavy_attend(q_kv, kvs):
    vmem = pl.BlockSpec(memory_space=pltpu.VMEM)
    own = kvs[0]
    return pl.pallas_call(
        heavy_kernel,
        in_specs=[vmem] * 2 + [pl.BlockSpec(memory_space=pl.ANY)] * 2 + [vmem],
        out_shape=jax.ShapeDtypeStruct((q_kv.shape[0], HALF, LANES), bf16),
        scratch_shapes=[pltpu.VMEM((2,) + own.shape, bf16), pltpu.SemaphoreType.DMA((2,))],
        compiler_params=params(28),
        cost_estimate=pl.CostEstimate(flops=10_000_000_000, transcendentals=8_000_000, bytes_accessed=2_000_000),
        name="heavy",
    )(q_kv, *kvs)


def light_kernel(q, k, v, even, odd, rows_in, out, rows_out, sem):
    count = rows_in.shape[0] // 4
    copies = [
        pltpu.make_async_copy(rows_in.at[pl.ds(n * count, count)], rows_out.at[pl.ds(n * count, count)], sem.at[n])
        for n in range(4)
    ]
    for copy in copies:
        copy.start()
    here = lax.axis_index(TOKENS)
    last = lax.axis_size(TOKENS) - 1
    rows, width = q.shape
    low = lane_ids((rows, LANES)) < HEAD
    i = lax.broadcasted_iota(jnp.int32, (2 * rows, BLOCK), 0) % rows
    j = lax.broadcasted_iota(jnp.int32, (2 * rows, BLOCK), 1)
    ahead = (j - i) * (1 - 2 * (here % 2))
    sees_even = ahead < 0
    sees_odd = (ahead > 0) & (here > 0) & (here < last)
    for p in range(width // LANES):
        c = slice(p * LANES, (p + 1) * LANES)
        cv = slice(width + p * LANES, width + (p + 1) * LANES)
        qq = q[:, c]
        zero = jnp.zeros_like(qq)
        two = jnp.concatenate([jnp.where(low, qq, zero), jnp.where(low, zero, qq)], axis=0)
        own = nt(two, k[:, c])
        first = jnp.where(sees_even, nt(two, even[:, c]), f32(-1e30))
        second = jnp.where(sees_odd, nt(two, odd[:, c]), f32(-1e30))
        peak = jnp.maximum(jnp.maximum(own, first), second).max(axis=1, keepdims=True)
        po, pe, pd = (jnp.exp2((s - peak) * (SCALE * LOG2E)) for s in (own, first, second))
        total = (po + pe + pd).sum(axis=1, keepdims=True)
        o = nn(po.astype(bf16), v[:, c]) + nn(pe.astype(bf16), even[:, cv]) + nn(pd.astype(bf16), odd[:, cv])
        o = o / total
        out[:, c] = jnp.where(low, o[:rows], o[rows:])
    for copy in copies:
        copy.wait()


def light_attend(q, k, v, even, odd, decoded):
    vmem = pl.BlockSpec(memory_space=pltpu.VMEM)
    hbm = pl.BlockSpec(memory_space=pl.ANY)
    return pl.pallas_call(
        light_kernel,
        in_specs=[vmem] * 5 + [hbm],
        out_specs=(vmem, hbm),
        out_shape=(jax.ShapeDtypeStruct(q.shape, f32), jax.ShapeDtypeStruct(decoded.shape, bf16)),
        scratch_shapes=[pltpu.SemaphoreType.DMA((4,))],
        compiler_params=params(12),
        cost_estimate=pl.CostEstimate(flops=3_000_000_000, transcendentals=800_000, bytes_accessed=2_000_000),
        name="light",
    )(q, k, v, even, odd, decoded)


def join_kernel(ids, light, heavy, out, both, sem):
    here = lax.axis_index(TOKENS)
    count = jnp.int32(0)
    for n in range(ids.shape[1]):
        count = count + jnp.where(ids[0, n] == here, 1, 0)
    scale = count.astype(f32)
    pairs = heavy.shape[0] // 2
    step = pairs // 4
    copies = []
    for p in range(pairs):
        e, o = heavy[2 * p], heavy[2 * p + 1]
        cols = slice(p * LANES, (p + 1) * LANES)
        for n in range(2):
            rows, lanes = slice(n * HALF, (n + 1) * HALF), slice(n * HEAD, (n + 1) * HEAD)
            added = jnp.concatenate([e[:, lanes], o[:, lanes]], axis=1)
            both[rows, cols] = (light[rows, cols] + added.astype(f32) * scale).astype(bf16)
        if p % step == step - 1:
            part = pl.ds((p + 1 - step) * LANES, step * LANES)
            copies.append(pltpu.make_async_copy(both.at[:, part], out.at[:, part], sem.at[p // step]))
            copies[-1].start()
    for copy in copies:
        copy.wait()


def join(ids, light, heavy):
    vmem = pl.BlockSpec(memory_space=pltpu.VMEM)
    return pl.pallas_call(
        join_kernel,
        in_specs=[pl.BlockSpec(memory_space=pltpu.SMEM), vmem, vmem],
        out_specs=pl.BlockSpec(memory_space=pl.ANY),
        out_shape=jax.ShapeDtypeStruct(light.shape, bf16),
        scratch_shapes=[pltpu.VMEM(light.shape, bf16), pltpu.SemaphoreType.DMA((4,))],
        compiler_params=params(6),
        name="join",
    )(ids, light, heavy)


def decode_kernel(q_hbm, e0, e1, e2, e3, out, q, sem):
    rows, width = q.shape
    at = pl.multiple_of(lax.axis_index("fine") * rows, rows)
    copy = pltpu.make_async_copy(q_hbm.at[pl.ds(at, rows)], q, sem)
    copy.start()
    copy.wait()
    zero = jnp.zeros((rows, HEAD), bf16)
    stack = jnp.concatenate(
        [
            jnp.concatenate([q[:, h * HEAD : (h + 1) * HEAD], zero], axis=1)
            for h in range(width // HEAD)
        ],
        axis=0,
    )
    keys = [e[...] for e in (e0, e1, e2, e3)]
    total, peak = summed(stack, keys)
    lane = lane_ids(total.shape)
    level = peak * SCALE + jnp.log(total)
    hi = level.astype(bf16).astype(f32)
    mid = (level - hi).astype(bf16).astype(f32)
    least = level - hi - mid
    parts = jnp.where(lane < 16, hi, jnp.where(lane < 32, mid, least))
    ratio = total / pltpu.roll(total, HEAD, 1)
    out[...] = jnp.where(lane < HEAD, parts, ratio).astype(bf16)


def decode(q, enc, rows):
    width = q.shape[1]
    vmem = pl.BlockSpec(memory_space=pltpu.VMEM)
    return pl.pallas_call(
        decode_kernel,
        in_specs=[pl.BlockSpec(memory_space=pltpu.HBM)] + [vmem] * len(enc),
        out_shape=jax.ShapeDtypeStruct((rows * (width // HEAD), LANES), bf16),
        scratch_shapes=[pltpu.VMEM((rows, width), bf16), pltpu.SemaphoreType.DMA(())],
        compiler_params=params(16),
        cost_estimate=pl.CostEstimate(flops=30_000_000_000, transcendentals=1_000_000, bytes_accessed=1_000_000),
        name="decode",
    )(q, *enc)


def meet_kernel(a, b, c, d, out):
    parts = [x[...].astype(f32) for x in (a, b, c, d)]
    levels = [x[:, 0:1] + x[:, 16:17] + x[:, 32:33] for x in parts]
    peak = jnp.maximum(jnp.maximum(levels[0], levels[1]), jnp.maximum(levels[2], levels[3]))
    scales = [jnp.exp(n - peak) for n in levels]
    total = scales[0] + scales[1] + scales[2] + scales[3]
    value = parts[0] * scales[0]
    for x, s in zip(parts[1:], scales[1:]):
        value = value + x * s
    value = (value / total).astype(bf16)
    copies, rows, width = out.shape
    for p in range(width // LANES):
        e = value[2 * p * rows : (2 * p + 1) * rows, HEAD:]
        o = value[(2 * p + 1) * rows : (2 * p + 2) * rows, HEAD:]
        both = jnp.concatenate([e, o], axis=1)
        for n in range(copies):
            out[n, :, p * LANES : (p + 1) * LANES] = both


def meet(parts, copies, rows, width):
    return pl.pallas_call(
        meet_kernel,
        out_shape=jax.ShapeDtypeStruct((copies, rows, width), bf16),
        compiler_params=params(8),
        cost_estimate=pl.CostEstimate(flops=30_000_000_000, transcendentals=0, bytes_accessed=2_000_000),
        name="meet",
    )(*parts)


def stack_kernel(*refs):
    parts, out = refs[:4], refs[-1]
    size = parts[0].shape[0]
    for n, part in enumerate(parts):
        out[n * size : (n + 1) * size] = part[...]


def stack(parts, *others):
    first = parts[0]
    specs = [pl.BlockSpec(memory_space=pltpu.VMEM)] * len(parts)
    return pl.pallas_call(
        stack_kernel,
        in_specs=specs + [pl.BlockSpec(memory_space=pl.ANY)] * len(others),
        out_shape=jax.ShapeDtypeStruct((len(parts) * first.shape[0],) + first.shape[1:], first.dtype),
        compiler_params=params(4),
        name="stack",
    )(*parts, *others)


def around(value, axis, stride=1, ring=None):
    size = lax.axis_size(axis)
    ring = ring or size

    def pairs(d):
        return [(i, i + ((i // stride % ring ^ d) - i // stride % ring) * stride) for i in range(size)]

    return [lax.ppermute(value, axis, pairs(d)) for d in range(1, ring)]


def after_all(value, *others):
    return lax.optimization_barrier((value, others))[0]


def local(
    q_light, k_light, v_light, q_heavy, k_heavy, v_heavy, enc_kv, dec_queries, query_ids, key_ids
):
    n_seq = lax.axis_size(TOKENS)
    n_fine = lax.axis_size("fine")
    side = 4
    width = q_light.shape[2]

    light_kv = jnp.concatenate([k_light[0], v_light[0]], axis=1)

    def rows_of(value):
        return [value] + around(value, "fine", 1, side)

    def square(row):
        return [row] + around(row, "fine", side, n_fine // side)

    chunks = pack(q_heavy[0], k_heavy[0], v_heavy[0])
    enc = square(stack(rows_of(enc_kv[0]), chunks))
    group = lax.all_to_all(after_all(chunks, enc[0]), "fine", 0, 0, tiled=True)

    dec_rows = dec_queries.shape[1] // n_fine
    part = decode(dec_queries[0], enc, dec_rows)

    parts = around(part, "coarse")
    own = pick(key_ids, after_all(group, part, light_kv)).reshape(KGRP * BLOCK, LANES)
    routed = [own] + around(own, "coarse")
    share = meet([after_all(part, own)] + parts, n_fine, dec_rows, width)
    decoded = lax.all_to_all(share, "fine", 0, 0, tiled=True)

    light_kv = after_all(light_kv, share)
    even = lax.ppermute(light_kv, TOKENS, [(i, i ^ 1) for i in range(n_seq)])
    odd = lax.ppermute(light_kv, TOKENS, [(i, (i - 1 ^ 1) + 1) for i in range(1, n_seq - 1)])

    heavy = heavy_attend(group, routed)
    heavy, decoded = lax.optimization_barrier((heavy, decoded))
    heavy = lax.all_to_all(heavy, "fine", 0, 0, tiled=True)
    light, decoded = light_attend(
        q_light[0], k_light[0], v_light[0], even, odd, decoded.reshape(-1, width)
    )
    encoded = join(query_ids, light, heavy)[None]
    return (encoded, decoded[None])


def solution(mesh):
    seq = P("doc", TOKENS, None)
    whole = P("doc", None, None)
    return jax.shard_map(
        local,
        mesh=mesh,
        in_specs=(seq,) * 7 + (whole, P("doc", None), P("doc", None)),
        out_specs=(seq, whole),
        check_vma=False,
    )
```

```python
import jax
import jax.numpy as jnp
from jax import lax
from jax.experimental import pallas as pl
from jax.experimental.pallas import tpu as pltpu
from jax.sharding import PartitionSpec as P

HEAD = 64
LANES = 2 * HEAD
BLOCK = 128
KGRP = 8
HALF = BLOCK // 2
SCALE = HEAD**-0.5
LOG2E = 1.4426950408889634
TOKENS = ("coarse", "fine")
MIB = 1024 * 1024

f32 = jnp.float32
bf16 = jnp.bfloat16


def params(mib):
    return pltpu.CompilerParams(vmem_limit_bytes=mib * MIB)


def lane_ids(shape):
    return lax.broadcasted_iota(jnp.int32, shape, len(shape) - 1)


def nt(a, b):
    return lax.dot_general(a, b, (((1,), (1,)), ((), ())), preferred_element_type=f32)


def nn(a, b):
    return jnp.dot(a, b, preferred_element_type=f32)


def pack_kernel(q_hbm, k_hbm, v_hbm, out, q, k, v, sem):
    copies = [
        pltpu.make_async_copy(src, dst, sem.at[n])
        for n, (src, dst) in enumerate(((k_hbm, k), (v_hbm, v), (q_hbm, q)))
    ]
    for c in copies:
        c.start()
    heads = out.shape[0]
    copies[0].wait()
    copies[1].wait()
    for h in range(heads):
        cols = slice(h * HEAD, (h + 1) * HEAD)
        out[h, :BLOCK] = jnp.concatenate([k[:, cols], v[:, cols]], axis=1)
    copies[2].wait()
    for h in range(heads):
        qh = q[:, h * HEAD : (h + 1) * HEAD]
        out[h, BLOCK:] = jnp.concatenate([qh[:HALF], qh[HALF:]], axis=1)


def pack(q, k, v):
    heads = q.shape[1] // HEAD
    hbm = pl.BlockSpec(memory_space=pltpu.HBM)
    return pl.pallas_call(
        pack_kernel,
        in_specs=[hbm] * 3,
        out_shape=jax.ShapeDtypeStruct((heads, BLOCK + HALF, LANES), bf16),
        scratch_shapes=[pltpu.VMEM(x.shape, bf16) for x in (q, k, v)]
        + [pltpu.SemaphoreType.DMA((3,))],
        compiler_params=params(8),
        name="pack",
    )(*(pltpu.with_memory_space_constraint(x, pltpu.HBM) for x in (q, k, v)))


def pick_kernel(ids, kv, out):
    group = lax.axis_index("coarse")
    for s in range(KGRP):
        out[s] = kv[ids[0, group * KGRP + s] - group * kv.shape[0], :BLOCK]


def pick(ids, kv):
    return pl.pallas_call(
        pick_kernel,
        out_shape=jax.ShapeDtypeStruct((KGRP, BLOCK, LANES), bf16),
        in_specs=[pl.BlockSpec(memory_space=pltpu.SMEM), pl.BlockSpec(memory_space=pltpu.VMEM)],
        compiler_params=params(4),
        name="pick",
    )(ids, kv)


def with_ones(kv):
    return jnp.where(lane_ids(kv.shape) < HEAD, jnp.ones_like(kv), kv)


def summed(q, keys):
    peak = total = None
    for k in keys:
        s = nt(q, k)
        top = s.max(axis=1, keepdims=True)
        top = top if peak is None else jnp.maximum(peak, top)
        o = nn(jnp.exp2((s - top) * (SCALE * LOG2E)).astype(bf16), with_ones(k))
        total = o if peak is None else total * jnp.exp2((peak - top) * (SCALE * LOG2E)) + o
        peak = top
    return total, peak


def heavy_kernel(q, kv0, kv1, kv2, kv3, out, late, sem):
    copies = [pltpu.make_async_copy(kv, late.at[n], sem.at[n]) for n, kv in enumerate((kv1, kv2))]
    for copy in copies:
        copy.start()

    def arriving():
        yield kv0[...]
        yield kv3[...]
        for n, copy in enumerate(copies):
            copy.wait()
            yield late[n]

    rows = q.shape[0] * HALF
    both = q[:, BLOCK:].reshape(rows, LANES)
    zero = jnp.zeros((rows, HEAD), bf16)
    a, _ = summed(jnp.concatenate([both[:, :HEAD], zero], axis=1), arriving())
    keys = [kv0[...], kv3[...]] + [late[n] for n in range(len(copies))]
    b, _ = summed(jnp.concatenate([both[:, HEAD:], zero], axis=1), keys)
    low = lane_ids(a.shape) < HEAD
    top = jnp.where(low, pltpu.roll(a, HEAD, 1), b)
    sums = jnp.where(low, a, pltpu.roll(b, HEAD, 1))
    out[...] = (top / sums).astype(bf16).reshape(out.shape)


def heavy_attend(q_kv, kvs):
    vmem = pl.BlockSpec(memory_space=pltpu.VMEM)
    own = kvs[0]
    return pl.pallas_call(
        heavy_kernel,
        in_specs=[vmem] * 2 + [pl.BlockSpec(memory_space=pl.ANY)] * 2 + [vmem],
        out_shape=jax.ShapeDtypeStruct((q_kv.shape[0], HALF, LANES), bf16),
        scratch_shapes=[pltpu.VMEM((2,) + own.shape, bf16), pltpu.SemaphoreType.DMA((2,))],
        compiler_params=params(28),
        cost_estimate=pl.CostEstimate(flops=10_000_000_000, transcendentals=8_000_000, bytes_accessed=2_000_000),
        name="heavy",
    )(q_kv, *kvs)


def light_kernel(q, k, v, even, odd, rows_in, out, rows_out, sem):
    count = rows_in.shape[0] // 4
    copies = [
        pltpu.make_async_copy(rows_in.at[pl.ds(n * count, count)], rows_out.at[pl.ds(n * count, count)], sem.at[n])
        for n in range(4)
    ]
    for copy in copies:
        copy.start()
    here = lax.axis_index(TOKENS)
    last = lax.axis_size(TOKENS) - 1
    rows, width = q.shape
    low = lane_ids((rows, LANES)) < HEAD
    i = lax.broadcasted_iota(jnp.int32, (2 * rows, BLOCK), 0) % rows
    j = lax.broadcasted_iota(jnp.int32, (2 * rows, BLOCK), 1)
    ahead = (j - i) * (1 - 2 * (here % 2))
    sees_even = ahead < 0
    sees_odd = (ahead > 0) & (here > 0) & (here < last)
    for p in range(width // LANES):
        c = slice(p * LANES, (p + 1) * LANES)
        cv = slice(width + p * LANES, width + (p + 1) * LANES)
        qq = q[:, c]
        zero = jnp.zeros_like(qq)
        two = jnp.concatenate([jnp.where(low, qq, zero), jnp.where(low, zero, qq)], axis=0)
        own = nt(two, k[:, c])
        first = jnp.where(sees_even, nt(two, even[:, c]), f32(-1e30))
        second = jnp.where(sees_odd, nt(two, odd[:, c]), f32(-1e30))
        peak = jnp.maximum(jnp.maximum(own, first), second).max(axis=1, keepdims=True)
        po, pe, pd = (jnp.exp2((s - peak) * (SCALE * LOG2E)) for s in (own, first, second))
        total = (po + pe + pd).sum(axis=1, keepdims=True)
        o = nn(po.astype(bf16), v[:, c]) + nn(pe.astype(bf16), even[:, cv]) + nn(pd.astype(bf16), odd[:, cv])
        o = o / total
        out[:, c] = jnp.where(low, o[:rows], o[rows:])
    for copy in copies:
        copy.wait()


def light_attend(q, k, v, even, odd, decoded):
    vmem = pl.BlockSpec(memory_space=pltpu.VMEM)
    hbm = pl.BlockSpec(memory_space=pl.ANY)
    return pl.pallas_call(
        light_kernel,
        in_specs=[vmem] * 5 + [hbm],
        out_specs=(vmem, hbm),
        out_shape=(jax.ShapeDtypeStruct(q.shape, f32), jax.ShapeDtypeStruct(decoded.shape, bf16)),
        scratch_shapes=[pltpu.SemaphoreType.DMA((4,))],
        compiler_params=params(12),
        cost_estimate=pl.CostEstimate(flops=3_000_000_000, transcendentals=800_000, bytes_accessed=2_000_000),
        name="light",
    )(q, k, v, even, odd, decoded)


def join_kernel(ids, light, heavy, out, both, sem):
    here = lax.axis_index(TOKENS)
    count = jnp.int32(0)
    for n in range(ids.shape[1]):
        count = count + jnp.where(ids[0, n] == here, 1, 0)
    scale = count.astype(f32)
    pairs = heavy.shape[0] // 2
    step = pairs // 4
    copies = []
    for p in range(pairs):
        e, o = heavy[2 * p], heavy[2 * p + 1]
        cols = slice(p * LANES, (p + 1) * LANES)
        for n in range(2):
            rows, lanes = slice(n * HALF, (n + 1) * HALF), slice(n * HEAD, (n + 1) * HEAD)
            added = jnp.concatenate([e[:, lanes], o[:, lanes]], axis=1)
            both[rows, cols] = (light[rows, cols] + added.astype(f32) * scale).astype(bf16)
        if p % step == step - 1:
            part = pl.ds((p + 1 - step) * LANES, step * LANES)
            copies.append(pltpu.make_async_copy(both.at[:, part], out.at[:, part], sem.at[p // step]))
            copies[-1].start()
    for copy in copies:
        copy.wait()


def join(ids, light, heavy):
    vmem = pl.BlockSpec(memory_space=pltpu.VMEM)
    return pl.pallas_call(
        join_kernel,
        in_specs=[pl.BlockSpec(memory_space=pltpu.SMEM), vmem, vmem],
        out_specs=pl.BlockSpec(memory_space=pl.ANY),
        out_shape=jax.ShapeDtypeStruct(light.shape, bf16),
        scratch_shapes=[pltpu.VMEM(light.shape, bf16), pltpu.SemaphoreType.DMA((4,))],
        compiler_params=params(6),
        name="join",
    )(ids, light, heavy)


def decode_kernel(q_hbm, e0, e1, e2, e3, out, q, sem):
    rows, width = q.shape
    at = pl.multiple_of(lax.axis_index("fine") * rows, rows)
    copy = pltpu.make_async_copy(q_hbm.at[pl.ds(at, rows)], q, sem)
    copy.start()
    copy.wait()
    zero = jnp.zeros((rows, HEAD), bf16)
    stack = jnp.concatenate(
        [
            jnp.concatenate([q[:, h * HEAD : (h + 1) * HEAD], zero], axis=1)
            for h in range(width // HEAD)
        ],
        axis=0,
    )
    keys = [e[...] for e in (e0, e1, e2, e3)]
    total, peak = summed(stack, keys)
    lane = lane_ids(total.shape)
    level = peak * SCALE + jnp.log(total)
    hi = level.astype(bf16).astype(f32)
    mid = (level - hi).astype(bf16).astype(f32)
    least = level - hi - mid
    parts = jnp.where(lane < 16, hi, jnp.where(lane < 32, mid, least))
    ratio = total / pltpu.roll(total, HEAD, 1)
    out[...] = jnp.where(lane < HEAD, parts, ratio).astype(bf16)


def decode(q, enc, rows):
    width = q.shape[1]
    vmem = pl.BlockSpec(memory_space=pltpu.VMEM)
    return pl.pallas_call(
        decode_kernel,
        in_specs=[pl.BlockSpec(memory_space=pltpu.HBM)] + [vmem] * len(enc),
        out_shape=jax.ShapeDtypeStruct((rows * (width // HEAD), LANES), bf16),
        scratch_shapes=[pltpu.VMEM((rows, width), bf16), pltpu.SemaphoreType.DMA(())],
        compiler_params=params(16),
        cost_estimate=pl.CostEstimate(flops=30_000_000_000, transcendentals=1_000_000, bytes_accessed=1_000_000),
        name="decode",
    )(q, *enc)


def meet_kernel(a, b, c, d, out, share, sem):
    parts = [x[...].astype(f32) for x in (a, b, c, d)]
    levels = [x[:, 0:1] + x[:, 16:17] + x[:, 32:33] for x in parts]
    peak = jnp.maximum(jnp.maximum(levels[0], levels[1]), jnp.maximum(levels[2], levels[3]))
    scales = [jnp.exp(n - peak) for n in levels]
    total = scales[0] + scales[1] + scales[2] + scales[3]
    value = parts[0] * scales[0]
    for x, s in zip(parts[1:], scales[1:]):
        value = value + x * s
    value = (value / total).astype(bf16)
    rows, width = share.shape
    for p in range(width // LANES):
        e = value[2 * p * rows : (2 * p + 1) * rows, HEAD:]
        o = value[(2 * p + 1) * rows : (2 * p + 2) * rows, HEAD:]
        share[:, p * LANES : (p + 1) * LANES] = jnp.concatenate([e, o], axis=1)
    copies = [pltpu.make_async_copy(share, out.at[n], sem.at[n]) for n in range(out.shape[0])]
    for copy in copies:
        copy.start()
    for copy in copies:
        copy.wait()


def meet(parts, copies, rows, width):
    return pl.pallas_call(
        meet_kernel,
        out_specs=pl.BlockSpec(memory_space=pl.ANY),
        scratch_shapes=[pltpu.VMEM((rows, width), bf16), pltpu.SemaphoreType.DMA((copies,))],
        out_shape=jax.ShapeDtypeStruct((copies, rows, width), bf16),
        compiler_params=params(8),
        cost_estimate=pl.CostEstimate(flops=30_000_000_000, transcendentals=0, bytes_accessed=2_000_000),
        name="meet",
    )(*parts)


def stack_kernel(*refs):
    parts, out = refs[:4], refs[-1]
    size = parts[0].shape[0]
    for n, part in enumerate(parts):
        out[n * size : (n + 1) * size] = part[...]


def stack(parts, *others):
    first = parts[0]
    specs = [pl.BlockSpec(memory_space=pltpu.VMEM)] * len(parts)
    return pl.pallas_call(
        stack_kernel,
        in_specs=specs + [pl.BlockSpec(memory_space=pl.ANY)] * len(others),
        out_shape=jax.ShapeDtypeStruct((len(parts) * first.shape[0],) + first.shape[1:], first.dtype),
        compiler_params=params(4),
        name="stack",
    )(*parts, *others)


def around(value, axis, stride=1, ring=None):
    size = lax.axis_size(axis)
    ring = ring or size

    def pairs(d):
        return [(i, i + ((i // stride % ring ^ d) - i // stride % ring) * stride) for i in range(size)]

    return [lax.ppermute(value, axis, pairs(d)) for d in range(1, ring)]


def after_all(value, *others):
    return lax.optimization_barrier((value, others))[0]


def local(
    q_light, k_light, v_light, q_heavy, k_heavy, v_heavy, enc_kv, dec_queries, query_ids, key_ids
):
    n_seq = lax.axis_size(TOKENS)
    n_fine = lax.axis_size("fine")
    side = 4
    width = q_light.shape[2]

    light_kv = jnp.concatenate([k_light[0], v_light[0]], axis=1)

    def rows_of(value):
        return [value] + around(value, "fine", 1, side)

    def square(row):
        return [row] + around(row, "fine", side, n_fine // side)

    chunks = pack(q_heavy[0], k_heavy[0], v_heavy[0])
    enc = square(stack(rows_of(enc_kv[0]), chunks))
    group = lax.all_to_all(after_all(chunks, enc[0]), "fine", 0, 0, tiled=True)

    dec_rows = dec_queries.shape[1] // n_fine
    part = decode(dec_queries[0], enc, dec_rows)

    parts = around(part, "coarse")
    own = pick(key_ids, after_all(group, part, light_kv)).reshape(KGRP * BLOCK, LANES)
    routed = [own] + around(own, "coarse")
    share = meet([after_all(part, own)] + parts, n_fine, dec_rows, width)
    decoded = lax.all_to_all(share, "fine", 0, 0, tiled=True)

    light_kv = after_all(light_kv, share)
    even = lax.ppermute(light_kv, TOKENS, [(i, i ^ 1) for i in range(n_seq)])
    odd = lax.ppermute(light_kv, TOKENS, [(i, (i - 1 ^ 1) + 1) for i in range(1, n_seq - 1)])

    heavy = heavy_attend(group, routed)
    heavy, decoded = lax.optimization_barrier((heavy, decoded))
    heavy = lax.all_to_all(heavy, "fine", 0, 0, tiled=True)
    light, decoded = light_attend(
        q_light[0], k_light[0], v_light[0], even, odd, decoded.reshape(-1, width)
    )
    encoded = join(query_ids, light, heavy)[None]
    return (encoded, decoded[None])


def solution(mesh):
    seq = P("doc", TOKENS, None)
    whole = P("doc", None, None)
    return jax.shard_map(
        local,
        mesh=mesh,
        in_specs=(seq,) * 7 + (whole, P("doc", None), P("doc", None)),
        out_specs=(seq, whole),
        check_vma=False,
    )
```
